32 devices in a mesh: dp: 8 (over y, x, core), tensor: 4 (over z).
Axes of the slice: x: 2, y: 2, z: 4, core: 2. Of those that a mesh axis runs over, the one named last changes fastest.
Arguments:
- tokens: bfloat16 [4096, 1024], P(('dp', 'tensor')), may hold values from -6 to 6
- segment_ids: int32 [8, 512], P('dp'), may hold values from 0 to 3, never falling along the last dimension, each value on 1 to 256 neighbouring positions
- query_weight: float32 [2, 1024, 1024], P(None, 'dp', 'tensor'), may hold values from -0.1875 to 0.1875
- key_weight: float32 [2, 1024, 1024], P(None, 'dp', 'tensor'), may hold values from -0.1875 to 0.1875
- value_weight: float32 [2, 1024, 2048], P(None, 'dp', 'tensor'), may hold values from -0.1875 to 0.1875
- gate_weight: float32 [2, 1024, 2048], P(None, 'dp', 'tensor'), may hold values from -0.1875 to 0.1875
- decay_weight: float32 [2, 1024, 16], P(None, 'dp', 'tensor'), may hold values from -0.1875 to 0.1875
- out_weight: float32 [2, 1024, 2048], P(None, 'dp', 'tensor'), may hold values from -0.25 to 0.25
- swiglu_gate: float32 [2, 1024, 2816], P(None, 'dp', 'tensor'), may hold values from -0.1875 to 0.1875
- swiglu_up: float32 [2, 1024, 2816], P(None, 'dp', 'tensor'), may hold values from -0.1875 to 0.1875
- swiglu_down: float32 [2, 1024, 2816], P(None, 'dp', 'tensor'), may hold values from -0.21875 to 0.21875
- conv_query_key: float32 [2, 2, 4, 1024], P(None, None, None, 'tensor'), may hold values from -3 to 3
- conv_value: float32 [2, 4, 2048], P(None, None, 'tensor'), may hold values from -3 to 3
- head_params: float32 [2, 2, 8], P(None, None, 'tensor'), may hold values from -6 to 0
- norm_gains: float32 [2, 2, 1024], replicated, may hold values from 0.1 to 1.9
- out_gain: float32 [2, 256], replicated, may hold values from 0.1 to 1.9
- cotangent: bfloat16 [4096, 1024], P(('dp', 'tensor')), may hold values from -6 to 6
Outputs:
- output: float32 [4096, 1024], P(('dp', 'tensor'))
- input_grad: float32 [4096, 1024], P(('dp', 'tensor'))
- query_weight_grad: float32 [2, 1024, 1024], P(None, 'dp', 'tensor')
- key_weight_grad: float32 [2, 1024, 1024], P(None, 'dp', 'tensor')
- value_weight_grad: float32 [2, 1024, 2048], P(None, 'dp', 'tensor')
- gate_weight_grad: float32 [2, 1024, 2048], P(None, 'dp', 'tensor')
- decay_weight_grad: float32 [2, 1024, 16], P(None, 'dp', 'tensor')
- out_weight_grad: float32 [2, 1024, 2048], P(None, 'dp', 'tensor')
- swiglu_gate_grad: float32 [2, 1024, 2816], P(None, 'dp', 'tensor')
- swiglu_up_grad: float32 [2, 1024, 2816], P(None, 'dp', 'tensor')
- swiglu_down_grad: float32 [2, 1024, 2816], P(None, 'dp', 'tensor')
- conv_query_key_grad: float32 [2, 2, 4, 1024], P(None, None, None, 'tensor')
- conv_value_grad: float32 [2, 4, 2048], P(None, None, 'tensor')
- head_params_grad: float32 [2, 2, 8], P(None, None, 'tensor')
- norm_gains_grad: float32 [2, 2, 1024], replicated
- out_gain_grad: float32 [2, 256], replicated
The draws below stay inside these ranges and needn't reach their ends.
Inputs may be any that keep to these rules, and one draw needn't show every extreme that they name: `segment_ids`: segment ids never fall along a sequence; every document holds 1 to 256 tokens.
All inputs are finite; a program needn't handle non-finite values.
Results may differ from the reference program's by a relative error of at most 0.025.
Values may be sent and summed in bfloat16 or wider, within the bound.
A program may use at most 192 MiB of HBM per device.

```python
import math
import jax
import jax.numpy as jnp
import numpy as np
from jax import lax

D = 1024
H = 8
DK = 128
DV = 256
FF = 2816
CONV = 4
SPAN = 64
LAYERS = 2
DOCS = 4
LEN = 512
SEQS = 8
TOKENS = 4096


def strengthened(entries, rng, source, target, shards_of, factor):
    def block_of(axis_at):
        return (jnp.arange(entries.shape[axis_at]) // (entries.shape[axis_at] // shards_of)).reshape((-1,) + (1,) * (entries.ndim - 1 - axis_at))

    near = jax.random.permutation(rng, shards_of)[block_of(target)]
    other_side = (block_of(target) + shards_of // 2) % shards_of
    return jnp.where((block_of(source) == near) | (block_of(source) == other_side), factor * entries, entries)


def steps_of(own_key, dims, pieces, smallest, top_value):
    level = 1.0
    for axis_at, shards_of in pieces:
        heights = jax.random.uniform(jax.random.fold_in(jax.random.fold_in(own_key, 6), axis_at), (shards_of,), jnp.float32, smallest / len(pieces), top_value / len(pieces))
        level = level * jnp.repeat(jnp.exp(heights), dims[axis_at] // shards_of).reshape((-1,) + (1,) * (len(dims) - 1 - axis_at))
    return level


def split_up(number_of, total, bound, slope):
    loads = [(1 << 20) // math.isqrt(standing ** slope) + 1 for standing in range(2, number_of + 1)]
    spare, given = total - bound - (number_of - 1), [1] * (number_of - 1)
    while spare > 0:
        free = [i for i in range(number_of - 1) if given[i] < bound]
        pool, left = sum([loads[i] for i in free]), spare
        for i in free:
            more = min(bound - given[i], max(1, left * loads[i] // pool), spare)
            given[i] = given[i] + more
            spare = spare - more
    return np.array([bound] + given)


def ragged_sizes(rng, number_of, total, bound, skew):
    if number_of == 2:
        one = jax.random.randint(rng, (), max(1, total - bound), min(bound, total - 1) + 1)
        return jnp.stack([one, total - one])
    lengths = jnp.asarray(split_up(number_of, total, bound, skew), jnp.int32)
    couples = (number_of - 1) // 2
    donor, receiver = lengths[1:1 + 2 * couples:2], lengths[2:2 + 2 * couples:2]
    margin = jnp.minimum(donor - 1, bound - receiver)
    passed = jax.random.randint(jax.random.fold_in(rng, 1), (couples,), 0, 1 << 20) % (margin + 1)
    lengths = lengths.at[1:1 + 2 * couples:2].set(donor - passed).at[2:2 + 2 * couples:2].set(receiver + passed)
    return lengths[jax.random.permutation(jax.random.fold_in(rng, 2), number_of)]


def gaussian(rng, dims, spread, limit, cuts=(), kind=jnp.bfloat16):
    drawn = jax.random.normal(rng, dims, jnp.float32) * spread
    if len(cuts) > 0:
        drawn = steps_of(rng, dims, cuts, -0.22, 0.18) * drawn
    return jnp.clip(drawn, min=-limit, max=limit).astype(kind)


def heavy_noise(stream_key, dims, width, bound, pieces, heavy, kind=jnp.bfloat16):
    drawn = width * jax.random.normal(stream_key, dims, jnp.float32)
    if pieces:
        drawn = drawn * steps_of(stream_key, dims, pieces, -0.22, 0.18)
    return jnp.clip(strengthened(drawn, jax.random.fold_in(stream_key, 3), *heavy), -bound, bound).astype(kind)


def setup_inputs(seed: int = 0) -> dict:
    key_of = jax.random.split(jax.random.key(seed), 18)
    return {
        "tokens": gaussian(key_of[0], (TOKENS, D), 1.0, 6.0, ((0, 32),)),
        "segment_ids": jax.vmap(lambda own: jnp.searchsorted(jnp.cumsum(ragged_sizes(own, DOCS, LEN, LEN // 2, 1)), jnp.arange(LEN), side="right"))(jax.random.split(key_of[1], SEQS)).reshape((SEQS, LEN)).astype(jnp.int32),
        "query_weight": gaussian(key_of[2], (LAYERS, D, H * DK), D ** -0.5, 0.1875, ((1, 8), (2, 4)), jnp.float32),
        "key_weight": gaussian(key_of[3], (LAYERS, D, H * DK), D ** -0.5, 0.1875, ((1, 8), (2, 4)), jnp.float32),
        "value_weight": gaussian(key_of[4], (LAYERS, D, H * DV), D ** -0.5, 0.1875, ((1, 8), (2, 4)), jnp.float32),
        "gate_weight": gaussian(key_of[5], (LAYERS, D, H * DV), D ** -0.5, 0.1875, ((1, 8), (2, 4)), jnp.float32),
        "decay_weight": gaussian(key_of[6], (LAYERS, D, 2 * H), D ** -0.5, 0.1875, ((1, 8), (2, 4)), jnp.float32),
        "out_weight": gaussian(key_of[7], (LAYERS, D, H * DV), (H * DV // 4) ** -0.5, 0.25, ((1, 8), (2, 4)), jnp.float32),
        "swiglu_gate": gaussian(key_of[8], (LAYERS, D, FF), D ** -0.5, 0.1875, ((1, 8), (2, 4)), jnp.float32),
        "swiglu_up": gaussian(key_of[9], (LAYERS, D, FF), D ** -0.5, 0.1875, ((1, 8), (2, 4)), jnp.float32),
        "swiglu_down": gaussian(key_of[10], (LAYERS, D, FF), (FF // 4) ** -0.5, 0.21875, ((1, 8), (2, 4)), jnp.float32),
        "conv_query_key": gaussian(key_of[11], (LAYERS, 2, CONV, H * DK), CONV ** -0.5, 3.0, ((3, 4),), jnp.float32),
        "conv_value": gaussian(key_of[12], (LAYERS, CONV, H * DV), CONV ** -0.5, 3.0, ((2, 4),), jnp.float32),
        "head_params": jnp.clip(-6.0 + 6.0 * jax.random.uniform(key_of[13], (LAYERS, 2, H), jnp.float32) ** steps_of(key_of[13], (LAYERS, 2, H), ((2, 4),), -0.2, 0.2), -6.0, 0.0),
        "norm_gains": jnp.clip(1.0 + 0.18 * jax.random.normal(key_of[14], (LAYERS, 2, D), jnp.float32), 0.1, 1.9),
        "out_gain": jnp.clip(1.0 + 0.18 * jax.random.normal(key_of[15], (LAYERS, DV), jnp.float32), 0.1, 1.9),
        "cotangent": heavy_noise(key_of[16], (TOKENS, D), 1.0, 6.0, ((0, 32),), (0, 1, 32, 2.75)),
    }


@jax.custom_vjp
def low(v):
    return lax.optimization_barrier(v.astype(jnp.bfloat16)).astype(jnp.float32)

@jax.custom_vjp
def low_back(v):
    return v

def low_keep(v):
    return (low(v), None)

def low_pass(kept, grad):
    return (grad,)

def back_keep(v):
    return (v, None)

def back_low(kept, grad):
    return (low(grad),)
low.defvjp(low_keep, low_pass)
low_back.defvjp(back_keep, back_low)
epsilon = 1e-06
out_floor = 0.01
highest = lax.Precision.HIGHEST

def rms_gain(matrix, gain_vector):
    scaling = lax.rsqrt(lax.optimization_barrier(jnp.mean(matrix * matrix, axis=-1, keepdims=True)) + epsilon)
    return matrix * scaling * gain_vector

def matmul(left, right):
    return jnp.dot(left.astype(jnp.float32), right.astype(jnp.float32), precision=highest, preferred_element_type=jnp.float32)

def matmul_trans(left, right):
    return jnp.dot(left.astype(jnp.float32), right.T.astype(jnp.float32), precision=highest, preferred_element_type=jnp.float32)

def causal_conv(signal, kernel, segment_ids):
    length = signal.shape[1]
    summed = signal * kernel[0]
    for offset in range(1, kernel.shape[0]):
        shifted = jnp.pad(signal, ((0, 0), (offset, 0), (0, 0)))[:, :length]
        earlier = jnp.pad(segment_ids, ((0, 0), (offset, 0)), constant_values=-1)[:, :length]
        matching = (earlier == segment_ids).astype(signal.dtype)[:, :, None]
        summed = summed + shifted * matching * kernel[offset]
    return summed

def block_step(carried, block_in):
    memory_state, last_segment = carried
    queries, keys_in, values_in, beta_gate, log_decay, segment_block = block_in
    kind = keys_in.dtype
    extent = segment_block.shape[1]
    cumulative = jnp.cumsum(log_decay, axis=-1)
    positions = jnp.arange(extent, dtype=jnp.int32)
    lower_incl = positions[:, None] >= positions[None, :]
    strict_lower = (positions[:, None] > positions[None, :]).astype(kind)
    same_segment = segment_block[:, :, None] == segment_block[:, None, :]
    allowed = (same_segment & lower_incl[None]).astype(kind)[:, None]
    fading = jnp.exp((cumulative[..., :, None] - cumulative[..., None, :]) * allowed) * allowed
    carried_mask = (segment_block == last_segment[:, None]).astype(kind)[:, None, :]
    entry_scale = jnp.exp(cumulative) * carried_mask
    key_products = jnp.einsum('bhtk,bhsk->bhts', keys_in, keys_in, precision=highest)
    mixing = beta_gate[..., :, None] * key_products * fading * strict_lower
    recalled = jnp.einsum('bhtk,bhkv->bhtv', keys_in, memory_state, precision=highest)
    target = beta_gate[..., None] * (values_in - entry_scale[..., None] * recalled)
    unit_lower = jnp.eye(extent, dtype=kind) + mixing
    corrected = jax.scipy.linalg.solve_triangular(unit_lower, target, lower=True, unit_diagonal=True)
    query_keys = jnp.einsum('bhtk,bhsk->bhts', queries, keys_in, precision=highest)
    from_state = jnp.einsum('bhtk,bhkv->bhtv', queries, memory_state, precision=highest)
    outputs = entry_scale[..., None] * from_state + jnp.einsum('bhts,bhsv->bhtv', query_keys * fading, corrected, precision=highest)
    final_segment = segment_block[:, -1].astype(jnp.int32)
    tail_mask = (segment_block == final_segment[:, None]).astype(kind)[:, None, :]
    tail_weight = jnp.exp(cumulative[..., -1:] - cumulative) * tail_mask
    new_state = entry_scale[..., -1][..., None, None] * memory_state + jnp.einsum('bhsk,bhsv->bhkv', keys_in * tail_weight[..., None], corrected, precision=highest)
    return ((new_state.astype(memory_state.dtype), final_segment), outputs)

def delta_core(proj_query, proj_key, proj_value, proj_gate, proj_pair, kernel_pair, kernel_value, head_table, gain_vector, segment_ids):
    batches, length = segment_ids.shape
    head_count = proj_pair.shape[1] // 2
    key_dim = proj_query.shape[1] // head_count
    value_dim = proj_value.shape[1] // head_count
    blocks = length // SPAN

    def sequences(matrix):
        return matrix.reshape(batches, length, matrix.shape[1])
    queries = jax.nn.silu(causal_conv(sequences(proj_query), kernel_pair[0], segment_ids))
    keys_in = jax.nn.silu(causal_conv(sequences(proj_key), kernel_pair[1], segment_ids))
    values_in = jax.nn.silu(causal_conv(sequences(proj_value), kernel_value, segment_ids))
    queries = queries.reshape(batches, length, head_count, key_dim)
    keys_in = keys_in.reshape(batches, length, head_count, key_dim)
    values_in = values_in.reshape(batches, length, head_count, value_dim)
    queries = queries * lax.rsqrt(lax.optimization_barrier(jnp.sum(queries * queries, axis=-1, keepdims=True)) + epsilon) * key_dim ** (-0.5)
    keys_in = keys_in * lax.rsqrt(lax.optimization_barrier(jnp.sum(keys_in * keys_in, axis=-1, keepdims=True)) + epsilon)
    pairs = proj_pair.reshape(batches, length, head_count, 2)
    beta_gate = jax.nn.sigmoid(pairs[..., 1])
    log_decay = -jnp.exp(head_table[0]) * jax.nn.softplus(pairs[..., 0] + head_table[1])

    def to_blocks(array):
        array = array.reshape((batches, blocks, SPAN) + array.shape[2:])
        return jnp.moveaxis(jnp.moveaxis(array, 1, 0), 3, 2)
    segment_blocks = jnp.moveaxis(segment_ids.reshape(batches, blocks, SPAN), 1, 0).astype(jnp.int32)
    start_state = jnp.zeros((batches, head_count, key_dim, value_dim), keys_in.dtype)
    inputs = (to_blocks(queries), to_blocks(keys_in), to_blocks(values_in), to_blocks(beta_gate), to_blocks(log_decay), segment_blocks)
    ignored, outputs = lax.scan(jax.checkpoint(block_step), (start_state, segment_ids[:, 0].astype(jnp.int32)), inputs)
    recurrent = jnp.moveaxis(jnp.moveaxis(outputs, 0, 1), 2, 3).reshape(batches * length, head_count, value_dim)
    gate_pre = proj_gate.reshape(batches * length, head_count, value_dim)
    normalized = recurrent * lax.rsqrt(lax.optimization_barrier(jnp.mean(recurrent * recurrent, axis=-1, keepdims=True)) + out_floor)
    return (normalized * gain_vector * jax.nn.silu(gate_pre)).reshape(batches * length, head_count * value_dim)

def forward(params, residual, segments_now):
    query_mat, key_mat, value_mat, gate_mat, decay_mat, out_mat, swiglu_gate_mat, swiglu_up_mat, swiglu_down_mat, kernel_pairs, kernel_values, head_tables, norm_table, gain_table = params
    for layer_idx in range(LAYERS):
        normed = low(rms_gain(residual, norm_table[layer_idx, 0]))
        projected = [low_back(matmul(normed, low(matrix[layer_idx]))) for matrix in (query_mat, key_mat, value_mat, gate_mat, decay_mat)]
        mixer_out = delta_core(projected[0], projected[1], projected[2], projected[3], projected[4], kernel_pairs[layer_idx], kernel_values[layer_idx], head_tables[layer_idx], gain_table[layer_idx], segments_now)
        middle = residual + low_back(matmul_trans(low(mixer_out), low(out_mat[layer_idx])))
        normed_ffn = low(rms_gain(middle, norm_table[layer_idx, 1]))
        gate_pre = low_back(matmul(normed_ffn, low(swiglu_gate_mat[layer_idx])))
        up_pre = low_back(matmul(normed_ffn, low(swiglu_up_mat[layer_idx])))
        hidden = low(jax.nn.silu(gate_pre) * up_pre)
        residual = middle + low_back(matmul_trans(hidden, low(swiglu_down_mat[layer_idx])))
    return residual

def reference(tokens, segment_ids, query_weight, key_weight, value_weight, gate_weight, decay_weight, out_weight, swiglu_gate, swiglu_up, swiglu_down, conv_query_key, conv_value, head_params, norm_gains, out_gain, cotangent):
    sequences_all = segment_ids.shape[0]
    length = segment_ids.shape[1]
    model_width = tokens.shape[1]
    grouped = 1
    for candidate in range(1, sequences_all + 1):
        if sequences_all % candidate == 0 and candidate * length <= 4096:
            grouped = candidate
    rounds = sequences_all // grouped
    params = (query_weight, key_weight, value_weight, gate_weight, decay_weight, out_weight, swiglu_gate, swiglu_up, swiglu_down, conv_query_key, conv_value, head_params, norm_gains, out_gain)
    token_blocks = tokens.astype(jnp.float32).reshape(rounds, grouped * length, model_width)
    cot_blocks = cotangent.astype(jnp.float32).reshape(rounds, grouped * length, model_width)
    segment_blocks = segment_ids.astype(jnp.int32).reshape(rounds, grouped, length)
    zeros_init = tuple((jnp.zeros_like(param) for param in params))

    def one_round(summed_grads, round_in):
        round_tokens, round_segments, round_cot = round_in
        result, pull_back = jax.vjp(lambda weights, inputs: forward(weights, inputs, round_segments), params, round_tokens)
        weight_grads, input_grads = pull_back(round_cot)
        summed = tuple((before + extra.astype(before.dtype) for before, extra in zip(summed_grads, weight_grads)))
        return (summed, (result, input_grads))
    totals, (results, input_grads) = lax.scan(one_round, zeros_init, (token_blocks, segment_blocks, cot_blocks))
    return (results.reshape(sequences_all * length, model_width), input_grads.reshape(sequences_all * length, model_width), totals[0], totals[1], totals[2], totals[3], totals[4], totals[5], totals[6], totals[7], totals[8], totals[9], totals[10], totals[11], totals[12], totals[13])
```

```python
import functools
import jax
import jax.numpy as jnp
from jax import lax
from jax.experimental import pallas as pl
from jax.experimental.pallas import tpu as pltpu
from jax.sharding import PartitionSpec as P

F32 = jnp.float32
BF16 = jnp.bfloat16
NN = (((1,), (0,)), ((), ()))
NT = (((1,), (1,)), ((), ()))
TN = (((0,), (0,)), ((), ()))
EPS = 1e-6
FLOOR = 0.01


def split(x):
    high = x.astype(BF16)
    return high, (x - high.astype(F32)).astype(BF16)


def mm(a, b, dims, passes=1):
    def one(p, q):
        return lax.dot_general(p, q, dims, preferred_element_type=F32)

    if passes == 1:
        return one(a.astype(BF16), b.astype(BF16))
    ah, al = split(a)
    bh, bl = split(b)
    return one(ah, bh) + (one(ah, bl) + one(al, bh))


def iota(shape, axis):
    return lax.broadcasted_iota(jnp.int32, shape, axis)


def shifted_rows(x, by):
    return pltpu.roll(x, by % x.shape[0], 0) if by else x


def conv(signal, taps, masks):
    total = signal * taps[0:1]
    for j in range(1, 4):
        total = total + shifted_rows(signal, j) * masks[j - 1] * taps[j : j + 1]
    return total


def chunk_scan(row, chunk, backward=False):
    length = row.shape[1]
    place = iota(row.shape, 1) % chunk
    step = 1
    while step < chunk:
        if backward:
            moved = pltpu.roll(row, length - step, 1)
            row = row + jnp.where(place < chunk - step, moved, 0.0)
        else:
            moved = pltpu.roll(row, step, 1)
            row = row + jnp.where(place >= step, moved, 0.0)
        step *= 2
    return row


def unit_lower_inverse(lower, refine):
    size = lower[0].shape[0]
    rows, cols = iota((size, size), 0), iota((size, size), 1)
    eye = (rows == cols).astype(F32)

    def off(block):
        return ((rows // (2 * block) == cols // (2 * block)) & (rows // block != cols // block)).astype(F32)

    found = [eye - part * off(1) for part in lower]
    block = 2
    while block < size:
        mask = off(block)
        half = [mm(x, part * mask, NN) for x, part in zip(found, lower)]
        found = [x - mm(t, x, NN) for x, t in zip(found, half)]
        block *= 2
    for _ in range(refine):
        rest = [(x - eye) + mm(part, x, NN, 3) for x, part in zip(found, lower)]
        found = [x - mm(x, r, NN, 1) for x, r in zip(found, rest)]
    return found


def prepared(head, chunk, qref, kref, vref, pair_ref, tap_qk, tap_v, head_table, col_info, row_info):
    length, dk = qref.shape
    masks = [col_info[:, j : j + 1] for j in range(3)]
    masks = [jnp.broadcast_to(m, (length, dk)) for m in masks]
    dv = vref.shape[1]
    wide = [jnp.concatenate([m] * (dv // dk), axis=1) for m in masks]
    pre_q = conv(qref[...], tap_qk[0], masks)
    pre_k = conv(kref[...], tap_qk[1], masks)
    pre_v = conv(vref[...], tap_v[...], wide)
    out = dict(masks=masks, wide=wide, pre_q=pre_q, pre_k=pre_k, pre_v=pre_v)
    for name, pre in (("q", pre_q), ("k", pre_k), ("v", pre_v)):
        sig = lax.logistic(pre)
        out["sig_" + name] = sig
        out["act_" + name] = pre * sig
    out["inv_q"] = lax.rsqrt(jnp.sum(out["act_q"] ** 2, axis=1, keepdims=True) + EPS)
    out["inv_k"] = lax.rsqrt(jnp.sum(out["act_k"] ** 2, axis=1, keepdims=True) + EPS)
    out["q"] = out["act_q"] * out["inv_q"] * dk ** (-0.5)
    out["k"] = out["act_k"] * out["inv_k"]
    out["v"] = out["act_v"]
    pair = jnp.transpose(pair_ref[...])
    picked = iota(pair.shape, 0)
    a_row = jnp.sum(jnp.where(picked == 2 * head, pair, 0.0), axis=0, keepdims=True)
    b_row = jnp.sum(jnp.where(picked == 2 * head + 1, pair, 0.0), axis=0, keepdims=True)
    rate = jnp.exp(jnp.full((1, length), head_table[0, head], F32))
    a_row = a_row + head_table[1, head]
    softplus = jnp.maximum(a_row, 0.0) + jnp.log1p(jnp.exp(-jnp.abs(a_row)))
    decay = -rate * softplus
    beta = lax.logistic(b_row)
    total = chunk_scan(decay, chunk)
    entry = jnp.exp(total) * row_info[0:1]
    chunks = length // chunk
    place = iota((1, length), 1)
    ends = [total[:, (i + 1) * chunk - 1 : (i + 1) * chunk] for i in range(chunks)]
    last = ends[0]
    for i in range(1, chunks):
        last = jnp.where(place >= i * chunk, ends[i], jnp.broadcast_to(last, (1, length)))
    tail = jnp.exp(last - total) * row_info[1:2]
    rows = jnp.concatenate([beta, total, entry, tail, jnp.zeros((124, length), F32)], axis=0)
    cols = jnp.transpose(rows)
    out.update(
        a_row=a_row, rate=rate, decay=decay, beta_row=beta, total_row=total, entry_row=entry, tail_row=tail,
        beta=cols[:, 0:1], total=cols[:, 1:2], entry=cols[:, 2:3], tail=cols[:, 3:4],
    )
    return out


def chunk_parts(pre, i, chunk, col_info, row_info):
    s = slice(i * chunk, (i + 1) * chunk)
    q, k, v = pre["q"][s], pre["k"][s], pre["v"][s]
    beta, total, entry, tail = pre["beta"][s], pre["total"][s], pre["entry"][s], pre["tail"][s]
    rows, cols = iota((chunk, chunk), 0), iota((chunk, chunk), 1)
    allowed = (col_info[s, 3:4] == row_info[2:3, s]) & (rows >= cols)
    fading = jnp.where(allowed, jnp.exp(jnp.where(allowed, total - pre["total_row"][:, s], 0.0)), 0.0)
    both = mm(jnp.concatenate([q, k], axis=0), k, NT)
    strict_fading = jnp.where(rows > cols, fading, 0.0)
    qk, kk = both[:chunk], both[chunk:]
    return dict(
        q=q, k=k, v=v, beta=beta, entry=entry, tail=tail, fading=fading, strict=strict_fading,
        mixed=qk * fading, kk_faded=kk * strict_fading, lower=beta * (kk * strict_fading),
        exit=pre["entry_row"][:, (i + 1) * chunk - 1 : (i + 1) * chunk], rows=s,
    )


def forward_kernel(
    chunk, refine, qref, kref, vref, gref, pair_ref, tap_qk, tap_v, head_table, gain, col_ref, row_ref,
    mix_ref, rec_ref, fix_ref, inv_ref, state_ref,
):
    head = pl.program_id(1)
    col_info, row_info = col_ref[0], row_ref[0]
    pre = prepared(head, chunk, qref, kref, vref, pair_ref, tap_qk, tap_v, head_table, col_info, row_info)
    length, dk = qref.shape
    dv = vref.shape[1]
    chunks = length // chunk
    parts = [chunk_parts(pre, i, chunk, col_info, row_info) for i in range(chunks)]
    inverses = unit_lower_inverse([p["lower"] for p in parts], refine)
    state = jnp.zeros((dk, dv), F32)
    steps = []
    for p, inverse in zip(parts, inverses):
        target = jnp.concatenate([p["beta"] * p["entry"] * p["k"], p["beta"] * p["v"]], axis=1)
        solved = mm(inverse, target, NN)
        pushed = mm(p["k"] * p["tail"], solved, TN)
        steps.append((solved, pushed))
    states = []
    for p, (solved, pushed) in zip(parts, steps):
        states.append(state)
        state = p["exit"] * state - mm(pushed[:, :dk], state, NN) + pushed[:, dk:]
    gain_row = gain[...]
    for i, (p, inverse, (solved, pushed)) in enumerate(zip(parts, inverses, steps)):
        seen = mm(jnp.concatenate([solved[:, :dk], p["q"] * p["entry"]], axis=0), states[i], NN)
        fixed = solved[:, dk:] - seen[:chunk]
        rec = seen[chunk:] + mm(p["mixed"], fixed, NN)
        s = p["rows"]
        rec_ref[s, :] = rec
        fix_ref[s, :] = fixed
        inv_ref[0, 0, i] = inverse
        state_ref[0, 0, i] = states[i]
        normal = rec * lax.rsqrt(jnp.mean(rec * rec, axis=1, keepdims=True) + FLOOR)
        gate = gref[s, :]
        mix_ref[s, :] = (normal * gain_row * (gate * lax.logistic(gate))).astype(BF16)


def silu_grad(pre, sig):
    return sig * (1.0 + pre * (1.0 - sig))


def backward_kernel(
    chunk, heads, qref, kref, vref, gref, pair_ref, tap_qk, tap_v, head_table, gain, col_ref, row_ref,
    rec_ref, fix_ref, inv_ref, state_ref, dmix_ref,
    dproj_ref, dtap_qk, dtap_v, dhead_ref, dgain_ref,
):
    seq, head = pl.program_id(0), pl.program_id(1)
    col_info, row_info = col_ref[0], row_ref[0]
    pre = prepared(head, chunk, qref, kref, vref, pair_ref, tap_qk, tap_v, head_table, col_info, row_info)
    length, dk = qref.shape
    dv = vref.shape[1]
    chunks = length // chunk
    parts = [chunk_parts(pre, i, chunk, col_info, row_info) for i in range(chunks)]
    gain_row = gain[...]
    dgain = jnp.zeros((1, dv), F32)
    v_at = 2 * heads * dk
    g_at = v_at + heads * dv
    p_at = g_at + heads * dv
    for p in parts:
        s = p["rows"]
        rec, gate, dmix = rec_ref[s, :], gref[s, :], dmix_ref[s, :]
        scale = lax.rsqrt(jnp.mean(rec * rec, axis=1, keepdims=True) + FLOOR)
        sig = lax.logistic(gate)
        gated = dmix * (gate * sig)
        normal = rec * scale
        dgain = dgain + jnp.sum(gated * normal, axis=0, keepdims=True)
        dgate = dmix * normal * gain_row * silu_grad(gate, sig)
        dproj_ref[s, pl.ds(pl.multiple_of(g_at + head * dv, dv), dv)] = dgate.astype(BF16)
        dn = gated * gain_row
        p["drec"] = scale * dn - rec * (scale * scale * scale) * jnp.mean(dn * rec, axis=1, keepdims=True)
    for i, p in enumerate(parts):
        inverse = inv_ref[0, 0, i]
        p["inverse"] = inverse
        solved = mm(inverse, p["beta"] * p["entry"] * p["k"], NN)
        back = mm(p["mixed"], p["drec"], TN)
        p["back"] = back
        ahead = mm(solved, p["k"] * p["tail"], TN)
        given = mm(
            jnp.concatenate([p["q"] * p["entry"], -solved], axis=0),
            jnp.concatenate([p["drec"], back], axis=0), TN,
        )
        p["ahead"], p["given"] = ahead, given
    dstate = jnp.zeros((dk, dv), F32)
    for p in reversed(parts):
        p["dstate"] = dstate
        dstate = p["exit"] * dstate - mm(p["ahead"], dstate, NN) + p["given"]
    cols = iota((chunk, 8), 1)
    col_parts, row_parts, dqs, dks, dvs = [], [], [], [], []
    for i, p in enumerate(parts):
        s = p["rows"]
        state, dstate, fixed, drec = state_ref[0, 0, i], p["dstate"], fix_ref[s, :], p["drec"]
        q, k, v, beta, entry, tail = p["q"], p["k"], p["v"], p["beta"], p["entry"], p["tail"]
        dfixed = p["back"] + mm(k * tail, dstate, NN)
        dtarget = mm(p["inverse"], dfixed, TN)
        outer = mm(
            jnp.concatenate([drec, dtarget], axis=0), jnp.concatenate([state, fixed], axis=0), NT
        )
        drec_state, dtarget_state = outer[:chunk, :dk], outer[chunk:, :dk]
        dmixed, dlower = outer[:chunk, dk:], -outer[chunk:, dk:]
        fixed_dstate = mm(fixed, dstate, NT)
        g1 = dmixed * p["fading"]
        g2 = (beta * dlower) * p["strict"]
        stacked = jnp.concatenate([g1, g2], axis=0)
        first = mm(stacked, k, NN)
        second = mm(stacked, jnp.concatenate([q, k], axis=0), TN)
        key_state = jnp.sum(dtarget_state * k, axis=1, keepdims=True)
        dqs.append(entry * drec_state + first[:chunk])
        dks.append(first[chunk:] + second + tail * fixed_dstate - (beta * entry) * dtarget_state)
        dvs.append(beta * dtarget)
        dentry = jnp.sum(drec_state * q, axis=1, keepdims=True) - beta * key_state
        dtail = jnp.sum(fixed_dstate * k, axis=1, keepdims=True) * tail
        high = dmixed * p["mixed"] + dlower * p["lower"]
        dbeta = (
            jnp.sum(dtarget * v, axis=1, keepdims=True)
            - entry * key_state
            + jnp.sum(dlower * p["kk_faded"], axis=1, keepdims=True)
        )
        dtotal = jnp.sum(high, axis=1, keepdims=True) + dentry * entry - dtail
        end = p["exit"] * jnp.sum(jnp.sum(dstate * state, axis=1, keepdims=True), axis=0, keepdims=True)
        end = end + jnp.sum(dtail, axis=0, keepdims=True)
        dtotal = dtotal + jnp.where(iota((chunk, 1), 0) == chunk - 1, end, 0.0)
        row_parts.append(jnp.sum(high, axis=0, keepdims=True))
        col_parts.append(jnp.where(cols == 0, dtotal, jnp.where(cols == 1, dbeta, 0.0)))
    lanes = jnp.concatenate(col_parts, axis=0)
    lanes = jnp.concatenate([lanes, jnp.zeros((length, 120), F32)], axis=1)
    turned = jnp.transpose(lanes)
    dtotal_row = turned[0:1] - jnp.concatenate(row_parts, axis=1)
    dbeta_row = turned[1:2]
    ddecay = chunk_scan(dtotal_row, chunk, backward=True)
    da = -ddecay * pre["rate"] * lax.logistic(pre["a_row"])
    db = dbeta_row * pre["beta_row"] * (1.0 - pre["beta_row"])
    spread = iota((128, length), 0)
    dpair = jnp.where(spread == 2 * head, da, jnp.where(spread == 2 * head + 1, db, 0.0))
    dpair = jnp.transpose(dpair).astype(BF16)

    @pl.when(head == 0)
    def _():
        dproj_ref[:, p_at:] = dpair

    @pl.when(head != 0)
    def _():
        dproj_ref[:, p_at:] = dproj_ref[:, p_at:] + dpair

    dscale = jnp.sum(ddecay * pre["decay"], axis=1, keepdims=True)
    dbias = jnp.sum(da, axis=1, keepdims=True)
    which = iota((8, 128), 0)
    dhead = jnp.where(which == 0, dscale, jnp.where(which == 1, dbias, 0.0))
    dq, dk_all, dv_all = (jnp.concatenate(x, axis=0) for x in (dqs, dks, dvs))

    def through_norm(grad, act, inv, factor):
        return factor * (inv * grad - act * (inv * inv * inv) * jnp.sum(grad * act, axis=1, keepdims=True))

    dq = through_norm(dq, pre["act_q"], pre["inv_q"], dk ** (-0.5))
    dk_all = through_norm(dk_all, pre["act_k"], pre["inv_k"], 1.0)
    taps_out = []
    for grad, name, src, taps, masks, at in (
        (dq, "q", qref, tap_qk[0], pre["masks"], head * dk),
        (dk_all, "k", kref, tap_qk[1], pre["masks"], heads * dk + head * dk),
        (dv_all, "v", vref, tap_v[...], pre["wide"], v_at + head * dv),
    ):
        dpre = grad * silu_grad(pre["pre_" + name], pre["sig_" + name])
        signal = src[...]
        dsignal = dpre * taps[0:1]
        dtaps = [jnp.sum(dpre * signal, axis=0, keepdims=True)]
        for j in range(1, 4):
            masked = dpre * masks[j - 1]
            dsignal = dsignal + shifted_rows(masked, -j) * taps[j : j + 1]
            dtaps.append(jnp.sum(masked * shifted_rows(signal, j), axis=0, keepdims=True))
        width = grad.shape[1]
        dproj_ref[:, pl.ds(pl.multiple_of(at, width), width)] = dsignal.astype(BF16)
        taps_out.append(jnp.concatenate(dtaps, axis=0))
    dtap_qk[0, 0] = taps_out[0]
    dtap_qk[0, 1] = taps_out[1]
    dtap_v[0] = taps_out[2]
    dhead_ref[0, 0] = dhead
    dgain_ref[0, 0] = dgain


def specs(length, heads, dk, dv):
    v_block = 2 * heads * dk // dv
    return [
        pl.BlockSpec((length, dk), lambda s, h: (s, h)),
        pl.BlockSpec((length, dk), lambda s, h: (s, heads + h)),
        pl.BlockSpec((length, dv), lambda s, h: (s, v_block + h)),
        pl.BlockSpec((length, dv), lambda s, h: (s, v_block + heads + h)),
        pl.BlockSpec((length, 128), lambda s, h: (s, (2 * heads * dk + 2 * heads * dv) // 128)),
        pl.BlockSpec((2, 4, dk), lambda s, h: (0, 0, h)),
        pl.BlockSpec((4, dv), lambda s, h: (0, h)),
        pl.BlockSpec(memory_space=pltpu.SMEM),
        pl.BlockSpec((1, dv), lambda s, h: (0, 0)),
        pl.BlockSpec((1, length, 8), lambda s, h: (s, 0, 0)),
        pl.BlockSpec((1, 8, length), lambda s, h: (s, 0, 0)),
    ]


def segment_tables(segment_ids, chunk):
    seqs, length = segment_ids.shape
    place = jnp.arange(length)
    conv_masks = []
    for j in range(1, 4):
        earlier = jnp.pad(segment_ids, ((0, 0), (j, 0)), constant_values=-1)[:, :length]
        conv_masks.append(earlier == segment_ids)
    blocks = segment_ids.reshape(seqs, length // chunk, chunk)
    finals = blocks[:, :, -1]
    before = jnp.concatenate([segment_ids[:, :1], finals[:, :-1]], axis=1)
    carried = (blocks == before[:, :, None]).reshape(seqs, length)
    tailed = (blocks == finals[:, :, None]).reshape(seqs, length)
    zero = jnp.zeros((seqs, length), F32)
    ids = segment_ids.astype(F32)
    rows = jnp.stack([carried.astype(F32), tailed.astype(F32), ids] + [zero] * 5, axis=1)
    cols = jnp.stack([m.astype(F32) for m in conv_masks] + [ids] + [zero] * 4, axis=2)
    return cols, rows


def delta_forward(proj, taps_qk, taps_v, head_table, gain, tables, seqs, heads, chunk, refine):
    cols, rows = tables
    length = cols.shape[1]
    dk, dv = taps_qk.shape[2] // heads, taps_v.shape[1] // heads
    chunks = length // chunk
    tokens = seqs * length
    column = pl.BlockSpec((length, dv), lambda s, h: (s, h))
    return pl.pallas_call(
        functools.partial(forward_kernel, chunk, refine),
        grid=(seqs, heads),
        in_specs=specs(length, heads, dk, dv),
        out_specs=[
            column, column, column,
            pl.BlockSpec((1, 1, chunks, chunk, chunk), lambda s, h: (s, h, 0, 0, 0)),
            pl.BlockSpec((1, 1, chunks, dk, dv), lambda s, h: (s, h, 0, 0, 0)),
        ],
        out_shape=[
            jax.ShapeDtypeStruct((tokens, heads * dv), BF16),
            jax.ShapeDtypeStruct((tokens, heads * dv), F32),
            jax.ShapeDtypeStruct((tokens, heads * dv), F32),
            jax.ShapeDtypeStruct((seqs, heads, chunks, chunk, chunk), F32),
            jax.ShapeDtypeStruct((seqs, heads, chunks, dk, dv), F32),
        ],
        compiler_params=pltpu.CompilerParams(vmem_limit_bytes=48 * 2**20),
        name="delta_forward",
    )(proj, proj, proj, proj, proj, taps_qk, taps_v, head_table, gain, cols, rows)


def delta_backward(proj, taps_qk, taps_v, head_table, gain, tables, saved, dmix, seqs, heads, chunk):
    cols, rows = tables
    length = cols.shape[1]
    dk, dv = taps_qk.shape[2] // heads, taps_v.shape[1] // heads
    chunks = length // chunk
    tokens = seqs * length
    width = proj.shape[1]
    column = pl.BlockSpec((length, dv), lambda s, h: (s, h))
    return pl.pallas_call(
        functools.partial(backward_kernel, chunk, heads),
        grid=(seqs, heads),
        in_specs=specs(length, heads, dk, dv)
        + [
            column, column,
            pl.BlockSpec((1, 1, chunks, chunk, chunk), lambda s, h: (s, h, 0, 0, 0)),
            pl.BlockSpec((1, 1, chunks, dk, dv), lambda s, h: (s, h, 0, 0, 0)),
            column,
        ],
        out_specs=[
            pl.BlockSpec((length, width), lambda s, h: (s, 0)),
            pl.BlockSpec((1, 2, 4, dk), lambda s, h: (s, 0, 0, h)),
            pl.BlockSpec((1, 4, dv), lambda s, h: (s, 0, h)),
            pl.BlockSpec((1, 1, 8, 128), lambda s, h: (s, h, 0, 0)),
            pl.BlockSpec((1, 1, 1, dv), lambda s, h: (s, h, 0, 0)),
        ],
        out_shape=[
            jax.ShapeDtypeStruct((tokens, width), BF16),
            jax.ShapeDtypeStruct((seqs, 2, 4, heads * dk), F32),
            jax.ShapeDtypeStruct((seqs, 4, heads * dv), F32),
            jax.ShapeDtypeStruct((seqs, heads, 8, 128), F32),
            jax.ShapeDtypeStruct((seqs, heads, 1, dv), F32),
        ],
        compiler_params=pltpu.CompilerParams(vmem_limit_bytes=56 * 2**20),
        name="delta_backward",
    )(proj, proj, proj, proj, proj, taps_qk, taps_v, head_table, gain, cols, rows, *saved, dmix)


LAYERS = 2
CHUNK = 128
REFINE = 1


def rms_gain(matrix, gain_vector):
    scaling = lax.rsqrt(jnp.mean(matrix * matrix, axis=-1, keepdims=True) + EPS)
    return matrix * scaling * gain_vector


def times_transposed(left, right):
    return lax.dot_general(left, right, NT, preferred_element_type=F32)


def over_rows(left, right):
    return lax.dot_general(left, right, TN, preferred_element_type=F32)


def times(left, right):
    return jnp.dot(left, right, preferred_element_type=F32)


def padded(matrix, width):
    return jnp.pad(matrix, ((0, 0), (0, width - matrix.shape[1])))


def up_to(size, unit):
    return -(-size // unit) * unit


def body(
    tokens,
    segment_ids,
    query_weight,
    key_weight,
    value_weight,
    gate_weight,
    decay_weight,
    out_weight,
    swiglu_gate,
    swiglu_up,
    swiglu_down,
    conv_query_key,
    conv_value,
    head_params,
    norm_gains,
    out_gain,
    cotangent,
):
    seqs, length = segment_ids.shape
    heads = head_params.shape[2]
    qk_width, v_width, pair_width = query_weight.shape[2], value_weight.shape[2], decay_weight.shape[2]
    hidden_width = swiglu_gate.shape[2]
    hidden_pad = up_to(hidden_width, 128)
    in_width = 2 * qk_width + 2 * v_width + 128
    tables = segment_tables(segment_ids, CHUNK)

    def gathered(matrix):
        return lax.all_gather(matrix, "dp", axis=0, tiled=True)

    def layer_weights(l):
        low = lambda m: m[l].astype(BF16)
        first = gathered(jnp.concatenate(
            [low(query_weight), low(key_weight), low(value_weight), low(gate_weight), padded(low(decay_weight), 128)], axis=1
        ))
        second = gathered(jnp.concatenate(
            [low(out_weight), padded(low(swiglu_gate), hidden_pad), padded(low(swiglu_up), hidden_pad),
             padded(low(swiglu_down), hidden_pad)], axis=1
        ))
        return (
            first, second[:, :v_width], second[:, v_width : v_width + 2 * hidden_pad], second[:, v_width + 2 * hidden_pad :]
        )

    def spread(matrix):
        return lax.all_gather(matrix.astype(BF16), "tensor", axis=0, tiled=True)

    def collect(term):
        return lax.psum_scatter(term.astype(BF16), "tensor", scatter_dimension=0, tiled=True).astype(F32)

    residual = tokens.astype(F32)
    kept = []
    for l in range(LAYERS):
        w_in, w_out, w_up, w_down = layer_weights(l)
        first_norm, first_back = jax.vjp(rms_gain, residual, norm_gains[l, 0])
        normed = spread(first_norm)
        proj = times(normed, w_in)
        small = (conv_query_key[l], conv_value[l], head_params[l], out_gain[l][None])
        mixer, *saved = delta_forward(proj, *small, tables, seqs, heads, CHUNK, REFINE)
        middle = residual + collect(times_transposed(mixer, w_out))
        second_norm, second_back = jax.vjp(rms_gain, middle, norm_gains[l, 1])
        normed_ffn = spread(second_norm)
        pre = times(normed_ffn, w_up)
        hidden = (jax.nn.silu(pre[:, :hidden_pad]) * pre[:, hidden_pad:]).astype(BF16)
        residual = middle + collect(times_transposed(hidden, w_down))
        kept.append((w_in, w_out, w_up, w_down, first_back, normed, proj, small, mixer, saved, second_back, normed_ffn, pre, hidden))
    grad = cotangent.astype(F32)
    ffn_grads, mixer_grads, tap_grads, norm_grads, gain_grads = ([None] * LAYERS for _ in range(5))
    for l in reversed(range(LAYERS)):
        w_in, w_out, w_up, w_down, first_back, normed, proj, small, mixer, saved, second_back, normed_ffn, pre, hidden = kept[l]
        ffn_cot = spread(grad)
        down_grad = over_rows(ffn_cot, hidden)
        d_hidden = times(ffn_cot, w_down)
        gate_pre, up_pre = pre[:, :hidden_pad], pre[:, hidden_pad:]
        sig = jax.nn.sigmoid(gate_pre)
        d_pre = jnp.concatenate(
            [d_hidden * up_pre * sig * (1.0 + gate_pre * (1.0 - sig)), d_hidden * gate_pre * sig], axis=1
        ).astype(BF16)
        d_middle, second_gain = second_back(collect(times_transposed(d_pre, w_up)))
        up_grad = over_rows(normed_ffn, d_pre)
        ffn_grads[l] = lax.psum_scatter(
            jnp.concatenate([down_grad, up_grad], axis=1).astype(BF16), "dp", scatter_dimension=0, tiled=True
        )
        grad = grad + d_middle
        mixer_cot = spread(grad)
        d_mixer = times(mixer_cot, w_out)
        d_proj, d_qk, d_v, d_head, d_gain = delta_backward(
            proj, *small, tables, saved, d_mixer, seqs, heads, CHUNK
        )
        d_input, first_gain = first_back(collect(times_transposed(d_proj, w_in)))
        out_grad = over_rows(mixer_cot, mixer)
        in_grad = over_rows(normed, d_proj)
        mixer_grads[l] = lax.psum_scatter(
            jnp.concatenate([out_grad, in_grad], axis=1).astype(BF16), "dp", scatter_dimension=0, tiled=True
        )
        grad = grad + d_input
        tap_grads[l] = (d_qk.sum(0), d_v.sum(0), d_head.sum(0)[:, :2, 0].T)
        norm_grads[l] = jnp.stack([first_gain, second_gain])
        gain_grads[l] = d_gain.sum((0, 1, 2))

    def columns(parts, start, width):
        return jnp.stack([part[:, start : start + width] for part in parts]).astype(F32)

    at = v_width
    in_grads = []
    for width in (qk_width, qk_width, v_width, v_width, pair_width):
        in_grads.append(columns(mixer_grads, at, width))
        at += width
    out_grad = columns(mixer_grads, 0, v_width)
    down_grad = columns(ffn_grads, 0, hidden_width)
    gate_grad = columns(ffn_grads, hidden_pad, hidden_width)
    up_grad = columns(ffn_grads, 2 * hidden_pad, hidden_width)
    taps = tuple(jnp.stack([tap_grads[l][i] for l in range(LAYERS)]) for i in range(3))
    taps = lax.psum(taps, "dp")
    norms = lax.psum((jnp.stack(norm_grads), jnp.stack(gain_grads)), ("dp", "tensor"))
    return (residual, grad, *in_grads, out_grad, gate_grad, up_grad, down_grad, *taps, *norms)


def solution(mesh):
    rows = P(("dp", "tensor"), None)
    weight = P(None, "dp", "tensor")
    small = (P(None, None, None, "tensor"), P(None, None, "tensor"), P(None, None, "tensor"), P(), P())
    return jax.shard_map(
        body,
        mesh=mesh,
        in_specs=(rows, P("dp", None)) + (weight,) * 9 + small + (rows,),
        out_specs=(rows, rows) + (weight,) * 9 + small,
        check_vma=False,
    )
```

```python
import functools
import jax
import jax.numpy as jnp
from jax import lax
from jax.experimental import pallas as pl
from jax.experimental.pallas import tpu as pltpu
from jax.sharding import PartitionSpec as P

F32 = jnp.float32
BF16 = jnp.bfloat16
NN = (((1,), (0,)), ((), ()))
NT = (((1,), (1,)), ((), ()))
TN = (((0,), (0,)), ((), ()))
EPS = 1e-6
FLOOR = 0.01


def split(x):
    high = x.astype(BF16)
    return high, (x - high.astype(F32)).astype(BF16)


def mm(a, b, dims, passes=1):
    def one(p, q):
        return lax.dot_general(p, q, dims, preferred_element_type=F32)

    if passes == 1:
        return one(a.astype(BF16), b.astype(BF16))
    ah, al = split(a)
    bh, bl = split(b)
    return one(ah, bh) + (one(ah, bl) + one(al, bh))


def iota(shape, axis):
    return lax.broadcasted_iota(jnp.int32, shape, axis)


def shifted_rows(x, by):
    return pltpu.roll(x, by % x.shape[0], 0) if by else x


def conv(signal, taps, masks):
    total = signal * taps[0:1]
    for j in range(1, 4):
        total = total + shifted_rows(signal, j) * masks[j - 1] * taps[j : j + 1]
    return total


def chunk_scan(row, chunk, backward=False):
    length = row.shape[1]
    place = iota(row.shape, 1) % chunk
    step = 1
    while step < chunk:
        if backward:
            moved = pltpu.roll(row, length - step, 1)
            row = row + jnp.where(place < chunk - step, moved, 0.0)
        else:
            moved = pltpu.roll(row, step, 1)
            row = row + jnp.where(place >= step, moved, 0.0)
        step *= 2
    return row


def unit_lower_inverse(lower, refine):
    size = lower[0].shape[0]
    rows, cols = iota((size, size), 0), iota((size, size), 1)
    eye = (rows == cols).astype(F32)

    def off(block):
        return ((rows // (2 * block) == cols // (2 * block)) & (rows // block != cols // block)).astype(F32)

    found = [eye - part * off(1) for part in lower]
    block = 2
    while block < size:
        mask = off(block)
        half = [mm(x, part * mask, NN) for x, part in zip(found, lower)]
        found = [x - mm(t, x, NN) for x, t in zip(found, half)]
        block *= 2
    for _ in range(refine):
        rest = [(x - eye) + mm(part, x, NN, 3) for x, part in zip(found, lower)]
        found = [x - mm(x, r, NN, 1) for x, r in zip(found, rest)]
    return found


def prepared(head, chunk, qref, kref, vref, pair_ref, tap_qk, tap_v, head_table, col_info, row_info):
    length, dk = qref.shape
    masks = [col_info[:, j : j + 1] for j in range(3)]
    masks = [jnp.broadcast_to(m, (length, dk)) for m in masks]
    dv = vref.shape[1]
    wide = [jnp.concatenate([m] * (dv // dk), axis=1) for m in masks]
    pre_q = conv(qref[...], tap_qk[0], masks)
    pre_k = conv(kref[...], tap_qk[1], masks)
    pre_v = conv(vref[...], tap_v[...], wide)
    out = dict(masks=masks, wide=wide, pre_q=pre_q, pre_k=pre_k, pre_v=pre_v)
    for name, pre in (("q", pre_q), ("k", pre_k), ("v", pre_v)):
        sig = lax.logistic(pre)
        out["sig_" + name] = sig
        out["act_" + name] = pre * sig
    out["inv_q"] = lax.rsqrt(jnp.sum(out["act_q"] ** 2, axis=1, keepdims=True) + EPS)
    out["inv_k"] = lax.rsqrt(jnp.sum(out["act_k"] ** 2, axis=1, keepdims=True) + EPS)
    out["q"] = out["act_q"] * out["inv_q"] * dk ** (-0.5)
    out["k"] = out["act_k"] * out["inv_k"]
    out["v"] = out["act_v"]
    pair = jnp.transpose(pair_ref[...])
    picked = iota(pair.shape, 0)
    a_row = jnp.sum(jnp.where(picked == 2 * head, pair, 0.0), axis=0, keepdims=True)
    b_row = jnp.sum(jnp.where(picked == 2 * head + 1, pair, 0.0), axis=0, keepdims=True)
    rate = jnp.exp(jnp.full((1, length), head_table[0, head], F32))
    a_row = a_row + head_table[1, head]
    softplus = jnp.maximum(a_row, 0.0) + jnp.log1p(jnp.exp(-jnp.abs(a_row)))
    decay = -rate * softplus
    beta = lax.logistic(b_row)
    total = chunk_scan(decay, chunk)
    entry = jnp.exp(total) * row_info[0:1]
    chunks = length // chunk
    place = iota((1, length), 1)
    ends = [total[:, (i + 1) * chunk - 1 : (i + 1) * chunk] for i in range(chunks)]
    last = ends[0]
    for i in range(1, chunks):
        last = jnp.where(place >= i * chunk, ends[i], jnp.broadcast_to(last, (1, length)))
    tail = jnp.exp(last - total) * row_info[1:2]
    rows = jnp.concatenate([beta, total, entry, tail, jnp.zeros((124, length), F32)], axis=0)
    cols = jnp.transpose(rows)
    out.update(
        a_row=a_row, rate=rate, decay=decay, beta_row=beta, total_row=total, entry_row=entry, tail_row=tail,
        beta=cols[:, 0:1], total=cols[:, 1:2], entry=cols[:, 2:3], tail=cols[:, 3:4],
    )
    return out


def chunk_parts(pre, i, chunk, col_info, row_info):
    s = slice(i * chunk, (i + 1) * chunk)
    q, k, v = pre["q"][s], pre["k"][s], pre["v"][s]
    beta, total, entry, tail = pre["beta"][s], pre["total"][s], pre["entry"][s], pre["tail"][s]
    rows, cols = iota((chunk, chunk), 0), iota((chunk, chunk), 1)
    allowed = (col_info[s, 3:4] == row_info[2:3, s]) & (rows >= cols)
    fading = jnp.where(allowed, jnp.exp(jnp.where(allowed, total - pre["total_row"][:, s], 0.0)), 0.0)
    both = mm(jnp.concatenate([q, k], axis=0), k, NT)
    strict_fading = jnp.where(rows > cols, fading, 0.0)
    qk, kk = both[:chunk], both[chunk:]
    return dict(
        q=q, k=k, v=v, beta=beta, entry=entry, tail=tail, fading=fading, strict=strict_fading,
        mixed=qk * fading, kk_faded=kk * strict_fading, lower=beta * (kk * strict_fading),
        exit=pre["entry_row"][:, (i + 1) * chunk - 1 : (i + 1) * chunk], rows=s,
    )


def forward_kernel(
    chunk, refine, qref, kref, vref, gref, pair_ref, tap_qk, tap_v, head_table, gain, col_ref, row_ref,
    mix_ref, rec_ref, fix_ref, inv_ref, state_ref,
):
    head = pl.program_id(1)
    col_info, row_info = col_ref[0], row_ref[0]
    pre = prepared(head, chunk, qref, kref, vref, pair_ref, tap_qk, tap_v, head_table, col_info, row_info)
    length, dk = qref.shape
    dv = vref.shape[1]
    chunks = length // chunk
    parts = [chunk_parts(pre, i, chunk, col_info, row_info) for i in range(chunks)]
    inverses = unit_lower_inverse([p["lower"] for p in parts], refine)
    state = jnp.zeros((dk, dv), F32)
    steps = []
    for p, inverse in zip(parts, inverses):
        target = jnp.concatenate([p["beta"] * p["entry"] * p["k"], p["beta"] * p["v"]], axis=1)
        solved = mm(inverse, target, NN)
        pushed = mm(p["k"] * p["tail"], solved, TN)
        steps.append((solved, pushed))
    states = []
    for p, (solved, pushed) in zip(parts, steps):
        states.append(state)
        state = p["exit"] * state - mm(pushed[:, :dk], state, NN) + pushed[:, dk:]
    gain_row = gain[...]
    for i, (p, inverse, (solved, pushed)) in enumerate(zip(parts, inverses, steps)):
        seen = mm(jnp.concatenate([solved[:, :dk], p["q"] * p["entry"]], axis=0), states[i], NN)
        fixed = solved[:, dk:] - seen[:chunk]
        rec = seen[chunk:] + mm(p["mixed"], fixed, NN)
        s = p["rows"]
        rec_ref[s, :] = rec
        fix_ref[s, :] = fixed
        inv_ref[0, 0, i] = inverse
        state_ref[0, 0, i] = states[i]
        normal = rec * lax.rsqrt(jnp.mean(rec * rec, axis=1, keepdims=True) + FLOOR)
        gate = gref[s, :]
        mix_ref[s, :] = (normal * gain_row * (gate * lax.logistic(gate))).astype(BF16)


def silu_grad(pre, sig):
    return sig * (1.0 + pre * (1.0 - sig))


def backward_kernel(
    chunk, heads, qref, kref, vref, gref, pair_ref, tap_qk, tap_v, head_table, gain, col_ref, row_ref,
    rec_ref, fix_ref, inv_ref, state_ref, dmix_ref,
    dproj_ref, dtap_qk, dtap_v, dhead_ref, dgain_ref,
):
    seq, head = pl.program_id(0), pl.program_id(1)
    col_info, row_info = col_ref[0], row_ref[0]
    pre = prepared(head, chunk, qref, kref, vref, pair_ref, tap_qk, tap_v, head_table, col_info, row_info)
    length, dk = qref.shape
    dv = vref.shape[1]
    chunks = length // chunk
    parts = [chunk_parts(pre, i, chunk, col_info, row_info) for i in range(chunks)]
    gain_row = gain[...]
    dgain = jnp.zeros((1, dv), F32)
    v_at = 2 * heads * dk
    g_at = v_at + heads * dv
    p_at = g_at + heads * dv
    for p in parts:
        s = p["rows"]
        rec, gate, dmix = rec_ref[s, :], gref[s, :], dmix_ref[s, :]
        scale = lax.rsqrt(jnp.mean(rec * rec, axis=1, keepdims=True) + FLOOR)
        sig = lax.logistic(gate)
        gated = dmix * (gate * sig)
        normal = rec * scale
        dgain = dgain + jnp.sum(gated * normal, axis=0, keepdims=True)
        dgate = dmix * normal * gain_row * silu_grad(gate, sig)
        dproj_ref[s, pl.ds(pl.multiple_of(g_at + head * dv, dv), dv)] = dgate.astype(BF16)
        dn = gated * gain_row
        p["drec"] = scale * dn - rec * (scale * scale * scale) * jnp.mean(dn * rec, axis=1, keepdims=True)
    for i, p in enumerate(parts):
        inverse = inv_ref[0, 0, i]
        p["inverse"] = inverse
        solved = mm(inverse, p["beta"] * p["entry"] * p["k"], NN)
        back = mm(p["mixed"], p["drec"], TN)
        p["back"] = back
        ahead = mm(solved, p["k"] * p["tail"], TN)
        given = mm(
            jnp.concatenate([p["q"] * p["entry"], -solved], axis=0),
            jnp.concatenate([p["drec"], back], axis=0), TN,
        )
        p["ahead"], p["given"] = ahead, given
    dstate = jnp.zeros((dk, dv), F32)
    for p in reversed(parts):
        p["dstate"] = dstate
        dstate = p["exit"] * dstate - mm(p["ahead"], dstate, NN) + p["given"]
    cols = iota((chunk, 8), 1)
    col_parts, row_parts, dqs, dks, dvs = [], [], [], [], []
    for i, p in enumerate(parts):
        s = p["rows"]
        state, dstate, fixed, drec = state_ref[0, 0, i], p["dstate"], fix_ref[s, :], p["drec"]
        q, k, v, beta, entry, tail = p["q"], p["k"], p["v"], p["beta"], p["entry"], p["tail"]
        dfixed = p["back"] + mm(k * tail, dstate, NN)
        dtarget = mm(p["inverse"], dfixed, TN)
        outer = mm(
            jnp.concatenate([drec, dtarget], axis=0), jnp.concatenate([state, fixed], axis=0), NT
        )
        drec_state, dtarget_state = outer[:chunk, :dk], outer[chunk:, :dk]
        dmixed, dlower = outer[:chunk, dk:], -outer[chunk:, dk:]
        fixed_dstate = mm(fixed, dstate, NT)
        g1 = dmixed * p["fading"]
        g2 = (beta * dlower) * p["strict"]
        stacked = jnp.concatenate([g1, g2], axis=0)
        first = mm(stacked, k, NN)
        second = mm(stacked, jnp.concatenate([q, k], axis=0), TN)
        key_state = jnp.sum(dtarget_state * k, axis=1, keepdims=True)
        dqs.append(entry * drec_state + first[:chunk])
        dks.append(first[chunk:] + second + tail * fixed_dstate - (beta * entry) * dtarget_state)
        dvs.append(beta * dtarget)
        dentry = jnp.sum(drec_state * q, axis=1, keepdims=True) - beta * key_state
        dtail = jnp.sum(fixed_dstate * k, axis=1, keepdims=True) * tail
        high = dmixed * p["mixed"] + dlower * p["lower"]
        dbeta = (
            jnp.sum(dtarget * v, axis=1, keepdims=True)
            - entry * key_state
            + jnp.sum(dlower * p["kk_faded"], axis=1, keepdims=True)
        )
        dtotal = jnp.sum(high, axis=1, keepdims=True) + dentry * entry - dtail
        end = p["exit"] * jnp.sum(jnp.sum(dstate * state, axis=1, keepdims=True), axis=0, keepdims=True)
        end = end + jnp.sum(dtail, axis=0, keepdims=True)
        dtotal = dtotal + jnp.where(iota((chunk, 1), 0) == chunk - 1, end, 0.0)
        row_parts.append(jnp.sum(high, axis=0, keepdims=True))
        col_parts.append(jnp.where(cols == 0, dtotal, jnp.where(cols == 1, dbeta, 0.0)))
    lanes = jnp.concatenate(col_parts, axis=0)
    lanes = jnp.concatenate([lanes, jnp.zeros((length, 120), F32)], axis=1)
    turned = jnp.transpose(lanes)
    dtotal_row = turned[0:1] - jnp.concatenate(row_parts, axis=1)
    dbeta_row = turned[1:2]
    ddecay = chunk_scan(dtotal_row, chunk, backward=True)
    da = -ddecay * pre["rate"] * lax.logistic(pre["a_row"])
    db = dbeta_row * pre["beta_row"] * (1.0 - pre["beta_row"])
    spread = iota((128, length), 0)
    dpair = jnp.where(spread == 2 * head, da, jnp.where(spread == 2 * head + 1, db, 0.0))
    dpair = jnp.transpose(dpair).astype(BF16)

    @pl.when(head == 0)
    def _():
        dproj_ref[:, p_at:] = dpair

    @pl.when(head != 0)
    def _():
        dproj_ref[:, p_at:] = dproj_ref[:, p_at:] + dpair

    dscale = jnp.sum(ddecay * pre["decay"], axis=1, keepdims=True)
    dbias = jnp.sum(da, axis=1, keepdims=True)
    which = iota((8, 128), 0)
    dhead = jnp.where(which == 0, dscale, jnp.where(which == 1, dbias, 0.0))
    dq, dk_all, dv_all = (jnp.concatenate(x, axis=0) for x in (dqs, dks, dvs))

    def through_norm(grad, act, inv, factor):
        return factor * (inv * grad - act * (inv * inv * inv) * jnp.sum(grad * act, axis=1, keepdims=True))

    dq = through_norm(dq, pre["act_q"], pre["inv_q"], dk ** (-0.5))
    dk_all = through_norm(dk_all, pre["act_k"], pre["inv_k"], 1.0)
    taps_out = []
    for grad, name, src, taps, masks, at in (
        (dq, "q", qref, tap_qk[0], pre["masks"], head * dk),
        (dk_all, "k", kref, tap_qk[1], pre["masks"], heads * dk + head * dk),
        (dv_all, "v", vref, tap_v[...], pre["wide"], v_at + head * dv),
    ):
        dpre = grad * silu_grad(pre["pre_" + name], pre["sig_" + name])
        signal = src[...]
        dsignal = dpre * taps[0:1]
        dtaps = [jnp.sum(dpre * signal, axis=0, keepdims=True)]
        for j in range(1, 4):
            masked = dpre * masks[j - 1]
            dsignal = dsignal + shifted_rows(masked, -j) * taps[j : j + 1]
            dtaps.append(jnp.sum(masked * shifted_rows(signal, j), axis=0, keepdims=True))
        width = grad.shape[1]
        dproj_ref[:, pl.ds(pl.multiple_of(at, width), width)] = dsignal.astype(BF16)
        taps_out.append(jnp.concatenate(dtaps, axis=0))
    dtap_qk[0, 0] = taps_out[0]
    dtap_qk[0, 1] = taps_out[1]
    dtap_v[0] = taps_out[2]
    dhead_ref[0, 0] = dhead
    dgain_ref[0, 0] = dgain


def specs(length, heads, dk, dv):
    v_block = 2 * heads * dk // dv
    return [
        pl.BlockSpec((length, dk), lambda s, h: (s, h)),
        pl.BlockSpec((length, dk), lambda s, h: (s, heads + h)),
        pl.BlockSpec((length, dv), lambda s, h: (s, v_block + h)),
        pl.BlockSpec((length, dv), lambda s, h: (s, v_block + heads + h)),
        pl.BlockSpec((length, 128), lambda s, h: (s, (2 * heads * dk + 2 * heads * dv) // 128)),
        pl.BlockSpec((2, 4, dk), lambda s, h: (0, 0, h)),
        pl.BlockSpec((4, dv), lambda s, h: (0, h)),
        pl.BlockSpec(memory_space=pltpu.SMEM),
        pl.BlockSpec((1, dv), lambda s, h: (0, 0)),
        pl.BlockSpec((1, length, 8), lambda s, h: (s, 0, 0)),
        pl.BlockSpec((1, 8, length), lambda s, h: (s, 0, 0)),
    ]


def segment_tables(segment_ids, chunk):
    seqs, length = segment_ids.shape
    place = jnp.arange(length)
    conv_masks = []
    for j in range(1, 4):
        earlier = jnp.pad(segment_ids, ((0, 0), (j, 0)), constant_values=-1)[:, :length]
        conv_masks.append(earlier == segment_ids)
    blocks = segment_ids.reshape(seqs, length // chunk, chunk)
    finals = blocks[:, :, -1]
    before = jnp.concatenate([segment_ids[:, :1], finals[:, :-1]], axis=1)
    carried = (blocks == before[:, :, None]).reshape(seqs, length)
    tailed = (blocks == finals[:, :, None]).reshape(seqs, length)
    zero = jnp.zeros((seqs, length), F32)
    ids = segment_ids.astype(F32)
    rows = jnp.stack([carried.astype(F32), tailed.astype(F32), ids] + [zero] * 5, axis=1)
    cols = jnp.stack([m.astype(F32) for m in conv_masks] + [ids] + [zero] * 4, axis=2)
    return cols, rows


def delta_forward(proj, taps_qk, taps_v, head_table, gain, tables, seqs, heads, chunk, refine):
    cols, rows = tables
    length = cols.shape[1]
    dk, dv = taps_qk.shape[2] // heads, taps_v.shape[1] // heads
    chunks = length // chunk
    tokens = seqs * length
    column = pl.BlockSpec((length, dv), lambda s, h: (s, h))
    return pl.pallas_call(
        functools.partial(forward_kernel, chunk, refine),
        grid=(seqs, heads),
        in_specs=specs(length, heads, dk, dv),
        out_specs=[
            column, column, column,
            pl.BlockSpec((1, 1, chunks, chunk, chunk), lambda s, h: (s, h, 0, 0, 0)),
            pl.BlockSpec((1, 1, chunks, dk, dv), lambda s, h: (s, h, 0, 0, 0)),
        ],
        out_shape=[
            jax.ShapeDtypeStruct((tokens, heads * dv), BF16),
            jax.ShapeDtypeStruct((tokens, heads * dv), F32),
            jax.ShapeDtypeStruct((tokens, heads * dv), F32),
            jax.ShapeDtypeStruct((seqs, heads, chunks, chunk, chunk), F32),
            jax.ShapeDtypeStruct((seqs, heads, chunks, dk, dv), F32),
        ],
        compiler_params=pltpu.CompilerParams(vmem_limit_bytes=48 * 2**20),
        name="delta_forward",
    )(proj, proj, proj, proj, proj, taps_qk, taps_v, head_table, gain, cols, rows)


def delta_backward(proj, taps_qk, taps_v, head_table, gain, tables, saved, dmix, seqs, heads, chunk):
    cols, rows = tables
    length = cols.shape[1]
    dk, dv = taps_qk.shape[2] // heads, taps_v.shape[1] // heads
    chunks = length // chunk
    tokens = seqs * length
    width = proj.shape[1]
    column = pl.BlockSpec((length, dv), lambda s, h: (s, h))
    return pl.pallas_call(
        functools.partial(backward_kernel, chunk, heads),
        grid=(seqs, heads),
        in_specs=specs(length, heads, dk, dv)
        + [
            column, column,
            pl.BlockSpec((1, 1, chunks, chunk, chunk), lambda s, h: (s, h, 0, 0, 0)),
            pl.BlockSpec((1, 1, chunks, dk, dv), lambda s, h: (s, h, 0, 0, 0)),
            column,
        ],
        out_specs=[
            pl.BlockSpec((length, width), lambda s, h: (s, 0)),
            pl.BlockSpec((1, 2, 4, dk), lambda s, h: (s, 0, 0, h)),
            pl.BlockSpec((1, 4, dv), lambda s, h: (s, 0, h)),
            pl.BlockSpec((1, 1, 8, 128), lambda s, h: (s, h, 0, 0)),
            pl.BlockSpec((1, 1, 1, dv), lambda s, h: (s, h, 0, 0)),
        ],
        out_shape=[
            jax.ShapeDtypeStruct((tokens, width), BF16),
            jax.ShapeDtypeStruct((seqs, 2, 4, heads * dk), F32),
            jax.ShapeDtypeStruct((seqs, 4, heads * dv), F32),
            jax.ShapeDtypeStruct((seqs, heads, 8, 128), F32),
            jax.ShapeDtypeStruct((seqs, heads, 1, dv), F32),
        ],
        compiler_params=pltpu.CompilerParams(vmem_limit_bytes=56 * 2**20),
        name="delta_backward",
    )(proj, proj, proj, proj, proj, taps_qk, taps_v, head_table, gain, cols, rows, *saved, dmix)


MESH = pl.DeviceIdType.MESH
VMEM_LIMIT = 58 * 2**20
HALVES = 2


class Line:
    def __init__(self, send_sem, recv_sem):
        self.send_sem, self.recv_sem = send_sem, recv_sem
        self.me = lax.axis_index("tensor")

    def greet(self):
        barrier = pltpu.get_barrier_semaphore()
        for m in range(4):
            @pl.when(self.me == m)
            def _():
                others = [t for t in range(4) if t != m and {t, m} != {0, 3}]
                for t in others:
                    pl.semaphore_signal(barrier, inc=1, device_id={"tensor": t}, device_id_type=MESH)
                pl.semaphore_wait(barrier, len(others))

    def copy(self, phase, source, target, to, send_at, recv_at):
        return pltpu.make_async_remote_copy(
            src_ref=source, dst_ref=target, send_sem=self.send_sem.at[phase, send_at],
            recv_sem=self.recv_sem.at[phase, recv_at], device_id={"tensor": to}, device_id_type=MESH,
        )

    def gather_start(self, phase, blocks):
        for m in range(4):
            @pl.when(self.me == m)
            def _():
                for t in range(4):
                    if t != m and {t, m} != {0, 3}:
                        self.copy(phase, blocks[m], blocks[m], t, t, m).start()

    def gather_finish(self, phase, blocks):
        for m in range(4):
            @pl.when(self.me == m)
            def _():
                if m in (1, 2):
                    far, to = (3, 0) if m == 1 else (0, 3)
                    self.copy(phase, blocks[far], blocks[far], to, m, far).wait_recv()
                    self.copy(phase, blocks[far], blocks[far], to, m, far).start()
                for b in range(4):
                    if b != m and not (m in (1, 2) and b == (3 if m == 1 else 0)):
                        self.copy(phase, blocks[b], blocks[b], b, b, b).wait_recv()

    def gather_drain(self, phase, blocks):
        for m in range(4):
            @pl.when(self.me == m)
            def _():
                for t in range(4):
                    if t != m and {t, m} != {0, 3}:
                        self.copy(phase, blocks[m], blocks[m], t, t, m).wait_send()
                if m in (1, 2):
                    far, to = (3, 0) if m == 1 else (0, 3)
                    self.copy(phase, blocks[far], blocks[far], to, m, far).wait_send()

    def scatter_start(self, phase, parts, slots):
        for m in range(4):
            @pl.when(self.me == m)
            def _():
                if m in (0, 3):
                    through = 1 if m == 0 else 2
                    self.copy(phase, parts[3 - m], slots[4], through, 3 - m, 4).start()
                for t in range(4):
                    if t != m and {t, m} != {0, 3}:
                        if not (m in (1, 2) and t == (3 if m == 1 else 0)):
                            self.copy(phase, parts[t], slots[m], t, t, m).start()

    def scatter_relay(self, phase, parts, slots):
        for m in (1, 2):
            @pl.when(self.me == m)
            def _():
                t = 3 if m == 1 else 0
                self.copy(phase, parts[t], slots[4], t, t, 4).wait_recv()
                parts[t][...] = (parts[t][...].astype(F32) + slots[4][...].astype(F32)).astype(BF16)
                self.copy(phase, parts[t], slots[m], t, t, m).start()

    def scatter_wait(self, phase, parts, slots):
        for m in range(4):
            @pl.when(self.me == m)
            def _():
                for s in range(4):
                    if s != m and {s, m} != {0, 3}:
                        self.copy(phase, parts[s], slots[s], s, s, s).wait_recv()

    def scatter_sum(self, total, parts, slots):
        for m in range(4):
            @pl.when(self.me == m)
            def _():
                value = parts[m][...].astype(F32)
                for s in range(4):
                    if s != m and {s, m} != {0, 3}:
                        value = value + slots[s][...].astype(F32)
                total[...] = value

    def scatter_drain(self, phase, parts, slots):
        for m in range(4):
            @pl.when(self.me == m)
            def _():
                for t in range(4):
                    if t != m:
                        self.copy(phase, parts[t], slots[m], t, t, m).wait_send()


def half_of(ref, h):
    value = ref[:, h]
    return value.reshape(value.shape[0] * value.shape[1], value.shape[2])


def blocks_of(ref, h):
    return [ref.at[b, h] for b in range(4)]


def parts_of(part, slots, k, h):
    return [part.at[k, h, t] for t in range(4)], [slots.at[k, h, s] for s in range(5)]


def for_tiles(size, tile, step):
    def run(i, carry):
        step(pl.multiple_of(i * tile, tile))
        return carry

    lax.fori_loop(0, size // tile, run, 0)


def partial_sums(left, weight, part, k, h):
    def step(n):
        value = lax.dot_general(left, weight[pl.ds(n, 256), :], NT, preferred_element_type=F32)
        part[k, h, :, :, pl.ds(n, 256)] = value.astype(BF16).reshape(4, left.shape[0] // 4, 256)

    for_tiles(weight.shape[0], 256, step)


def row_grads(left, right, out, column):
    rows = left.shape[0] * left.shape[1] * left.shape[2]
    width = right.shape[3]

    def piece(m):
        m = pl.multiple_of(m * 256, 256)
        turned = jnp.transpose(left[:, :, :, pl.ds(m, 256)].reshape(rows, 256))
        for n in range(0, width, 512):
            size = min(512, width - n)
            tile = right[:, :, :, n : n + size].reshape(rows, size)
            value = lax.dot_general(turned, tile, NN, preferred_element_type=F32)
            out[pl.ds(m, 256), column + n : column + n + size] = value.astype(BF16)

    return piece


def run_pieces(pieces, first, last):
    def run(m, carry):
        for piece in pieces:
            piece(m)
        return carry

    lax.fori_loop(first, last, run, 0)


def rms(value, gain):
    return value * lax.rsqrt(jnp.mean(value * value, axis=1, keepdims=True) + EPS) * gain


def rms_back(value, gain, grad):
    scale = lax.rsqrt(jnp.mean(value * value, axis=1, keepdims=True) + EPS)
    scaled = gain * grad
    back = scale * scaled - value * (scale * scale * scale) * jnp.mean(value * scaled, axis=1, keepdims=True)
    return back, jnp.sum(value * scale * grad, axis=0, keepdims=True)


def start_kernel(rows, cot, gain, normed, cot_all, send_sem, recv_sem):
    line = Line(send_sem, recv_sem)
    for h in range(HALVES):
        normed[line.me, h] = rms(rows[h].astype(F32), gain[...]).astype(BF16)
        cot_all[line.me, h] = cot[h]
    line.greet()
    for k, ref in ((0, normed), (2, cot_all)):
        for h in range(HALVES):
            line.gather_start(k + h, blocks_of(ref, h))
    for k, ref in ((0, normed), (2, cot_all)):
        for h in range(HALVES):
            line.gather_finish(k + h, blocks_of(ref, h))
    for k, ref in ((0, normed), (2, cot_all)):
        for h in range(HALVES):
            line.gather_drain(k + h, blocks_of(ref, h))


def ffn_forward_kernel(
    last, mixer, w_out, w_up, w_down, rows, gain, gain_next, middle, normed, pre, hidden, out_rows, *rest
):
    if last:
        part, slots, total, send_sem, recv_sem = rest
    else:
        normed_next, part, slots, total, send_sem, recv_sem = rest
    line = Line(send_sem, recv_sem)
    wide = w_down.shape[1]
    block = rows.shape[1]
    line.greet()
    for h in range(HALVES):
        partial_sums(half_of(mixer, h), w_out, part, 0, h)
        line.scatter_start(h, *parts_of(part, slots, 0, h))
    for h in range(HALVES):
        line.scatter_relay(h, *parts_of(part, slots, 0, h))
    for h in range(HALVES):
        both = parts_of(part, slots, 0, h)
        line.scatter_wait(h, *both)
        line.scatter_sum(total, *both)
        value = rows[h].astype(F32) + total[...]
        middle[h] = value
        normed[line.me, h] = rms(value, gain[...]).astype(BF16)
        line.gather_start(2 + h, blocks_of(normed, h))
    for h in range(HALVES):
        line.gather_finish(2 + h, blocks_of(normed, h))
        left = half_of(normed, h)

        def step(n):
            gate = jnp.dot(left, w_up[:, pl.ds(n, 256)], preferred_element_type=F32)
            up = jnp.dot(left, w_up[:, pl.ds(n + wide, 256)], preferred_element_type=F32)
            pre[:, h, :, pl.ds(n, 256)] = gate.reshape(4, block, 256)
            pre[:, h, :, pl.ds(n + wide, 256)] = up.reshape(4, block, 256)
            value = gate * lax.logistic(gate) * up
            hidden[:, h, :, pl.ds(n, 256)] = value.astype(BF16).reshape(4, block, 256)

        for_tiles(wide, 256, step)
        partial_sums(half_of(hidden, h), w_down, part, 1, h)
        line.scatter_start(4 + h, *parts_of(part, slots, 1, h))
    for h in range(HALVES):
        line.scatter_relay(4 + h, *parts_of(part, slots, 1, h))
    for h in range(HALVES):
        both = parts_of(part, slots, 1, h)
        line.scatter_wait(4 + h, *both)
        line.scatter_sum(total, *both)
        value = middle[h] + total[...]
        out_rows[h] = value
        if not last:
            normed_next[line.me, h] = rms(value, gain_next[...]).astype(BF16)
            line.gather_start(6 + h, blocks_of(normed_next, h))
    if not last:
        for h in range(HALVES):
            line.gather_finish(6 + h, blocks_of(normed_next, h))
    for h in range(HALVES):
        line.scatter_drain(h, *parts_of(part, slots, 0, h))
        line.gather_drain(2 + h, blocks_of(normed, h))
        line.scatter_drain(4 + h, *parts_of(part, slots, 1, h))
        if not last:
            line.gather_drain(6 + h, blocks_of(normed_next, h))


def ffn_backward_kernel(
    cot, hidden, pre, normed, middle, grad, gain, w_down, w_up, w_out,
    d_mixer, grads, mixer_cot, grad_out, d_gain, d_pre, part, slots, total, send_sem, recv_sem,
):
    line = Line(send_sem, recv_sem)
    wide = w_down.shape[1]
    block = middle.shape[1]
    line.greet()
    for h in range(HALVES):
        left = half_of(cot, h)

        def step(n):
            d_hidden = jnp.dot(left, w_down[:, pl.ds(n, 256)], preferred_element_type=F32)
            gate = pre[:, h, :, pl.ds(n, 256)].reshape(4 * block, 256)
            up = pre[:, h, :, pl.ds(n + wide, 256)].reshape(4 * block, 256)
            sig = lax.logistic(gate)
            d_gate = d_hidden * up * sig * (1.0 + gate * (1.0 - sig))
            d_up = d_hidden * gate * sig
            d_pre[:, h, :, pl.ds(n, 256)] = d_gate.astype(BF16).reshape(4, block, 256)
            d_pre[:, h, :, pl.ds(n + wide, 256)] = d_up.astype(BF16).reshape(4, block, 256)

        for_tiles(wide, 256, step)
        partial_sums(half_of(d_pre, h), w_up, part, 0, h)
        line.scatter_start(h, *parts_of(part, slots, 0, h))
    pieces = [row_grads(cot, hidden, grads, 0), row_grads(normed, d_pre, grads, wide)]
    run_pieces(pieces, 0, 2)
    for h in range(HALVES):
        line.scatter_relay(h, *parts_of(part, slots, 0, h))
    run_pieces(pieces, 2, 4)
    d_gain[...] = jnp.zeros_like(d_gain)
    for h in range(HALVES):
        both = parts_of(part, slots, 0, h)
        line.scatter_wait(h, *both)
        line.scatter_sum(total, *both)
        back, gain_part = rms_back(middle[h], gain[...], total[...])
        d_gain[...] += gain_part
        value = grad[h].astype(F32) + back
        grad_out[h] = value
        mixer_cot[line.me, h] = value.astype(BF16)
        line.gather_start(2 + h, blocks_of(mixer_cot, h))
    for h in range(HALVES):
        line.gather_finish(2 + h, blocks_of(mixer_cot, h))
        left = half_of(mixer_cot, h)
        for n in range(0, w_out.shape[1], 256):
            value = jnp.dot(left, w_out[:, n : n + 256], preferred_element_type=F32)
            d_mixer[:, h, :, n : n + 256] = value.reshape(4, block, 256)
    for h in range(HALVES):
        line.scatter_drain(h, *parts_of(part, slots, 0, h))
        line.gather_drain(2 + h, blocks_of(mixer_cot, h))


def mixer_backward_kernel(last, d_proj, w_in, normed, mixer, mixer_cot, rows, grad, gain, grad_out, d_gain, *rest):
    if last:
        part, slots, total, send_sem, recv_sem = rest
    else:
        grads, cot, part, slots, total, send_sem, recv_sem = rest
    line = Line(send_sem, recv_sem)
    line.greet()
    for h in range(HALVES):
        partial_sums(half_of(d_proj, h), w_in, part, 0, h)
        line.scatter_start(h, *parts_of(part, slots, 0, h))
    if not last:
        width = mixer.shape[3]
        pieces = [row_grads(mixer_cot, mixer, grads, 0), row_grads(normed, d_proj, grads, width)]
        run_pieces(pieces, 0, 2)
    for h in range(HALVES):
        line.scatter_relay(h, *parts_of(part, slots, 0, h))
    if not last:
        run_pieces(pieces, 2, 4)
    d_gain[...] = jnp.zeros_like(d_gain)
    for h in range(HALVES):
        both = parts_of(part, slots, 0, h)
        line.scatter_wait(h, *both)
        line.scatter_sum(total, *both)
        back, gain_part = rms_back(rows[h].astype(F32), gain[...], total[...])
        d_gain[...] += gain_part
        value = grad[h] + back
        grad_out[h] = value
        if not last:
            cot[line.me, h] = value.astype(BF16)
            line.gather_start(2 + h, blocks_of(cot, h))
    if not last:
        for h in range(HALVES):
            line.gather_finish(2 + h, blocks_of(cot, h))
    for h in range(HALVES):
        line.scatter_drain(h, *parts_of(part, slots, 0, h))
        if not last:
            line.gather_drain(2 + h, blocks_of(cot, h))


def line_call(kernel, operands, outs, scratch, phases, number, name):
    return pl.pallas_call(
        kernel,
        in_specs=[pl.BlockSpec(memory_space=pltpu.VMEM)] * len(operands),
        out_specs=[pl.BlockSpec(memory_space=pltpu.VMEM)] * len(outs),
        out_shape=[jax.ShapeDtypeStruct(*out) for out in outs],
        scratch_shapes=[pltpu.VMEM(*item) for item in scratch]
        + [pltpu.SemaphoreType.DMA((phases, 4)), pltpu.SemaphoreType.DMA((phases, 5))],
        compiler_params=pltpu.CompilerParams(
            collective_id=number, has_side_effects=True, vmem_limit_bytes=VMEM_LIMIT
        ),
        name=name,
    )(*operands)


def exchange_scratch(sums, block, width):
    return [
        ((sums, HALVES, 4, block, width), BF16),
        ((sums, HALVES, 5, block, width), BF16),
        ((block, width), F32),
    ]


def start_call(rows, cot, gain):
    _, block, width = rows.shape
    whole = ((4, HALVES, block, width), BF16)
    return line_call(start_kernel, (rows, cot, gain), [whole, whole], [], 4, 1, "start")


def ffn_forward_call(mixer, w_out, w_up, w_down, rows, gain, gain_next, layer, last):
    _, block, width = rows.shape
    wide = w_down.shape[1]
    own, whole = ((HALVES, block, width), F32), ((4, HALVES, block, width), BF16)
    outs = [own, whole, ((4, HALVES, block, 2 * wide), F32), ((4, HALVES, block, wide), BF16), own]
    if not last:
        outs.append(whole)
    return line_call(
        functools.partial(ffn_forward_kernel, last),
        (mixer, w_out, w_up, w_down, rows, gain, gain_next), outs,
        exchange_scratch(2, block, width), 8, 2 + layer, "ffn_forward",
    )


def ffn_backward_call(cot, hidden, pre, normed, middle, grad, gain, w_down, w_up, w_out, layer):
    _, block, width = middle.shape
    wide = w_down.shape[1]
    whole = ((4, HALVES, block, width), BF16)
    outs = [
        ((4, HALVES, block, w_out.shape[1]), F32), ((width, 3 * wide), BF16), whole,
        ((HALVES, block, width), F32), ((1, width), F32),
    ]
    scratch = [((4, HALVES, block, 2 * wide), BF16)] + exchange_scratch(1, block, width)
    return line_call(
        ffn_backward_kernel, (cot, hidden, pre, normed, middle, grad, gain, w_down, w_up, w_out), outs,
        scratch, 4, 4 + layer, "ffn_backward",
    )


def mixer_backward_call(d_proj, w_in, normed, mixer, mixer_cot, rows, grad, gain, layer, last):
    _, block, width = rows.shape
    outs = [((HALVES, block, width), F32), ((1, width), F32)]
    if not last:
        outs += [((width, mixer.shape[3] + w_in.shape[1]), BF16), ((4, HALVES, block, width), BF16)]
    return line_call(
        functools.partial(mixer_backward_kernel, last),
        (d_proj, w_in, normed, mixer, mixer_cot, rows, grad, gain), outs,
        exchange_scratch(1, block, width), 4, 6 + layer, "mixer_backward",
    )


LAYERS = 2
CHUNK = 128
REFINE = 1


def over_rows(left, right):
    return lax.dot_general(left, right, TN, preferred_element_type=F32)


def padded(matrix, width):
    return jnp.pad(matrix, ((0, 0), (0, width - matrix.shape[1])))


def body(
    tokens,
    segment_ids,
    query_weight,
    key_weight,
    value_weight,
    gate_weight,
    decay_weight,
    out_weight,
    swiglu_gate,
    swiglu_up,
    swiglu_down,
    conv_query_key,
    conv_value,
    head_params,
    norm_gains,
    out_gain,
    cotangent,
):
    seqs, length = segment_ids.shape
    heads = head_params.shape[2]
    qk_width, v_width, pair_width = query_weight.shape[2], value_weight.shape[2], decay_weight.shape[2]
    hidden_width = swiglu_gate.shape[2]
    hidden_pad = -(-hidden_width // 256) * 256
    local_rows, width = tokens.shape
    block = local_rows // HALVES
    total_rows = 4 * local_rows
    tables = segment_tables(segment_ids, CHUNK)

    def gathered(matrix):
        return lax.all_gather(matrix, "dp", axis=0, tiled=True)

    def reduced(matrix):
        return lax.psum_scatter(matrix, "dp", scatter_dimension=0, tiled=True)

    def layer_weights(l):
        low = lambda m: m[l].astype(BF16)
        first = gathered(jnp.concatenate(
            [low(query_weight), low(key_weight), low(value_weight), low(gate_weight), padded(low(decay_weight), 128)], axis=1
        ))
        second = gathered(jnp.concatenate(
            [low(out_weight), padded(low(swiglu_gate), hidden_pad), padded(low(swiglu_up), hidden_pad),
             padded(low(swiglu_down), hidden_pad)], axis=1
        ))
        return (
            first, second[:, :v_width], second[:, v_width : v_width + 2 * hidden_pad], second[:, v_width + 2 * hidden_pad :]
        )

    def split_rows(matrix):
        return matrix.reshape(HALVES, block, matrix.shape[1])

    def split_all(matrix):
        return matrix.reshape(4, HALVES, block, matrix.shape[1])

    def merged(array):
        return array.reshape(total_rows, array.shape[3])

    def gain_of(l, i):
        return norm_gains[l, i][None]

    weights = [layer_weights(l) for l in range(LAYERS)]
    rows = split_rows(tokens)
    cot_rows = split_rows(cotangent)
    normed, cot = start_call(rows, cot_rows, gain_of(0, 0))
    kept = []
    for l in range(LAYERS):
        w_in, w_out, w_up, w_down = weights[l]
        last = l == LAYERS - 1
        proj = jnp.dot(merged(normed), w_in, preferred_element_type=F32)
        small = (conv_query_key[l], conv_value[l], head_params[l], out_gain[l][None])
        mixer, *saved = delta_forward(proj, *small, tables, seqs, heads, CHUNK, REFINE)
        mixer = split_all(mixer)
        following = gain_of(min(l + 1, LAYERS - 1), 0)
        middle, normed_ffn, pre, hidden, out_rows, *following = ffn_forward_call(
            mixer, w_out, w_up, w_down, rows, gain_of(l, 1), following, l, last
        )
        kept.append((rows, normed, proj, small, mixer, saved, middle, normed_ffn, pre, hidden))
        rows = out_rows
        if not last:
            normed = following[0]
    output = rows.reshape(local_rows, width)
    grad = cot_rows
    ffn_grads, mixer_grads, tap_grads, norm_grads, gain_grads = ([None] * LAYERS for _ in range(5))
    for l in reversed(range(LAYERS)):
        w_in, w_out, w_up, w_down = weights[l]
        rows, normed, proj, small, mixer, saved, middle, normed_ffn, pre, hidden = kept[l]
        last = l == 0
        d_mixer, ffn_grad, mixer_cot, grad, second_gain = ffn_backward_call(
            cot, hidden, pre, normed_ffn, middle, grad, gain_of(l, 1), w_down, w_up, w_out, l
        )
        ffn_grads[l] = reduced(ffn_grad)
        d_proj, d_qk, d_v, d_head, d_gain = delta_backward(
            proj, *small, tables, saved, merged(d_mixer), seqs, heads, CHUNK
        )
        if last:
            mixer_grad = jnp.concatenate(
                [over_rows(merged(mixer_cot), merged(mixer)), over_rows(merged(normed), d_proj)], axis=1
            ).astype(BF16)
            mixer_grads[l] = reduced(mixer_grad)
        grad, first_gain, *others = mixer_backward_call(
            split_all(d_proj), w_in, normed, mixer, mixer_cot, rows, grad, gain_of(l, 0), l, last
        )
        if not last:
            mixer_grads[l] = reduced(others[0])
            cot = others[1]
        tap_grads[l] = (d_qk.sum(0), d_v.sum(0), d_head.sum(0)[:, :2, 0].T)
        norm_grads[l] = jnp.concatenate([first_gain, second_gain], axis=0)
        gain_grads[l] = d_gain.sum((0, 1, 2))

    def columns(parts, start, size):
        return jnp.stack([part[:, start : start + size] for part in parts]).astype(F32)

    start = v_width
    in_grads = []
    for size in (qk_width, qk_width, v_width, v_width, pair_width):
        in_grads.append(columns(mixer_grads, start, size))
        start += size
    out_grad = columns(mixer_grads, 0, v_width)
    down_grad = columns(ffn_grads, 0, hidden_width)
    gate_grad = columns(ffn_grads, hidden_pad, hidden_width)
    up_grad = columns(ffn_grads, 2 * hidden_pad, hidden_width)
    taps = tuple(jnp.stack([tap_grads[l][i] for l in range(LAYERS)]) for i in range(3))
    taps = lax.psum(taps, "dp")
    norms = lax.psum((jnp.stack(norm_grads), jnp.stack(gain_grads)), ("dp", "tensor"))
    return (
        output, grad.reshape(local_rows, width), *in_grads, out_grad, gate_grad, up_grad, down_grad, *taps, *norms
    )


def solution(mesh):
    rows = P(("dp", "tensor"), None)
    weight = P(None, "dp", "tensor")
    small = (P(None, None, None, "tensor"), P(None, None, "tensor"), P(None, None, "tensor"), P(), P())
    return jax.shard_map(
        body,
        mesh=mesh,
        in_specs=(rows, P("dp", None)) + (weight,) * 9 + small + (rows,),
        out_specs=(rows, rows) + (weight,) * 9 + small,
        check_vma=False,
    )
```

```python
import functools
import jax
import jax.numpy as jnp
from jax import lax
from jax.experimental import pallas as pl
from jax.experimental.pallas import tpu as pltpu
from jax.sharding import PartitionSpec as P

F32 = jnp.float32
BF16 = jnp.bfloat16
NN = (((1,), (0,)), ((), ()))
NT = (((1,), (1,)), ((), ()))
TN = (((0,), (0,)), ((), ()))
EPS = 1e-6
FLOOR = 0.01


def cost(micros):
    return pl.CostEstimate(flops=0, bytes_accessed=int(micros * 3.5e6), transcendentals=0)


def split(x):
    high = x.astype(BF16)
    return high, (x - high.astype(F32)).astype(BF16)


def mm(a, b, dims, passes=3):
    def one(p, q):
        return lax.dot_general(p, q, dims, preferred_element_type=F32)

    if passes == 1:
        return one(a.astype(BF16), b.astype(BF16))
    ah, al = split(a)
    bh, bl = split(b)
    return one(ah, bh) + (one(ah, bl) + one(al, bh))


def iota(shape, axis):
    return lax.broadcasted_iota(jnp.int32, shape, axis)


def shifted_rows(x, by):
    return pltpu.roll(x, by % x.shape[0], 0) if by else x


def conv(signal, taps, masks):
    total = signal * taps[0:1]
    for j in range(1, 4):
        total = total + shifted_rows(signal, j) * masks[j - 1] * taps[j : j + 1]
    return total


def chunk_scan(row, chunk, backward=False):
    length = row.shape[1]
    place = iota(row.shape, 1) % chunk
    step = 1
    while step < chunk:
        if backward:
            moved = pltpu.roll(row, length - step, 1)
            row = row + jnp.where(place < chunk - step, moved, 0.0)
        else:
            moved = pltpu.roll(row, step, 1)
            row = row + jnp.where(place >= step, moved, 0.0)
        step *= 2
    return row


def unit_lower_inverse(lower, refine):
    size = lower[0].shape[0]
    rows, cols = iota((size, size), 0), iota((size, size), 1)
    eye = (rows == cols).astype(F32)

    def off(block):
        return ((rows // (2 * block) == cols // (2 * block)) & (rows // block != cols // block)).astype(F32)

    found = [eye - part * off(1) for part in lower]
    block = 2
    while block < size:
        mask = off(block)
        half = [mm(x, part * mask, NN) for x, part in zip(found, lower)]
        found = [x - mm(t, x, NN) for x, t in zip(found, half)]
        block *= 2
    for _ in range(refine):
        rest = [(x - eye) + mm(part, x, NN) for x, part in zip(found, lower)]
        found = [x - mm(x, r, NN) for x, r in zip(found, rest)]
    return found


def prepared(head, chunk, qref, kref, vref, pair_ref, tap_qk, tap_v, head_table, col_info, row_info):
    length, dk = qref.shape
    masks = [col_info[:, j : j + 1] for j in range(3)]
    masks = [jnp.broadcast_to(m, (length, dk)) for m in masks]
    dv = vref.shape[1]
    wide = [jnp.concatenate([m] * (dv // dk), axis=1) for m in masks]
    pre_q = conv(qref[...], tap_qk[0], masks)
    pre_k = conv(kref[...], tap_qk[1], masks)
    pre_v = conv(vref[...], tap_v[...], wide)
    out = dict(masks=masks, wide=wide, pre_q=pre_q, pre_k=pre_k, pre_v=pre_v)
    for name, pre in (("q", pre_q), ("k", pre_k), ("v", pre_v)):
        sig = lax.logistic(pre)
        out["sig_" + name] = sig
        out["act_" + name] = pre * sig
    out["inv_q"] = lax.rsqrt(jnp.sum(out["act_q"] ** 2, axis=1, keepdims=True) + EPS)
    out["inv_k"] = lax.rsqrt(jnp.sum(out["act_k"] ** 2, axis=1, keepdims=True) + EPS)
    out["q"] = out["act_q"] * out["inv_q"] * dk ** (-0.5)
    out["k"] = out["act_k"] * out["inv_k"]
    out["v"] = out["act_v"]
    pair = jnp.transpose(pair_ref[...])
    picked = iota(pair.shape, 0)
    a_row = jnp.sum(jnp.where(picked == 2 * head, pair, 0.0), axis=0, keepdims=True)
    b_row = jnp.sum(jnp.where(picked == 2 * head + 1, pair, 0.0), axis=0, keepdims=True)
    rate = jnp.exp(jnp.full((1, length), head_table[0, head], F32))
    a_row = a_row + head_table[1, head]
    softplus = jnp.maximum(a_row, 0.0) + jnp.log1p(jnp.exp(-jnp.abs(a_row)))
    decay = -rate * softplus
    beta = lax.logistic(b_row)
    total = chunk_scan(decay, chunk)
    entry = jnp.exp(total) * row_info[0:1]
    chunks = length // chunk
    place = iota((1, length), 1)
    ends = [total[:, (i + 1) * chunk - 1 : (i + 1) * chunk] for i in range(chunks)]
    last = ends[0]
    for i in range(1, chunks):
        last = jnp.where(place >= i * chunk, ends[i], jnp.broadcast_to(last, (1, length)))
    tail = jnp.exp(last - total) * row_info[1:2]
    rows = jnp.concatenate([beta, total, entry, tail, jnp.zeros((124, length), F32)], axis=0)
    cols = jnp.transpose(rows)
    out.update(
        a_row=a_row, rate=rate, decay=decay, beta_row=beta, total_row=total, entry_row=entry, tail_row=tail,
        beta=cols[:, 0:1], total=cols[:, 1:2], entry=cols[:, 2:3], tail=cols[:, 3:4],
    )
    return out


def chunk_parts(pre, i, chunk, col_info, row_info):
    s = slice(i * chunk, (i + 1) * chunk)
    q, k, v = pre["q"][s], pre["k"][s], pre["v"][s]
    beta, total, entry, tail = pre["beta"][s], pre["total"][s], pre["entry"][s], pre["tail"][s]
    rows, cols = iota((chunk, chunk), 0), iota((chunk, chunk), 1)
    allowed = (col_info[s, 3:4] == row_info[2:3, s]) & (rows >= cols)
    fading = jnp.where(allowed, jnp.exp(jnp.where(allowed, total - pre["total_row"][:, s], 0.0)), 0.0)
    both = mm(jnp.concatenate([q, k], axis=0), k, NT)
    strict_fading = jnp.where(rows > cols, fading, 0.0)
    qk, kk = both[:chunk], both[chunk:]
    return dict(
        q=q, k=k, v=v, beta=beta, entry=entry, tail=tail, fading=fading, strict=strict_fading,
        mixed=qk * fading, kk_faded=kk * strict_fading, lower=beta * (kk * strict_fading),
        exit=pre["entry_row"][:, (i + 1) * chunk - 1 : (i + 1) * chunk], rows=s,
    )


def forward_kernel(
    chunk, refine, qref, kref, vref, gref, pair_ref, tap_qk, tap_v, head_table, gain, col_ref, row_ref,
    mix_ref, rec_ref, fix_ref, inv_ref, state_ref,
):
    head = pl.program_id(1)
    col_info, row_info = col_ref[0], row_ref[0]
    pre = prepared(head, chunk, qref, kref, vref, pair_ref, tap_qk, tap_v, head_table, col_info, row_info)
    length, dk = qref.shape
    dv = vref.shape[1]
    chunks = length // chunk
    parts = [chunk_parts(pre, i, chunk, col_info, row_info) for i in range(chunks)]
    inverses = unit_lower_inverse([p["lower"] for p in parts], refine)
    state = jnp.zeros((dk, dv), F32)
    steps = []
    for p, inverse in zip(parts, inverses):
        target = jnp.concatenate([p["beta"] * p["entry"] * p["k"], p["beta"] * p["v"]], axis=1)
        solved = mm(inverse, target, NN)
        pushed = mm(p["k"] * p["tail"], solved, TN)
        steps.append((solved, pushed))
    states = []
    for p, (solved, pushed) in zip(parts, steps):
        states.append(state)
        state = p["exit"] * state - mm(pushed[:, :dk], state, NN) + pushed[:, dk:]
    gain_row = gain[...]
    for i, (p, inverse, (solved, pushed)) in enumerate(zip(parts, inverses, steps)):
        seen = mm(jnp.concatenate([solved[:, :dk], p["q"] * p["entry"]], axis=0), states[i], NN)
        fixed = solved[:, dk:] - seen[:chunk]
        rec = seen[chunk:] + mm(p["mixed"], fixed, NN)
        s = p["rows"]
        rec_ref[s, :] = rec
        fix_ref[s, :] = fixed
        inv_ref[0, 0, i] = inverse
        state_ref[0, 0, i] = states[i]
        normal = rec * lax.rsqrt(jnp.mean(rec * rec, axis=1, keepdims=True) + FLOOR)
        gate = gref[s, :]
        mix_ref[s, :] = (normal * gain_row * (gate * lax.logistic(gate))).astype(BF16)


def silu_grad(pre, sig):
    return sig * (1.0 + pre * (1.0 - sig))


def backward_kernel(
    chunk, heads, qref, kref, vref, gref, pair_ref, tap_qk, tap_v, head_table, gain, col_ref, row_ref,
    rec_ref, fix_ref, inv_ref, state_ref, dmix_ref,
    dproj_ref, dtap_qk, dtap_v, dhead_ref, dgain_ref,
):
    seq, head = pl.program_id(0), pl.program_id(1)
    col_info, row_info = col_ref[0], row_ref[0]
    pre = prepared(head, chunk, qref, kref, vref, pair_ref, tap_qk, tap_v, head_table, col_info, row_info)
    length, dk = qref.shape
    dv = vref.shape[1]
    chunks = length // chunk
    parts = [chunk_parts(pre, i, chunk, col_info, row_info) for i in range(chunks)]
    gain_row = gain[...]
    dgain = jnp.zeros((1, dv), F32)
    v_at = 2 * heads * dk
    g_at = v_at + heads * dv
    p_at = g_at + heads * dv
    for p in parts:
        s = p["rows"]
        rec, gate, dmix = rec_ref[s, :], gref[s, :], dmix_ref[s, :]
        scale = lax.rsqrt(jnp.mean(rec * rec, axis=1, keepdims=True) + FLOOR)
        sig = lax.logistic(gate)
        gated = dmix * (gate * sig)
        normal = rec * scale
        dgain = dgain + jnp.sum(gated * normal, axis=0, keepdims=True)
        dgate = dmix * normal * gain_row * silu_grad(gate, sig)
        dproj_ref[s, pl.ds(pl.multiple_of(g_at + head * dv, dv), dv)] = dgate.astype(BF16)
        dn = gated * gain_row
        p["drec"] = scale * dn - rec * (scale * scale * scale) * jnp.mean(dn * rec, axis=1, keepdims=True)
    for i, p in enumerate(parts):
        inverse = inv_ref[0, 0, i]
        p["inverse"] = inverse
        solved = mm(inverse, p["beta"] * p["entry"] * p["k"], NN)
        back = mm(p["mixed"], p["drec"], TN)
        p["back"] = back
        ahead = mm(solved, p["k"] * p["tail"], TN)
        given = mm(
            jnp.concatenate([p["q"] * p["entry"], -solved], axis=0),
            jnp.concatenate([p["drec"], back], axis=0), TN,
        )
        p["ahead"], p["given"] = ahead, given
    dstate = jnp.zeros((dk, dv), F32)
    for p in reversed(parts):
        p["dstate"] = dstate
        dstate = p["exit"] * dstate - mm(p["ahead"], dstate, NN) + p["given"]
    cols = iota((chunk, 8), 1)
    col_parts, row_parts, dqs, dks, dvs = [], [], [], [], []
    for i, p in enumerate(parts):
        s = p["rows"]
        state, dstate, fixed, drec = state_ref[0, 0, i], p["dstate"], fix_ref[s, :], p["drec"]
        q, k, v, beta, entry, tail = p["q"], p["k"], p["v"], p["beta"], p["entry"], p["tail"]
        dfixed = p["back"] + mm(k * tail, dstate, NN)
        dtarget = mm(p["inverse"], dfixed, TN)
        outer = mm(
            jnp.concatenate([drec, dtarget], axis=0), jnp.concatenate([state, fixed], axis=0), NT
        )
        drec_state, dtarget_state = outer[:chunk, :dk], outer[chunk:, :dk]
        dmixed, dlower = outer[:chunk, dk:], -outer[chunk:, dk:]
        fixed_dstate = mm(fixed, dstate, NT)
        g1 = dmixed * p["fading"]
        g2 = (beta * dlower) * p["strict"]
        stacked = jnp.concatenate([g1, g2], axis=0)
        first = mm(stacked, k, NN)
        second = mm(stacked, jnp.concatenate([q, k], axis=0), TN)
        key_state = jnp.sum(dtarget_state * k, axis=1, keepdims=True)
        dqs.append(entry * drec_state + first[:chunk])
        dks.append(first[chunk:] + second + tail * fixed_dstate - (beta * entry) * dtarget_state)
        dvs.append(beta * dtarget)
        dentry = jnp.sum(drec_state * q, axis=1, keepdims=True) - beta * key_state
        dtail = jnp.sum(fixed_dstate * k, axis=1, keepdims=True) * tail
        high = dmixed * p["mixed"] + dlower * p["lower"]
        dbeta = (
            jnp.sum(dtarget * v, axis=1, keepdims=True)
            - entry * key_state
            + jnp.sum(dlower * p["kk_faded"], axis=1, keepdims=True)
        )
        dtotal = jnp.sum(high, axis=1, keepdims=True) + dentry * entry - dtail
        end = p["exit"] * jnp.sum(jnp.sum(dstate * state, axis=1, keepdims=True), axis=0, keepdims=True)
        end = end + jnp.sum(dtail, axis=0, keepdims=True)
        dtotal = dtotal + jnp.where(iota((chunk, 1), 0) == chunk - 1, end, 0.0)
        row_parts.append(jnp.sum(high, axis=0, keepdims=True))
        col_parts.append(jnp.where(cols == 0, dtotal, jnp.where(cols == 1, dbeta, 0.0)))
    lanes = jnp.concatenate(col_parts, axis=0)
    lanes = jnp.concatenate([lanes, jnp.zeros((length, 120), F32)], axis=1)
    turned = jnp.transpose(lanes)
    dtotal_row = turned[0:1] - jnp.concatenate(row_parts, axis=1)
    dbeta_row = turned[1:2]
    ddecay = chunk_scan(dtotal_row, chunk, backward=True)
    da = -ddecay * pre["rate"] * lax.logistic(pre["a_row"])
    db = dbeta_row * pre["beta_row"] * (1.0 - pre["beta_row"])
    spread = iota((128, length), 0)
    dpair = jnp.where(spread == 2 * head, da, jnp.where(spread == 2 * head + 1, db, 0.0))
    dpair = jnp.transpose(dpair).astype(BF16)

    @pl.when(head == 0)
    def _():
        dproj_ref[:, p_at:] = dpair

    @pl.when(head != 0)
    def _():
        dproj_ref[:, p_at:] = dproj_ref[:, p_at:] + dpair

    dscale = jnp.sum(ddecay * pre["decay"], axis=1, keepdims=True)
    dbias = jnp.sum(da, axis=1, keepdims=True)
    which = iota((8, 128), 0)
    dhead = jnp.where(which == 0, dscale, jnp.where(which == 1, dbias, 0.0))
    dq, dk_all, dv_all = (jnp.concatenate(x, axis=0) for x in (dqs, dks, dvs))

    def through_norm(grad, act, inv, factor):
        return factor * (inv * grad - act * (inv * inv * inv) * jnp.sum(grad * act, axis=1, keepdims=True))

    dq = through_norm(dq, pre["act_q"], pre["inv_q"], dk ** (-0.5))
    dk_all = through_norm(dk_all, pre["act_k"], pre["inv_k"], 1.0)
    taps_out = []
    for grad, name, src, taps, masks, at in (
        (dq, "q", qref, tap_qk[0], pre["masks"], head * dk),
        (dk_all, "k", kref, tap_qk[1], pre["masks"], heads * dk + head * dk),
        (dv_all, "v", vref, tap_v[...], pre["wide"], v_at + head * dv),
    ):
        dpre = grad * silu_grad(pre["pre_" + name], pre["sig_" + name])
        signal = src[...]
        dsignal = dpre * taps[0:1]
        dtaps = [jnp.sum(dpre * signal, axis=0, keepdims=True)]
        for j in range(1, 4):
            masked = dpre * masks[j - 1]
            dsignal = dsignal + shifted_rows(masked, -j) * taps[j : j + 1]
            dtaps.append(jnp.sum(masked * shifted_rows(signal, j), axis=0, keepdims=True))
        width = grad.shape[1]
        dproj_ref[:, pl.ds(pl.multiple_of(at, width), width)] = dsignal.astype(BF16)
        taps_out.append(jnp.concatenate(dtaps, axis=0))
    dtap_qk[0, 0] = taps_out[0]
    dtap_qk[0, 1] = taps_out[1]
    dtap_v[0] = taps_out[2]
    dhead_ref[0, 0] = dhead
    dgain_ref[0, 0] = dgain


def specs(length, heads, dk, dv):
    v_block = 2 * heads * dk // dv
    return [
        pl.BlockSpec((length, dk), lambda s, h: (s, h)),
        pl.BlockSpec((length, dk), lambda s, h: (s, heads + h)),
        pl.BlockSpec((length, dv), lambda s, h: (s, v_block + h)),
        pl.BlockSpec((length, dv), lambda s, h: (s, v_block + heads + h)),
        pl.BlockSpec((length, 128), lambda s, h: (s, (2 * heads * dk + 2 * heads * dv) // 128)),
        pl.BlockSpec((2, 4, dk), lambda s, h: (0, 0, h)),
        pl.BlockSpec((4, dv), lambda s, h: (0, h)),
        pl.BlockSpec(memory_space=pltpu.SMEM),
        pl.BlockSpec((1, dv), lambda s, h: (0, 0)),
        pl.BlockSpec((1, length, 8), lambda s, h: (s, 0, 0)),
        pl.BlockSpec((1, 8, length), lambda s, h: (s, 0, 0)),
    ]


def segment_tables(segment_ids, chunk):
    seqs, length = segment_ids.shape
    place = jnp.arange(length)
    conv_masks = []
    for j in range(1, 4):
        earlier = jnp.pad(segment_ids, ((0, 0), (j, 0)), constant_values=-1)[:, :length]
        conv_masks.append(earlier == segment_ids)
    blocks = segment_ids.reshape(seqs, length // chunk, chunk)
    finals = blocks[:, :, -1]
    before = jnp.concatenate([segment_ids[:, :1], finals[:, :-1]], axis=1)
    carried = (blocks == before[:, :, None]).reshape(seqs, length)
    tailed = (blocks == finals[:, :, None]).reshape(seqs, length)
    zero = jnp.zeros((seqs, length), F32)
    ids = segment_ids.astype(F32)
    rows = jnp.stack([carried.astype(F32), tailed.astype(F32), ids] + [zero] * 5, axis=1)
    cols = jnp.stack([m.astype(F32) for m in conv_masks] + [ids] + [zero] * 4, axis=2)
    return cols, rows


def delta_forward(proj, taps_qk, taps_v, head_table, gain, tables, seqs, heads, chunk, refine):
    cols, rows = tables
    length = cols.shape[1]
    dk, dv = taps_qk.shape[2] // heads, taps_v.shape[1] // heads
    chunks = length // chunk
    tokens = seqs * length
    column = pl.BlockSpec((length, dv), lambda s, h: (s, h))
    return pl.pallas_call(
        functools.partial(forward_kernel, chunk, refine),
        grid=(seqs, heads),
        in_specs=specs(length, heads, dk, dv),
        out_specs=[
            column, column, column,
            pl.BlockSpec((1, 1, chunks, chunk, chunk), lambda s, h: (s, h, 0, 0, 0)),
            pl.BlockSpec((1, 1, chunks, dk, dv), lambda s, h: (s, h, 0, 0, 0)),
        ],
        out_shape=[
            jax.ShapeDtypeStruct((tokens, heads * dv), BF16),
            jax.ShapeDtypeStruct((tokens, heads * dv), F32),
            jax.ShapeDtypeStruct((tokens, heads * dv), F32),
            jax.ShapeDtypeStruct((seqs, heads, chunks, chunk, chunk), F32),
            jax.ShapeDtypeStruct((seqs, heads, chunks, dk, dv), F32),
        ],
        compiler_params=pltpu.CompilerParams(vmem_limit_bytes=48 * 2**20),
        cost_estimate=cost(15),
        name="delta_forward",
    )(proj, proj, proj, proj, proj, taps_qk, taps_v, head_table, gain, cols, rows)


def delta_backward(proj, taps_qk, taps_v, head_table, gain, tables, saved, dmix, seqs, heads, chunk):
    cols, rows = tables
    length = cols.shape[1]
    dk, dv = taps_qk.shape[2] // heads, taps_v.shape[1] // heads
    chunks = length // chunk
    tokens = seqs * length
    width = proj.shape[1]
    column = pl.BlockSpec((length, dv), lambda s, h: (s, h))
    return pl.pallas_call(
        functools.partial(backward_kernel, chunk, heads),
        grid=(seqs, heads),
        in_specs=specs(length, heads, dk, dv)
        + [
            column, column,
            pl.BlockSpec((1, 1, chunks, chunk, chunk), lambda s, h: (s, h, 0, 0, 0)),
            pl.BlockSpec((1, 1, chunks, dk, dv), lambda s, h: (s, h, 0, 0, 0)),
            column,
        ],
        out_specs=[
            pl.BlockSpec((length, width), lambda s, h: (s, 0)),
            pl.BlockSpec((1, 2, 4, dk), lambda s, h: (s, 0, 0, h)),
            pl.BlockSpec((1, 4, dv), lambda s, h: (s, 0, h)),
            pl.BlockSpec((1, 1, 8, 128), lambda s, h: (s, h, 0, 0)),
            pl.BlockSpec((1, 1, 1, dv), lambda s, h: (s, h, 0, 0)),
        ],
        out_shape=[
            jax.ShapeDtypeStruct((tokens, width), BF16),
            jax.ShapeDtypeStruct((seqs, 2, 4, heads * dk), F32),
            jax.ShapeDtypeStruct((seqs, 4, heads * dv), F32),
            jax.ShapeDtypeStruct((seqs, heads, 8, 128), F32),
            jax.ShapeDtypeStruct((seqs, heads, 1, dv), F32),
        ],
        compiler_params=pltpu.CompilerParams(vmem_limit_bytes=56 * 2**20),
        cost_estimate=cost(25),
        name="delta_backward",
    )(proj, proj, proj, proj, proj, taps_qk, taps_v, head_table, gain, cols, rows, *saved, dmix)


MESH = pl.DeviceIdType.MESH
VMEM_LIMIT = 58 * 2**20
HALVES = 2


class Line:
    def __init__(self, send_sem, recv_sem):
        self.send_sem, self.recv_sem = send_sem, recv_sem
        self.me = lax.axis_index("tensor")

    def greet(self):
        barrier = pltpu.get_barrier_semaphore()
        for m in range(4):
            @pl.when(self.me == m)
            def _():
                for t in range(4):
                    if t != m and {t, m} != {0, 3}:
                        pl.semaphore_signal(barrier, inc=1, device_id={"tensor": t}, device_id_type=MESH)

    def meet(self, others=0):
        barrier = pltpu.get_barrier_semaphore()
        for m in range(4):
            @pl.when(self.me == m)
            def _():
                pl.semaphore_wait(barrier, others + (2 if m in (0, 3) else 3))

    def copy(self, phase, source, target, to, send_at, recv_at):
        return pltpu.make_async_remote_copy(
            src_ref=source, dst_ref=target, send_sem=self.send_sem.at[phase, send_at],
            recv_sem=self.recv_sem.at[phase, recv_at], device_id={"tensor": to}, device_id_type=MESH,
        )

    def gather_start(self, phase, blocks):
        for m in range(4):
            @pl.when(self.me == m)
            def _():
                for t in range(4):
                    if t != m and {t, m} != {0, 3}:
                        self.copy(phase, blocks[m], blocks[m], t, t, m).start()

    def gather_forward(self, phase, blocks):
        for m in (1, 2):
            @pl.when(self.me == m)
            def _():
                far, to = (3, 0) if m == 1 else (0, 3)
                self.copy(phase, blocks[far], blocks[far], to, m, far).wait_recv()
                self.copy(phase, blocks[far], blocks[far], to, m, far).start()

    def gather_wait(self, phase, blocks):
        for m in range(4):
            @pl.when(self.me == m)
            def _():
                for b in range(4):
                    if b != m and not (m in (1, 2) and b == (3 if m == 1 else 0)):
                        self.copy(phase, blocks[b], blocks[b], b, b, b).wait_recv()

    def gather_drain(self, phase, blocks):
        for m in range(4):
            @pl.when(self.me == m)
            def _():
                for t in range(4):
                    if t != m and {t, m} != {0, 3}:
                        self.copy(phase, blocks[m], blocks[m], t, t, m).wait_send()
                if m in (1, 2):
                    far, to = (3, 0) if m == 1 else (0, 3)
                    self.copy(phase, blocks[far], blocks[far], to, m, far).wait_send()

    def scatter_start(self, phase, parts, slots):
        for m in range(4):
            @pl.when(self.me == m)
            def _():
                if m in (0, 3):
                    through = 1 if m == 0 else 2
                    self.copy(phase, parts[3 - m], slots[4], through, 3 - m, 4).start()
                for t in range(4):
                    if t != m and {t, m} != {0, 3}:
                        if not (m in (1, 2) and t == (3 if m == 1 else 0)):
                            self.copy(phase, parts[t], slots[m], t, t, m).start()

    def scatter_relay(self, phase, parts, slots):
        for m in (1, 2):
            @pl.when(self.me == m)
            def _():
                t = 3 if m == 1 else 0
                self.copy(phase, parts[t], slots[4], t, t, 4).wait_recv()
                parts[t][...] = (parts[t][...].astype(F32) + slots[4][...].astype(F32)).astype(BF16)
                self.copy(phase, parts[t], slots[m], t, t, m).start()

    def scatter_wait(self, phase, parts, slots):
        for m in range(4):
            @pl.when(self.me == m)
            def _():
                for s in range(4):
                    if s != m and {s, m} != {0, 3}:
                        self.copy(phase, parts[s], slots[s], s, s, s).wait_recv()

    def scatter_sum(self, total, parts, slots):
        for m in range(4):
            @pl.when(self.me == m)
            def _():
                value = parts[m][...].astype(F32)
                for s in range(4):
                    if s != m and {s, m} != {0, 3}:
                        value = value + slots[s][...].astype(F32)
                total[...] = value

    def scatter_drain(self, phase, parts, slots):
        for m in range(4):
            @pl.when(self.me == m)
            def _():
                for t in range(4):
                    if t != m:
                        self.copy(phase, parts[t], slots[m], t, t, m).wait_send()


TURN_AT = 1


class Turns:
    def __init__(self, gate):
        self.gate = gate
        self.me = lax.axis_index("dp")
        self.second = lax.rem(self.me, 2)
        self.sibling = self.me + 1 - 2 * self.second

    def greet(self):
        pl.semaphore_signal(
            pltpu.get_barrier_semaphore(), inc=1, device_id={"dp": self.sibling}, device_id_type=MESH
        )

    def wait(self):
        @pl.when(self.second == 1)
        def _():
            pl.semaphore_wait(self.gate, 1)

    def give(self):
        @pl.when(self.second == 0)
        def _():
            pl.semaphore_signal(self.gate, inc=1, device_id={"dp": self.sibling}, device_id_type=MESH)


class Sums:
    def __init__(self, source, near, far, near_send, near_recv, far_send, far_recv):
        self.source, self.near, self.far = source, near, far
        self.near_send, self.near_recv, self.far_send, self.far_recv = near_send, near_recv, far_send, far_recv
        self.pairs = source.shape[0]
        self.group = self.pairs // 4
        me = lax.axis_index("dp")
        self.parity, self.mine = lax.rem(me, 2), lax.div(me, 2)

    def greet(self):
        barrier = pltpu.get_barrier_semaphore()
        sibling = 2 * self.mine + 1 - self.parity
        pl.semaphore_signal(barrier, inc=1, device_id={"dp": sibling}, device_id_type=MESH)

        def signal(i, carry):
            other = 2 * lax.rem(self.mine + i, self.pairs) + self.parity
            pl.semaphore_signal(barrier, inc=1, device_id={"dp": other}, device_id_type=MESH)
            return carry

        lax.fori_loop(1, self.pairs, signal, 0)
        return self.pairs

    def near_copy(self, m):
        span = pl.ds(m * self.group, self.group)
        return pltpu.make_async_remote_copy(
            src_ref=self.source.at[span, 1 - self.parity], dst_ref=self.near.at[span],
            send_sem=self.near_send.at[m], recv_sem=self.near_recv.at[m],
            device_id={"dp": 2 * self.mine + 1 - self.parity}, device_id_type=MESH,
        )

    def far_copy(self, j, slot, to):
        return pltpu.make_async_remote_copy(
            src_ref=self.near.at[j], dst_ref=self.far.at[slot], send_sem=self.far_send.at[j],
            recv_sem=self.far_recv.at[slot], device_id={"dp": 2 * to + self.parity}, device_id_type=MESH,
        )

    def start(self, m):
        self.near_copy(m).start()

    def turn(self, m):
        self.near_copy(m).wait_recv()
        rows = self.near.shape[1]
        step = 16

        def add(i, carry):
            j = m * self.group + lax.div(i, rows // step)
            span = pl.ds(pl.multiple_of(lax.rem(i, rows // step) * step, step), step)
            both = self.source[j, self.parity, span, :].astype(F32) + self.near[j, span, :].astype(F32)
            self.near[j, span, :] = both.astype(BF16)
            return carry

        lax.fori_loop(0, self.group * (rows // step), add, 0)

        def send(i, carry):
            j = m * self.group + i

            @pl.when(j != self.mine)
            def _():
                self.far_copy(j, self.mine, j).start()

            return carry

        lax.fori_loop(0, self.group, send, 0)

    def finish(self, out):
        def arrive(i, carry):
            slot = lax.rem(self.mine + i, self.pairs)
            self.far_copy(slot, slot, slot).wait_recv()
            return carry

        lax.fori_loop(1, self.pairs, arrive, 0)
        rows = out.shape[0]
        step = 16

        def add(i, carry):
            span = pl.ds(pl.multiple_of(i * step, step), step)
            total = self.near[self.mine, span, :].astype(F32)

            def more(j, value):
                return value + self.far[lax.rem(self.mine + j, self.pairs), span, :].astype(F32)

            if self.pairs <= 4:
                for j in range(1, self.pairs):
                    total = more(j, total)
            else:
                total = lax.fori_loop(1, self.pairs, more, total)
            out[span, :] = total
            return carry

        lax.fori_loop(0, rows // step, add, 0)

        def sent(i, carry):
            slot = lax.rem(self.mine + i, self.pairs)
            self.far_copy(slot, slot, slot).wait_send()
            return carry

        lax.fori_loop(1, self.pairs, sent, 0)
        for m in range(4):
            self.near_copy(m).wait_send()


class Smalls:
    def __init__(self, axis, land, send_sem, recv_sem):
        self.axis, self.land, self.send_sem, self.recv_sem = axis, land, send_sem, recv_sem
        self.me, self.count = lax.axis_index(axis), land.shape[0]

    def other(self, i):
        return lax.rem(self.me + i, self.count)

    def greet(self):
        barrier = pltpu.get_barrier_semaphore()

        def signal(i, carry):
            pl.semaphore_signal(barrier, inc=1, device_id={self.axis: self.other(i)}, device_id_type=MESH)
            return carry

        lax.fori_loop(1, self.count, signal, 0)
        return self.count - 1

    def copy(self, slot, to):
        return pltpu.make_async_remote_copy(
            src_ref=self.land.at[self.me], dst_ref=self.land.at[slot], send_sem=self.send_sem.at[to],
            recv_sem=self.recv_sem.at[slot], device_id={self.axis: to}, device_id_type=MESH,
        )

    def start(self):
        def send(i, carry):
            self.copy(self.me, self.other(i)).start()
            return carry

        lax.fori_loop(1, self.count, send, 0)

    def finish(self):
        def arrive(i, carry):
            self.copy(self.other(i), self.other(i)).wait_recv()
            return carry

        lax.fori_loop(1, self.count, arrive, 0)

        def add(i, value):
            return value + self.land[i]

        total = lax.fori_loop(1, self.count, add, self.land[0])

        def sent(i, carry):
            self.copy(self.me, self.other(i)).wait_send()
            return carry

        lax.fori_loop(1, self.count, sent, 0)
        return total


def half_of(ref, h):
    value = ref[:, h]
    return value.reshape(value.shape[0] * value.shape[1], value.shape[2])


def blocks_of(ref, h):
    return [ref.at[b, h] for b in range(4)]


def parts_of(part, slots, k, h):
    return [part.at[k, h, t] for t in range(4)], [slots.at[k, h, s] for s in range(5)]


def for_tiles(size, tile, step):
    def run(i, carry):
        step(pl.multiple_of(i * tile, tile))
        return carry

    lax.fori_loop(0, size // tile, run, 0)


def partial_sums(left, weight, part, k, h):
    def step(n):
        value = lax.dot_general(left, weight[pl.ds(n, 256), :], NT, preferred_element_type=F32)
        part[k, h, :, :, pl.ds(n, 256)] = value.astype(BF16).reshape(4, left.shape[0] // 4, 256)

    for_tiles(weight.shape[0], 256, step)


def row_grads(left, right, out, column):
    rows = left.shape[0] * left.shape[1] * left.shape[2]
    width = right.shape[3]
    pairs, _, own, _ = out.shape
    group = pairs // 4
    tall = group * 2 * own

    def piece(m):
        start = pl.multiple_of(m * tall, tall)
        turned = jnp.transpose(left[:, :, :, pl.ds(start, tall)].reshape(rows, tall))
        for n in range(0, width, 512):
            size = min(512, width - n)
            tile = right[:, :, :, n : n + size].reshape(rows, size)
            value = lax.dot_general(turned, tile, NN, preferred_element_type=F32)
            span = pl.ds(m * group, group)
            out[span, :, :, column + n : column + n + size] = value.astype(BF16).reshape(group, 2, own, size)

    return piece


def run_pieces(pieces, first, last):
    def run(m, carry):
        for piece in pieces:
            piece(m)
        return carry

    lax.fori_loop(first, last, run, 0)


def rms(value, gain):
    return value * lax.rsqrt(jnp.mean(value * value, axis=1, keepdims=True) + EPS) * gain


def rms_back(value, gain, grad):
    scale = lax.rsqrt(jnp.mean(value * value, axis=1, keepdims=True) + EPS)
    scaled = gain * grad
    back = scale * scaled - value * (scale * scale * scale) * jnp.mean(value * scaled, axis=1, keepdims=True)
    return back, jnp.sum(value * scale * grad, axis=0, keepdims=True)


def start_kernel(rows, cot, gain, normed, cot_all, send_sem, recv_sem):
    line = Line(send_sem, recv_sem)
    line.greet()
    for h in range(HALVES):
        normed[line.me, h] = rms(rows[h].astype(F32), gain[...]).astype(BF16)
        cot_all[line.me, h] = cot[h]
    line.meet()
    both = [(k + h, blocks_of(ref, h)) for k, ref in ((0, normed), (2, cot_all)) for h in range(HALVES)]
    for item in both:
        line.gather_start(*item)
    for item in both:
        line.gather_forward(*item)
    for item in both:
        line.gather_wait(*item)
    for item in both:
        line.gather_drain(*item)


def slices_of(weights, v_width, wide):
    return (
        weights.at[:, :v_width],
        weights.at[:, v_width : v_width + 2 * wide],
        weights.at[:, v_width + 2 * wide :],
    )


def ffn_forward_kernel(last, mixer, weights, rows, gain, gain_next, middle, normed, pre, hidden, out_rows, *rest):
    if last:
        part, slots, total, send_sem, recv_sem = rest
    else:
        normed_next, part, slots, total, send_sem, recv_sem, gate = rest
    line = Line(send_sem, recv_sem)
    wide = hidden.shape[3]
    w_out, w_up, w_down = slices_of(weights, mixer.shape[3], wide)
    block = rows.shape[1]
    line.greet()
    if last:
        partial_sums(half_of(mixer, 0), w_out, part, 0, 0)
        line.meet()
    else:
        turns = Turns(gate)
        turns.greet()
        partial_sums(half_of(mixer, 0), w_out, part, 0, 0)
        line.meet(1)
        turns.wait()
    line.scatter_start(0, *parts_of(part, slots, 0, 0))
    partial_sums(half_of(mixer, 1), w_out, part, 0, 1)
    line.scatter_relay(0, *parts_of(part, slots, 0, 0))
    line.scatter_start(1, *parts_of(part, slots, 0, 1))
    line.scatter_relay(1, *parts_of(part, slots, 0, 1))
    for h in range(HALVES):
        both = parts_of(part, slots, 0, h)
        line.scatter_wait(h, *both)
        line.scatter_sum(total, *both)
        value = rows[h].astype(F32) + total[...]
        middle[h] = value
        normed[line.me, h] = rms(value, gain[...]).astype(BF16)
        line.gather_start(2 + h, blocks_of(normed, h))
    line.gather_forward(2, blocks_of(normed, 0))
    for h in range(HALVES):
        if h == 1:
            line.gather_forward(3, blocks_of(normed, 1))
        line.gather_wait(2 + h, blocks_of(normed, h))
        if h == TURN_AT and not last:
            turns.give()
        left = half_of(normed, h)

        def step(n):
            gate = jnp.dot(left, w_up[:, pl.ds(n, 256)], preferred_element_type=F32)
            up = jnp.dot(left, w_up[:, pl.ds(n + wide, 256)], preferred_element_type=F32)
            pre[:, h, :, pl.ds(n, 256)] = gate.reshape(4, block, 256)
            pre[:, h, :, pl.ds(n + wide, 256)] = up.reshape(4, block, 256)
            value = gate * lax.logistic(gate) * up
            hidden[:, h, :, pl.ds(n, 256)] = value.astype(BF16).reshape(4, block, 256)

        for_tiles(wide, 256, step)
        partial_sums(half_of(hidden, h), w_down, part, 1, h)
        if h == 1:
            line.scatter_relay(4, *parts_of(part, slots, 1, 0))
        line.scatter_start(4 + h, *parts_of(part, slots, 1, h))
    line.scatter_relay(5, *parts_of(part, slots, 1, 1))
    for h in range(HALVES):
        both = parts_of(part, slots, 1, h)
        line.scatter_wait(4 + h, *both)
        line.scatter_sum(total, *both)
        value = middle[h] + total[...]
        out_rows[h] = value
        if not last:
            normed_next[line.me, h] = rms(value, gain_next[...]).astype(BF16)
            line.gather_start(6 + h, blocks_of(normed_next, h))
    if not last:
        for h in range(HALVES):
            line.gather_forward(6 + h, blocks_of(normed_next, h))
        for h in range(HALVES):
            line.gather_wait(6 + h, blocks_of(normed_next, h))
    for h in range(HALVES):
        line.scatter_drain(h, *parts_of(part, slots, 0, h))
        line.gather_drain(2 + h, blocks_of(normed, h))
        line.scatter_drain(4 + h, *parts_of(part, slots, 1, h))
        if not last:
            line.gather_drain(6 + h, blocks_of(normed_next, h))


def ffn_backward_kernel(
    cot, hidden, pre, normed, middle, grad, gain, weights,
    d_mixer, grads, mixer_cot, grad_out, d_gain, d_pre, part, slots, total, send_sem, recv_sem,
):
    line = Line(send_sem, recv_sem)
    wide = hidden.shape[3]
    w_out, w_up, w_down = slices_of(weights, d_mixer.shape[3], wide)
    block = middle.shape[1]
    line.greet()
    line.meet()
    for h in range(HALVES):
        left = half_of(cot, h)

        def step(n):
            d_hidden = jnp.dot(left, w_down[:, pl.ds(n, 256)], preferred_element_type=F32)
            gate = pre[:, h, :, pl.ds(n, 256)].reshape(4 * block, 256)
            up = pre[:, h, :, pl.ds(n + wide, 256)].reshape(4 * block, 256)
            sig = lax.logistic(gate)
            d_gate = d_hidden * up * sig * (1.0 + gate * (1.0 - sig))
            d_up = d_hidden * gate * sig
            d_pre[:, h, :, pl.ds(n, 256)] = d_gate.astype(BF16).reshape(4, block, 256)
            d_pre[:, h, :, pl.ds(n + wide, 256)] = d_up.astype(BF16).reshape(4, block, 256)

        for_tiles(wide, 256, step)
        partial_sums(half_of(d_pre, h), w_up, part, 0, h)
        if h == 1:
            line.scatter_relay(0, *parts_of(part, slots, 0, 0))
        line.scatter_start(h, *parts_of(part, slots, 0, h))
    line.scatter_relay(1, *parts_of(part, slots, 0, 1))
    pieces = [row_grads(cot, hidden, grads, 0), row_grads(normed, d_pre, grads, wide)]
    run_pieces(pieces, 0, 2)
    d_gain[...] = jnp.zeros_like(d_gain)
    for h in range(HALVES):
        both = parts_of(part, slots, 0, h)
        line.scatter_wait(h, *both)
        line.scatter_sum(total, *both)
        back, gain_part = rms_back(middle[h], gain[...], total[...])
        d_gain[...] += gain_part
        value = grad[h].astype(F32) + back
        grad_out[h] = value
        mixer_cot[line.me, h] = value.astype(BF16)
        line.gather_start(2 + h, blocks_of(mixer_cot, h))
    run_pieces(pieces, 2, 3)
    line.gather_forward(2, blocks_of(mixer_cot, 0))
    line.gather_forward(3, blocks_of(mixer_cot, 1))
    run_pieces(pieces, 3, 4)
    for h in range(HALVES):
        line.gather_wait(2 + h, blocks_of(mixer_cot, h))
        left = half_of(mixer_cot, h)
        for n in range(0, w_out.shape[1], 256):
            value = jnp.dot(left, w_out[:, n : n + 256], preferred_element_type=F32)
            d_mixer[:, h, :, n : n + 256] = value.reshape(4, block, 256)
    for h in range(HALVES):
        line.scatter_drain(h, *parts_of(part, slots, 0, h))
        line.gather_drain(2 + h, blocks_of(mixer_cot, h))


def mixer_backward_kernel(
    d_proj, w_in, normed, mixer, mixer_cot, rows, grad, gain,
    grad_out, d_gain, grads, cot, part, slots, total, send_sem, recv_sem,
):
    line = Line(send_sem, recv_sem)
    line.greet()
    line.meet()
    partial_sums(half_of(d_proj, 0), w_in, part, 0, 0)
    line.scatter_start(0, *parts_of(part, slots, 0, 0))
    partial_sums(half_of(d_proj, 1), w_in, part, 0, 1)
    line.scatter_relay(0, *parts_of(part, slots, 0, 0))
    line.scatter_start(1, *parts_of(part, slots, 0, 1))
    line.scatter_relay(1, *parts_of(part, slots, 0, 1))
    width = mixer.shape[3]
    pieces = [row_grads(mixer_cot, mixer, grads, 0), row_grads(normed, d_proj, grads, width)]
    run_pieces(pieces, 0, 2)
    d_gain[...] = jnp.zeros_like(d_gain)
    for h in range(HALVES):
        both = parts_of(part, slots, 0, h)
        line.scatter_wait(h, *both)
        line.scatter_sum(total, *both)
        back, gain_part = rms_back(rows[h].astype(F32), gain[...], total[...])
        d_gain[...] += gain_part
        value = grad[h] + back
        grad_out[h] = value
        cot[line.me, h] = value.astype(BF16)
        line.gather_start(2 + h, blocks_of(cot, h))
    run_pieces(pieces, 2, 3)
    line.gather_forward(2, blocks_of(cot, 0))
    line.gather_forward(3, blocks_of(cot, 1))
    run_pieces(pieces, 3, 4)
    for h in range(HALVES):
        line.gather_wait(2 + h, blocks_of(cot, h))
    for h in range(HALVES):
        line.scatter_drain(h, *parts_of(part, slots, 0, h))
        line.gather_drain(2 + h, blocks_of(cot, h))


def last_kernel(gain_at, norm_rows, d_proj, w_in, normed, mixer, mixer_cot, rows, grad, gain, taps, norms,
                grad_out, summed, taps_out, norms_out,
                d_gain, grads, taps_land, line_land, norms_land,
                taps_send, taps_recv, line_send, line_recv, norms_send, norms_recv,
                part, slots, total, send_sem, recv_sem, *sum_refs):
    line = Line(send_sem, recv_sem)
    sums = Sums(grads, *sum_refs)
    small_taps = Smalls("dp", taps_land, taps_send, taps_recv)
    small_line = Smalls("tensor", line_land, line_send, line_recv)
    small_norms = Smalls("dp", norms_land, norms_send, norms_recv)
    line.greet()
    others = sums.greet() + small_taps.greet() + small_line.greet()
    taps_land[small_taps.me] = taps[...]
    partial_sums(half_of(d_proj, 0), w_in, part, 0, 0)
    line.meet(others)
    line.scatter_start(0, *parts_of(part, slots, 0, 0))
    small_taps.start()
    width = mixer.shape[3]
    pieces = [row_grads(mixer_cot, mixer, grads, 0), row_grads(normed, d_proj, grads, width)]
    run_pieces(pieces, 0, 1)
    sums.start(0)
    line.scatter_relay(0, *parts_of(part, slots, 0, 0))
    partial_sums(half_of(d_proj, 1), w_in, part, 0, 1)
    line.scatter_start(1, *parts_of(part, slots, 0, 1))
    for m in range(1, 4):
        run_pieces(pieces, m, m + 1)
        sums.start(m)
        sums.turn(m - 1)
    line.scatter_relay(1, *parts_of(part, slots, 0, 1))
    sums.turn(3)
    d_gain[...] = jnp.zeros_like(d_gain)
    for h in range(HALVES):
        both = parts_of(part, slots, 0, h)
        line.scatter_wait(h, *both)
        line.scatter_sum(total, *both)
        back, gain_part = rms_back(rows[h].astype(F32), gain[...], total[...])
        d_gain[...] += gain_part
        grad_out[h] = grad[h] + back
    line_land[line.me] = norms[...]
    for i in range(norm_rows):
        line_land[line.me, gain_at + i : gain_at + i + 1, :] = d_gain[:, 128 * i : 128 * (i + 1)]
    small_line.start()
    norms_land[small_norms.me] = small_line.finish()
    small_norms.start()
    taps_out[...] = small_taps.finish()
    for h in range(HALVES):
        line.scatter_drain(h, *parts_of(part, slots, 0, h))
    sums.finish(summed)
    norms_out[...] = small_norms.finish()


DMA = pltpu.SemaphoreType.DMA


def line_call(kernel, operands, outs, scratch, number, name, micros):
    return pl.pallas_call(
        kernel,
        in_specs=[pl.BlockSpec(memory_space=pltpu.VMEM)] * len(operands),
        out_specs=[pl.BlockSpec(memory_space=pltpu.VMEM)] * len(outs),
        out_shape=[jax.ShapeDtypeStruct(*out) for out in outs],
        scratch_shapes=scratch,
        compiler_params=pltpu.CompilerParams(
            collective_id=number, has_side_effects=True, vmem_limit_bytes=VMEM_LIMIT
        ),
        cost_estimate=cost(micros),
        name=name,
    )(*operands)


def line_scratch(sums, block, width, phases):
    return [
        pltpu.VMEM((sums, HALVES, 4, block, width), BF16),
        pltpu.VMEM((sums, HALVES, 5, block, width), BF16),
        pltpu.VMEM((block, width), F32),
        DMA((phases, 4)),
        DMA((phases, 5)),
    ]


def sums_scratch(shape):
    pairs, _, own, width = shape
    return [
        pltpu.VMEM((pairs, own, width), BF16), pltpu.VMEM((pairs, own, width), BF16),
        DMA((4,)), DMA((4,)), DMA((pairs,)), DMA((pairs,)),
    ]


def start_call(rows, cot, gain):
    _, block, width = rows.shape
    whole = ((4, HALVES, block, width), BF16)
    return line_call(start_kernel, (rows, cot, gain), [whole, whole], [DMA((4, 4)), DMA((4, 5))], 1, "start", 35)


def ffn_forward_call(mixer, weights, rows, gain, gain_next, layer, last):
    _, block, width = rows.shape
    wide = (weights.shape[1] - mixer.shape[3]) // 3
    own, whole = ((HALVES, block, width), F32), ((4, HALVES, block, width), BF16)
    outs = [own, whole, ((4, HALVES, block, 2 * wide), F32), ((4, HALVES, block, wide), BF16), own]
    if not last:
        outs.append(whole)
    return line_call(
        functools.partial(ffn_forward_kernel, last), (mixer, weights, rows, gain, gain_next), outs,
        line_scratch(2, block, width, 8) + ([] if last else [pltpu.SemaphoreType.REGULAR]), 2 + layer, "ffn_forward", 65,
    )


def ffn_backward_call(cot, hidden, pre, normed, middle, grad, gain, weights, v_width, grads_shape, layer):
    _, block, width = middle.shape
    wide = hidden.shape[3]
    whole = ((4, HALVES, block, width), BF16)
    outs = [
        ((4, HALVES, block, v_width), F32), (grads_shape + (3 * wide,), BF16), whole,
        ((HALVES, block, width), F32), ((1, width), F32),
    ]
    scratch = [pltpu.VMEM((4, HALVES, block, 2 * wide), BF16)] + line_scratch(1, block, width, 4)
    return line_call(
        ffn_backward_kernel, (cot, hidden, pre, normed, middle, grad, gain, weights), outs, scratch,
        4 + layer, "ffn_backward", 40,
    )


def mixer_backward_call(d_proj, w_in, normed, mixer, mixer_cot, rows, grad, gain, grads_shape, layer):
    _, block, width = rows.shape
    outs = [
        ((HALVES, block, width), F32), ((1, width), F32),
        (grads_shape + (mixer.shape[3] + w_in.shape[1],), BF16), ((4, HALVES, block, width), BF16),
    ]
    return line_call(
        mixer_backward_kernel, (d_proj, w_in, normed, mixer, mixer_cot, rows, grad, gain), outs,
        line_scratch(1, block, width, 4), 6 + layer, "mixer_backward", 40,
    )


def last_call(d_proj, w_in, normed, mixer, mixer_cot, rows, grad, gain, taps, norms, grads_shape, gain_at):
    _, block, width = rows.shape
    dp = 2 * grads_shape[0]
    shape = grads_shape + (mixer.shape[3] + w_in.shape[1],)
    outs = [((HALVES, block, width), F32), (shape[2:], F32), (taps.shape, F32), (norms.shape, F32)]
    scratch = [
        pltpu.VMEM((1, width), F32), pltpu.VMEM(shape, BF16), pltpu.VMEM((dp,) + taps.shape, F32),
        pltpu.VMEM((4,) + norms.shape, F32), pltpu.VMEM((dp,) + norms.shape, F32),
        DMA((dp,)), DMA((dp,)), DMA((4,)), DMA((4,)), DMA((dp,)), DMA((dp,)),
    ]
    return line_call(
        functools.partial(last_kernel, gain_at, width // 128),
        (d_proj, w_in, normed, mixer, mixer_cot, rows, grad, gain, taps, norms), outs,
        scratch + line_scratch(1, block, width, 2) + sums_scratch(shape), 8, "last", 40,
    )


def finish_kernel(places, *refs):
    sources, outs = refs[: 2 * LAYERS], refs[2 * LAYERS : 2 * LAYERS + len(places)]
    held, sems = refs[2 * LAYERS + len(places) : -1], refs[-1]
    for i, (kind, width, start) in enumerate(places):
        for l in range(LAYERS):
            source = sources[kind * LAYERS + l]
            held[i][l] = source[:, start : start + width].astype(F32)
        pltpu.make_async_copy(held[i], outs[i], sems.at[i]).start()
    for i in range(len(places)):
        pltpu.make_async_copy(held[i], outs[i], sems.at[i]).wait()


def finish_call(mixer_grads, ffn_grads, places):
    operands = list(mixer_grads) + list(ffn_grads)
    own = operands[0].shape[0]
    shapes = [(LAYERS, own, width) for _, width, _ in places]
    return pl.pallas_call(
        functools.partial(finish_kernel, places),
        in_specs=[pl.BlockSpec(memory_space=pltpu.VMEM)] * len(operands),
        out_specs=[pl.BlockSpec(memory_space=pl.ANY)] * len(places),
        out_shape=[jax.ShapeDtypeStruct(shape, F32) for shape in shapes],
        scratch_shapes=[pltpu.VMEM(shape, F32) for shape in shapes] + [DMA((len(places),))],
        compiler_params=pltpu.CompilerParams(vmem_limit_bytes=VMEM_LIMIT),
        name="finish",
    )(*operands)


LAYERS = 2
CHUNK = 128
REFINE = 1


def packed(arrays):
    flat = []
    for array in arrays:
        flat.append(jnp.pad(array.reshape(-1), (0, -array.size % 128)))
    flat = jnp.concatenate(flat)
    return jnp.pad(flat, (0, -flat.size % 1024)).reshape(-1, 128)


def unpacked(rows, like):
    found, start = [], 0
    for array in like:
        count = -(-array.size // 128)
        found.append(rows[start : start + count].reshape(-1)[: array.size].reshape(array.shape))
        start += count
    return tuple(found)


def padded(matrix, width):
    return jnp.pad(matrix, ((0, 0), (0, width - matrix.shape[1])))


def body(
    tokens,
    segment_ids,
    query_weight,
    key_weight,
    value_weight,
    gate_weight,
    decay_weight,
    out_weight,
    swiglu_gate,
    swiglu_up,
    swiglu_down,
    conv_query_key,
    conv_value,
    head_params,
    norm_gains,
    out_gain,
    cotangent,
):
    seqs, length = segment_ids.shape
    heads = head_params.shape[2]
    qk_width, v_width, pair_width = query_weight.shape[2], value_weight.shape[2], decay_weight.shape[2]
    hidden_width = swiglu_gate.shape[2]
    hidden_pad = -(-hidden_width // 256) * 256
    local_rows, width = tokens.shape
    block = local_rows // HALVES
    total_rows = 4 * local_rows
    tables = segment_tables(segment_ids, CHUNK)

    def gathered(matrix):
        return lax.all_gather(matrix, "dp", axis=0, tiled=True)

    def reduced(matrix):
        return lax.psum_scatter(matrix, "dp", scatter_dimension=0, tiled=True)

    def layer_weights(l):
        low = lambda m: m[l].astype(BF16)
        first = gathered(jnp.concatenate(
            [low(query_weight), low(key_weight), low(value_weight), low(gate_weight), padded(low(decay_weight), 128)], axis=1
        ))
        second = gathered(jnp.concatenate(
            [low(out_weight), padded(low(swiglu_gate), hidden_pad), padded(low(swiglu_up), hidden_pad),
             padded(low(swiglu_down), hidden_pad)], axis=1
        ))
        return first, second

    def split_rows(matrix):
        return matrix.reshape(HALVES, block, matrix.shape[1])

    def split_all(matrix):
        return matrix.reshape(4, HALVES, block, matrix.shape[1])

    def merged(array):
        return array.reshape(total_rows, array.shape[3])

    def gain_of(l, i):
        return norm_gains[l, i][None]

    weights = [layer_weights(l) for l in range(LAYERS)]
    rows = split_rows(tokens)
    cot_rows = split_rows(cotangent)
    normed, cot = start_call(rows, cot_rows, gain_of(0, 0))
    kept = []
    for l in range(LAYERS):
        w_in, w_rest = weights[l]
        last = l == LAYERS - 1
        proj = jnp.dot(merged(normed), w_in, preferred_element_type=F32)
        small = (conv_query_key[l], conv_value[l], head_params[l], out_gain[l][None])
        mixer, *saved = delta_forward(proj, *small, tables, seqs, heads, CHUNK, REFINE)
        mixer = split_all(mixer)
        gain_next = gain_of(min(l + 1, LAYERS - 1), 0)
        middle, normed_ffn, pre, hidden, out_rows, *following = ffn_forward_call(
            mixer, w_rest, rows, gain_of(l, 1), gain_next, l, last
        )
        kept.append((rows, normed, proj, small, mixer, saved, middle, normed_ffn, pre, hidden))
        rows = out_rows
        if not last:
            normed = following[0]
    output = rows.reshape(local_rows, width)
    grad = cot_rows
    dp = lax.axis_size("dp")
    grads_shape = (dp // 2, 2, width // dp)
    ffn_grads, mixer_grads, tap_grads, norm_grads, gain_grads = ([None] * LAYERS for _ in range(5))
    for l in reversed(range(LAYERS)):
        w_in, w_rest = weights[l]
        rows, normed, proj, small, mixer, saved, middle, normed_ffn, pre, hidden = kept[l]
        if l < LAYERS - 1:
            cot, ffn_grads[l + 1] = lax.optimization_barrier((cot, ffn_grads[l + 1]))
        d_mixer, ffn_grad, mixer_cot, grad, second_gain = ffn_backward_call(
            cot, hidden, pre, normed_ffn, middle, grad, gain_of(l, 1), w_rest, v_width, grads_shape, l
        )
        ffn_grads[l] = reduced(ffn_grad.reshape(width, 3 * hidden_pad))
        d_proj, d_qk, d_v, d_head, d_gain = delta_backward(
            proj, *small, tables, saved, merged(d_mixer), seqs, heads, CHUNK
        )
        tap_grads[l] = (d_qk.sum(0), d_v.sum(0), d_head.sum(0)[:, :2, 0].T)
        gain_grads[l] = d_gain.sum((0, 1, 2))
        d_proj = split_all(d_proj)
        if l > 0:
            grad, first_gain, mixer_grad, cot = mixer_backward_call(
                d_proj, w_in, normed, mixer, mixer_cot, rows, grad, gain_of(l, 0), grads_shape, l
            )
            mixer_grads[l] = reduced(mixer_grad.reshape(width, mixer_grad.shape[3]))
            norm_grads[l] = jnp.concatenate([first_gain, second_gain], axis=0)
    norm_grads[0] = jnp.concatenate([jnp.zeros_like(second_gain), second_gain], axis=0)
    taps = tuple(jnp.stack([tap_grads[l][i] for l in range(LAYERS)]) for i in range(3))
    norms = (jnp.stack(norm_grads), jnp.stack(gain_grads))
    d_proj, mixer_grads[1] = lax.optimization_barrier((d_proj, mixer_grads[1]))
    grad, mixer_grads[0], *small_sums = last_call(
        d_proj, w_in, normed, mixer, mixer_cot, rows, grad, gain_of(0, 0), packed(taps), packed(norms), grads_shape, 0
    )
    taps, norms = unpacked(small_sums[0], taps), unpacked(small_sums[1], norms)

    weight_grads = finish_call(
        mixer_grads, ffn_grads,
        [(0, qk_width, v_width), (0, qk_width, v_width + qk_width), (0, v_width, v_width + 2 * qk_width),
         (0, v_width, 2 * v_width + 2 * qk_width), (0, pair_width, 3 * v_width + 2 * qk_width), (0, v_width, 0),
         (1, hidden_width, hidden_pad), (1, hidden_width, 2 * hidden_pad), (1, hidden_width, 0)],
    )
    return (
        output, grad.reshape(local_rows, width), *weight_grads, *taps, *norms
    )


def solution(mesh):
    rows = P(("dp", "tensor"), None)
    weight = P(None, "dp", "tensor")
    small = (P(None, None, None, "tensor"), P(None, None, "tensor"), P(None, None, "tensor"), P(), P())
    return jax.shard_map(
        body,
        mesh=mesh,
        in_specs=(rows, P("dp", None)) + (weight,) * 9 + small + (rows,),
        out_specs=(rows, rows) + (weight,) * 9 + small,
        check_vma=False,
    )
```

```python
import functools
import jax
import jax.numpy as jnp
from jax import lax
from jax.experimental import pallas as pl
from jax.experimental.pallas import tpu as pltpu
from jax.sharding import PartitionSpec as P

F32 = jnp.float32
BF16 = jnp.bfloat16
NN = (((1,), (0,)), ((), ()))
NT = (((1,), (1,)), ((), ()))
TN = (((0,), (0,)), ((), ()))
EPS = 1e-6
FLOOR = 0.01


def cost(micros):
    return pl.CostEstimate(flops=0, bytes_accessed=int(micros * 3.5e6), transcendentals=0)


def split(x):
    high = x.astype(BF16)
    return high, (x - high.astype(F32)).astype(BF16)


def mm(a, b, dims, passes=3):
    def one(p, q):
        return lax.dot_general(p, q, dims, preferred_element_type=F32)

    if passes == 1:
        return one(a.astype(BF16), b.astype(BF16))
    ah, al = split(a)
    bh, bl = split(b)
    return one(ah, bh) + (one(ah, bl) + one(al, bh))


def iota(shape, axis):
    return lax.broadcasted_iota(jnp.int32, shape, axis)


def shifted_rows(x, by):
    return pltpu.roll(x, by % x.shape[0], 0) if by else x


def conv(signal, taps, masks):
    total = signal * taps[0:1]
    for j in range(1, 4):
        total = total + shifted_rows(signal, j) * masks[j - 1] * taps[j : j + 1]
    return total


def chunk_scan(row, chunk, backward=False):
    length = row.shape[1]
    place = iota(row.shape, 1) % chunk
    step = 1
    while step < chunk:
        if backward:
            moved = pltpu.roll(row, length - step, 1)
            row = row + jnp.where(place < chunk - step, moved, 0.0)
        else:
            moved = pltpu.roll(row, step, 1)
            row = row + jnp.where(place >= step, moved, 0.0)
        step *= 2
    return row


def unit_lower_inverse(lower, refine):
    size = lower[0].shape[0]
    rows, cols = iota((size, size), 0), iota((size, size), 1)
    eye = (rows == cols).astype(F32)

    def off(block):
        return ((rows // (2 * block) == cols // (2 * block)) & (rows // block != cols // block)).astype(F32)

    found = [eye - part * off(1) for part in lower]
    block = 2
    while block < size:
        mask = off(block)
        half = [mm(x, part * mask, NN, 1) for x, part in zip(found, lower)]
        found = [x - mm(t, x, NN, 1) for x, t in zip(found, half)]
        block *= 2
    for _ in range(refine):
        rest = [(x - eye) + mm(part, x, NN) for x, part in zip(found, lower)]
        found = [x - mm(x, r, NN, 1) for x, r in zip(found, rest)]
    return found


def prepared(head, chunk, qref, kref, vref, pair_ref, tap_qk, tap_v, head_table, col_info, row_info):
    length, dk = qref.shape
    masks = [col_info[:, j : j + 1] for j in range(3)]
    masks = [jnp.broadcast_to(m, (length, dk)) for m in masks]
    dv = vref.shape[1]
    wide = [jnp.concatenate([m] * (dv // dk), axis=1) for m in masks]
    pre_q = conv(qref[...], tap_qk[0], masks)
    pre_k = conv(kref[...], tap_qk[1], masks)
    pre_v = conv(vref[...], tap_v[...], wide)
    out = dict(masks=masks, wide=wide, pre_q=pre_q, pre_k=pre_k, pre_v=pre_v)
    for name, pre in (("q", pre_q), ("k", pre_k), ("v", pre_v)):
        sig = lax.logistic(pre)
        out["sig_" + name] = sig
        out["act_" + name] = pre * sig
    out["inv_q"] = lax.rsqrt(jnp.sum(out["act_q"] ** 2, axis=1, keepdims=True) + EPS)
    out["inv_k"] = lax.rsqrt(jnp.sum(out["act_k"] ** 2, axis=1, keepdims=True) + EPS)
    out["q"] = out["act_q"] * out["inv_q"] * dk ** (-0.5)
    out["k"] = out["act_k"] * out["inv_k"]
    out["v"] = out["act_v"]
    pair = jnp.transpose(pair_ref[...])
    picked = iota(pair.shape, 0)
    a_row = jnp.sum(jnp.where(picked == 2 * head, pair, 0.0), axis=0, keepdims=True)
    b_row = jnp.sum(jnp.where(picked == 2 * head + 1, pair, 0.0), axis=0, keepdims=True)
    rate = jnp.exp(jnp.full((1, length), head_table[0, head], F32))
    a_row = a_row + head_table[1, head]
    softplus = jnp.maximum(a_row, 0.0) + jnp.log1p(jnp.exp(-jnp.abs(a_row)))
    decay = -rate * softplus
    beta = lax.logistic(b_row)
    total = chunk_scan(decay, chunk)
    entry = jnp.exp(total) * row_info[0:1]
    chunks = length // chunk
    place = iota((1, length), 1)
    ends = [total[:, (i + 1) * chunk - 1 : (i + 1) * chunk] for i in range(chunks)]
    last = ends[0]
    for i in range(1, chunks):
        last = jnp.where(place >= i * chunk, ends[i], jnp.broadcast_to(last, (1, length)))
    tail = jnp.exp(last - total) * row_info[1:2]
    rows = jnp.concatenate([beta, total, entry, tail, jnp.zeros((124, length), F32)], axis=0)
    cols = jnp.transpose(rows)
    out.update(
        a_row=a_row, rate=rate, decay=decay, beta_row=beta, total_row=total, entry_row=entry, tail_row=tail,
        beta=cols[:, 0:1], total=cols[:, 1:2], entry=cols[:, 2:3], tail=cols[:, 3:4],
    )
    return out


def chunk_parts(pre, i, chunk, col_info, row_info):
    s = slice(i * chunk, (i + 1) * chunk)
    q, k, v = pre["q"][s], pre["k"][s], pre["v"][s]
    beta, total, entry, tail = pre["beta"][s], pre["total"][s], pre["entry"][s], pre["tail"][s]
    rows, cols = iota((chunk, chunk), 0), iota((chunk, chunk), 1)
    allowed = (col_info[s, 3:4] == row_info[2:3, s]) & (rows >= cols)
    fading = jnp.where(allowed, jnp.exp(jnp.where(allowed, total - pre["total_row"][:, s], 0.0)), 0.0)
    both = mm(jnp.concatenate([q, k], axis=0), k, NT)
    strict_fading = jnp.where(rows > cols, fading, 0.0)
    qk, kk = both[:chunk], both[chunk:]
    return dict(
        q=q, k=k, v=v, beta=beta, entry=entry, tail=tail, fading=fading, strict=strict_fading,
        mixed=qk * fading, kk_faded=kk * strict_fading, lower=beta * (kk * strict_fading),
        exit=pre["entry_row"][:, (i + 1) * chunk - 1 : (i + 1) * chunk], rows=s,
    )


def forward_kernel(
    chunk, refine, qref, kref, vref, gref, pair_ref, tap_qk, tap_v, head_table, gain, col_ref, row_ref,
    mix_ref, rec_ref, fix_ref, inv_ref, state_ref,
):
    head = pl.program_id(1)
    col_info, row_info = col_ref[0], row_ref[0]
    pre = prepared(head, chunk, qref, kref, vref, pair_ref, tap_qk, tap_v, head_table, col_info, row_info)
    length, dk = qref.shape
    dv = vref.shape[1]
    chunks = length // chunk
    parts = [chunk_parts(pre, i, chunk, col_info, row_info) for i in range(chunks)]
    inverses = unit_lower_inverse([p["lower"] for p in parts], refine)
    state = jnp.zeros((dk, dv), F32)
    steps = []
    for p, inverse in zip(parts, inverses):
        target = jnp.concatenate([p["beta"] * p["entry"] * p["k"], p["beta"] * p["v"]], axis=1)
        solved = mm(inverse, target, NN)
        pushed = mm(p["k"] * p["tail"], solved, TN)
        steps.append((solved, pushed))
    states = []
    for p, (solved, pushed) in zip(parts, steps):
        states.append(state)
        state = p["exit"] * state - mm(pushed[:, :dk], state, NN) + pushed[:, dk:]
    gain_row = gain[...]
    for i, (p, inverse, (solved, pushed)) in enumerate(zip(parts, inverses, steps)):
        seen = mm(jnp.concatenate([solved[:, :dk], p["q"] * p["entry"]], axis=0), states[i], NN)
        fixed = solved[:, dk:] - seen[:chunk]
        rec = seen[chunk:] + mm(p["mixed"], fixed, NN)
        s = p["rows"]
        rec_ref[s, :] = rec
        fix_ref[s, :] = fixed
        inv_ref[0, 0, i] = inverse
        state_ref[0, 0, i] = states[i]
        normal = rec * lax.rsqrt(jnp.mean(rec * rec, axis=1, keepdims=True) + FLOOR)
        gate = gref[s, :]
        mix_ref[s, :] = (normal * gain_row * (gate * lax.logistic(gate))).astype(BF16)


def silu_grad(pre, sig):
    return sig * (1.0 + pre * (1.0 - sig))


def backward_kernel(
    chunk, heads, qref, kref, vref, gref, pair_ref, tap_qk, tap_v, head_table, gain, col_ref, row_ref,
    rec_ref, fix_ref, inv_ref, state_ref, dmix_ref,
    dproj_ref, dtap_qk, dtap_v, dhead_ref, dgain_ref,
):
    seq, head = pl.program_id(0), pl.program_id(1)
    col_info, row_info = col_ref[0], row_ref[0]
    pre = prepared(head, chunk, qref, kref, vref, pair_ref, tap_qk, tap_v, head_table, col_info, row_info)
    length, dk = qref.shape
    dv = vref.shape[1]
    chunks = length // chunk
    parts = [chunk_parts(pre, i, chunk, col_info, row_info) for i in range(chunks)]
    gain_row = gain[...]
    dgain = jnp.zeros((1, dv), F32)
    v_at = 2 * heads * dk
    g_at = v_at + heads * dv
    p_at = g_at + heads * dv
    for p in parts:
        s = p["rows"]
        rec, gate, dmix = rec_ref[s, :], gref[s, :], dmix_ref[s, :]
        scale = lax.rsqrt(jnp.mean(rec * rec, axis=1, keepdims=True) + FLOOR)
        sig = lax.logistic(gate)
        gated = dmix * (gate * sig)
        normal = rec * scale
        dgain = dgain + jnp.sum(gated * normal, axis=0, keepdims=True)
        dgate = dmix * normal * gain_row * silu_grad(gate, sig)
        dproj_ref[s, pl.ds(pl.multiple_of(g_at + head * dv, dv), dv)] = dgate.astype(BF16)
        dn = gated * gain_row
        p["drec"] = scale * dn - rec * (scale * scale * scale) * jnp.mean(dn * rec, axis=1, keepdims=True)
    for i, p in enumerate(parts):
        inverse = inv_ref[0, 0, i]
        p["inverse"] = inverse
        solved = mm(inverse, p["beta"] * p["entry"] * p["k"], NN)
        back = mm(p["mixed"], p["drec"], TN)
        p["back"] = back
        ahead = mm(solved, p["k"] * p["tail"], TN)
        given = mm(
            jnp.concatenate([p["q"] * p["entry"], -solved], axis=0),
            jnp.concatenate([p["drec"], back], axis=0), TN,
        )
        p["ahead"], p["given"] = ahead, given
    dstate = jnp.zeros((dk, dv), F32)
    for p in reversed(parts):
        p["dstate"] = dstate
        dstate = p["exit"] * dstate - mm(p["ahead"], dstate, NN) + p["given"]
    cols = iota((chunk, 8), 1)
    col_parts, row_parts, dqs, dks, dvs = [], [], [], [], []
    for i, p in enumerate(parts):
        s = p["rows"]
        state, dstate, fixed, drec = state_ref[0, 0, i], p["dstate"], fix_ref[s, :], p["drec"]
        q, k, v, beta, entry, tail = p["q"], p["k"], p["v"], p["beta"], p["entry"], p["tail"]
        dfixed = p["back"] + mm(k * tail, dstate, NN)
        dtarget = mm(p["inverse"], dfixed, TN)
        outer = mm(
            jnp.concatenate([drec, dtarget], axis=0), jnp.concatenate([state, fixed], axis=0), NT
        )
        drec_state, dtarget_state = outer[:chunk, :dk], outer[chunk:, :dk]
        dmixed, dlower = outer[:chunk, dk:], -outer[chunk:, dk:]
        fixed_dstate = mm(fixed, dstate, NT)
        g1 = dmixed * p["fading"]
        g2 = (beta * dlower) * p["strict"]
        stacked = jnp.concatenate([g1, g2], axis=0)
        first = mm(stacked, k, NN)
        second = mm(stacked, jnp.concatenate([q, k], axis=0), TN)
        key_state = jnp.sum(dtarget_state * k, axis=1, keepdims=True)
        dqs.append(entry * drec_state + first[:chunk])
        dks.append(first[chunk:] + second + tail * fixed_dstate - (beta * entry) * dtarget_state)
        dvs.append(beta * dtarget)
        dentry = jnp.sum(drec_state * q, axis=1, keepdims=True) - beta * key_state
        dtail = jnp.sum(fixed_dstate * k, axis=1, keepdims=True) * tail
        high = dmixed * p["mixed"] + dlower * p["lower"]
        dbeta = (
            jnp.sum(dtarget * v, axis=1, keepdims=True)
            - entry * key_state
            + jnp.sum(dlower * p["kk_faded"], axis=1, keepdims=True)
        )
        dtotal = jnp.sum(high, axis=1, keepdims=True) + dentry * entry - dtail
        end = p["exit"] * jnp.sum(jnp.sum(dstate * state, axis=1, keepdims=True), axis=0, keepdims=True)
        end = end + jnp.sum(dtail, axis=0, keepdims=True)
        dtotal = dtotal + jnp.where(iota((chunk, 1), 0) == chunk - 1, end, 0.0)
        row_parts.append(jnp.sum(high, axis=0, keepdims=True))
        col_parts.append(jnp.where(cols == 0, dtotal, jnp.where(cols == 1, dbeta, 0.0)))
    lanes = jnp.concatenate(col_parts, axis=0)
    lanes = jnp.concatenate([lanes, jnp.zeros((length, 120), F32)], axis=1)
    turned = jnp.transpose(lanes)
    dtotal_row = turned[0:1] - jnp.concatenate(row_parts, axis=1)
    dbeta_row = turned[1:2]
    ddecay = chunk_scan(dtotal_row, chunk, backward=True)
    da = -ddecay * pre["rate"] * lax.logistic(pre["a_row"])
    db = dbeta_row * pre["beta_row"] * (1.0 - pre["beta_row"])
    spread = iota((128, length), 0)
    dpair = jnp.where(spread == 2 * head, da, jnp.where(spread == 2 * head + 1, db, 0.0))
    dpair = jnp.transpose(dpair).astype(BF16)

    @pl.when(head == 0)
    def _():
        dproj_ref[:, p_at:] = dpair

    @pl.when(head != 0)
    def _():
        dproj_ref[:, p_at:] = dproj_ref[:, p_at:] + dpair

    dscale = jnp.sum(ddecay * pre["decay"], axis=1, keepdims=True)
    dbias = jnp.sum(da, axis=1, keepdims=True)
    which = iota((8, 128), 0)
    dhead = jnp.where(which == 0, dscale, jnp.where(which == 1, dbias, 0.0))
    dq, dk_all, dv_all = (jnp.concatenate(x, axis=0) for x in (dqs, dks, dvs))

    def through_norm(grad, act, inv, factor):
        return factor * (inv * grad - act * (inv * inv * inv) * jnp.sum(grad * act, axis=1, keepdims=True))

    dq = through_norm(dq, pre["act_q"], pre["inv_q"], dk ** (-0.5))
    dk_all = through_norm(dk_all, pre["act_k"], pre["inv_k"], 1.0)
    taps_out = []
    for grad, name, src, taps, masks, at in (
        (dq, "q", qref, tap_qk[0], pre["masks"], head * dk),
        (dk_all, "k", kref, tap_qk[1], pre["masks"], heads * dk + head * dk),
        (dv_all, "v", vref, tap_v[...], pre["wide"], v_at + head * dv),
    ):
        dpre = grad * silu_grad(pre["pre_" + name], pre["sig_" + name])
        signal = src[...]
        dsignal = dpre * taps[0:1]
        dtaps = [jnp.sum(dpre * signal, axis=0, keepdims=True)]
        for j in range(1, 4):
            masked = dpre * masks[j - 1]
            dsignal = dsignal + shifted_rows(masked, -j) * taps[j : j + 1]
            dtaps.append(jnp.sum(masked * shifted_rows(signal, j), axis=0, keepdims=True))
        width = grad.shape[1]
        dproj_ref[:, pl.ds(pl.multiple_of(at, width), width)] = dsignal.astype(BF16)
        taps_out.append(jnp.concatenate(dtaps, axis=0))
    dtap_qk[0, 0] = taps_out[0]
    dtap_qk[0, 1] = taps_out[1]
    dtap_v[0] = taps_out[2]
    dhead_ref[0, 0] = dhead
    dgain_ref[0, 0] = dgain


def specs(length, heads, dk, dv):
    v_block = 2 * heads * dk // dv
    return [
        pl.BlockSpec((length, dk), lambda s, h: (s, h)),
        pl.BlockSpec((length, dk), lambda s, h: (s, heads + h)),
        pl.BlockSpec((length, dv), lambda s, h: (s, v_block + h)),
        pl.BlockSpec((length, dv), lambda s, h: (s, v_block + heads + h)),
        pl.BlockSpec((length, 128), lambda s, h: (s, (2 * heads * dk + 2 * heads * dv) // 128)),
        pl.BlockSpec((2, 4, dk), lambda s, h: (0, 0, h)),
        pl.BlockSpec((4, dv), lambda s, h: (0, h)),
        pl.BlockSpec(memory_space=pltpu.SMEM),
        pl.BlockSpec((1, dv), lambda s, h: (0, 0)),
        pl.BlockSpec((1, length, 8), lambda s, h: (s, 0, 0)),
        pl.BlockSpec((1, 8, length), lambda s, h: (s, 0, 0)),
    ]


def segment_tables(segment_ids, chunk):
    seqs, length = segment_ids.shape
    place = jnp.arange(length)
    conv_masks = []
    for j in range(1, 4):
        earlier = jnp.pad(segment_ids, ((0, 0), (j, 0)), constant_values=-1)[:, :length]
        conv_masks.append(earlier == segment_ids)
    blocks = segment_ids.reshape(seqs, length // chunk, chunk)
    finals = blocks[:, :, -1]
    before = jnp.concatenate([segment_ids[:, :1], finals[:, :-1]], axis=1)
    carried = (blocks == before[:, :, None]).reshape(seqs, length)
    tailed = (blocks == finals[:, :, None]).reshape(seqs, length)
    zero = jnp.zeros((seqs, length), F32)
    ids = segment_ids.astype(F32)
    rows = jnp.stack([carried.astype(F32), tailed.astype(F32), ids] + [zero] * 5, axis=1)
    cols = jnp.stack([m.astype(F32) for m in conv_masks] + [ids] + [zero] * 4, axis=2)
    return cols, rows


def delta_forward(proj, taps_qk, taps_v, head_table, gain, tables, seqs, heads, chunk, refine):
    cols, rows = tables
    length = cols.shape[1]
    dk, dv = taps_qk.shape[2] // heads, taps_v.shape[1] // heads
    chunks = length // chunk
    tokens = seqs * length
    column = pl.BlockSpec((length, dv), lambda s, h: (s, h))
    return pl.pallas_call(
        functools.partial(forward_kernel, chunk, refine),
        grid=(seqs, heads),
        in_specs=specs(length, heads, dk, dv),
        out_specs=[
            column, column, column,
            pl.BlockSpec((1, 1, chunks, chunk, chunk), lambda s, h: (s, h, 0, 0, 0)),
            pl.BlockSpec((1, 1, chunks, dk, dv), lambda s, h: (s, h, 0, 0, 0)),
        ],
        out_shape=[
            jax.ShapeDtypeStruct((tokens, heads * dv), BF16),
            pltpu.HBM((tokens, heads * dv), F32),
            pltpu.HBM((tokens, heads * dv), F32),
            pltpu.HBM((seqs, heads, chunks, chunk, chunk), F32),
            pltpu.HBM((seqs, heads, chunks, dk, dv), F32),
        ],
        compiler_params=pltpu.CompilerParams(vmem_limit_bytes=48 * 2**20),
        cost_estimate=cost(15),
        name="delta_forward",
    )(proj, proj, proj, proj, proj, taps_qk, taps_v, head_table, gain, cols, rows)


def delta_backward(proj, taps_qk, taps_v, head_table, gain, tables, saved, dmix, seqs, heads, chunk):
    cols, rows = tables
    length = cols.shape[1]
    dk, dv = taps_qk.shape[2] // heads, taps_v.shape[1] // heads
    chunks = length // chunk
    tokens = seqs * length
    width = proj.shape[1]
    column = pl.BlockSpec((length, dv), lambda s, h: (s, h))
    return pl.pallas_call(
        functools.partial(backward_kernel, chunk, heads),
        grid=(seqs, heads),
        in_specs=specs(length, heads, dk, dv)
        + [
            column, column,
            pl.BlockSpec((1, 1, chunks, chunk, chunk), lambda s, h: (s, h, 0, 0, 0)),
            pl.BlockSpec((1, 1, chunks, dk, dv), lambda s, h: (s, h, 0, 0, 0)),
            column,
        ],
        out_specs=[
            pl.BlockSpec((length, width), lambda s, h: (s, 0)),
            pl.BlockSpec((1, 2, 4, dk), lambda s, h: (s, 0, 0, h)),
            pl.BlockSpec((1, 4, dv), lambda s, h: (s, 0, h)),
            pl.BlockSpec((1, 1, 8, 128), lambda s, h: (s, h, 0, 0)),
            pl.BlockSpec((1, 1, 1, dv), lambda s, h: (s, h, 0, 0)),
        ],
        out_shape=[
            jax.ShapeDtypeStruct((tokens, width), BF16),
            jax.ShapeDtypeStruct((seqs, 2, 4, heads * dk), F32),
            jax.ShapeDtypeStruct((seqs, 4, heads * dv), F32),
            jax.ShapeDtypeStruct((seqs, heads, 8, 128), F32),
            jax.ShapeDtypeStruct((seqs, heads, 1, dv), F32),
        ],
        compiler_params=pltpu.CompilerParams(vmem_limit_bytes=56 * 2**20),
        cost_estimate=cost(25),
        name="delta_backward",
    )(proj, proj, proj, proj, proj, taps_qk, taps_v, head_table, gain, cols, rows, *saved, dmix)


MESH = pl.DeviceIdType.MESH
VMEM_LIMIT = 58 * 2**20
HALVES = 2
LAYERS = 2


class Line:
    def __init__(self, send_sem, recv_sem):
        self.send_sem, self.recv_sem = send_sem, recv_sem
        self.me = lax.axis_index("tensor")

    def greet(self):
        barrier = pltpu.get_barrier_semaphore()
        for m in range(4):
            @pl.when(self.me == m)
            def _():
                for t in range(4):
                    if t != m and {t, m} != {0, 3}:
                        pl.semaphore_signal(barrier, inc=1, device_id={"tensor": t}, device_id_type=MESH)

    def meet(self, others=0):
        barrier = pltpu.get_barrier_semaphore()
        for m in range(4):
            @pl.when(self.me == m)
            def _():
                pl.semaphore_wait(barrier, others + (2 if m in (0, 3) else 3))

    def copy(self, phase, source, target, to, send_at, recv_at):
        return pltpu.make_async_remote_copy(
            src_ref=source, dst_ref=target, send_sem=self.send_sem.at[phase, send_at],
            recv_sem=self.recv_sem.at[phase, recv_at], device_id={"tensor": to}, device_id_type=MESH,
        )

    def gather_start(self, phase, blocks):
        for m in range(4):
            @pl.when(self.me == m)
            def _():
                for t in range(4):
                    if t != m and {t, m} != {0, 3}:
                        self.copy(phase, blocks[m], blocks[m], t, t, m).start()

    def gather_forward(self, phase, blocks):
        for m in (1, 2):
            @pl.when(self.me == m)
            def _():
                far, to = (3, 0) if m == 1 else (0, 3)
                self.copy(phase, blocks[far], blocks[far], to, m, far).wait_recv()
                self.copy(phase, blocks[far], blocks[far], to, m, far).start()

    def gather_wait(self, phase, blocks):
        for m in range(4):
            @pl.when(self.me == m)
            def _():
                for b in range(4):
                    if b != m and not (m in (1, 2) and b == (3 if m == 1 else 0)):
                        self.copy(phase, blocks[b], blocks[b], b, b, b).wait_recv()

    def gather_drain(self, phase, blocks):
        for m in range(4):
            @pl.when(self.me == m)
            def _():
                for t in range(4):
                    if t != m and {t, m} != {0, 3}:
                        self.copy(phase, blocks[m], blocks[m], t, t, m).wait_send()
                if m in (1, 2):
                    far, to = (3, 0) if m == 1 else (0, 3)
                    self.copy(phase, blocks[far], blocks[far], to, m, far).wait_send()

    def scatter_start(self, phase, parts, slots):
        for m in range(4):
            @pl.when(self.me == m)
            def _():
                if m in (0, 3):
                    through = 1 if m == 0 else 2
                    self.copy(phase, parts[3 - m], slots[4], through, 3 - m, 4).start()
                for t in range(4):
                    if t != m and {t, m} != {0, 3}:
                        if not (m in (1, 2) and t == (3 if m == 1 else 0)):
                            self.copy(phase, parts[t], slots[m], t, t, m).start()

    def scatter_relay(self, phase, parts, slots):
        for m in (1, 2):
            @pl.when(self.me == m)
            def _():
                t = 3 if m == 1 else 0
                self.copy(phase, parts[t], slots[4], t, t, 4).wait_recv()
                parts[t][...] = (parts[t][...].astype(F32) + slots[4][...].astype(F32)).astype(BF16)
                self.copy(phase, parts[t], slots[m], t, t, m).start()

    def scatter_wait(self, phase, parts, slots):
        for m in range(4):
            @pl.when(self.me == m)
            def _():
                for s in range(4):
                    if s != m and {s, m} != {0, 3}:
                        self.copy(phase, parts[s], slots[s], s, s, s).wait_recv()

    def scatter_sum(self, total, parts, slots):
        for m in range(4):
            @pl.when(self.me == m)
            def _():
                value = parts[m][...].astype(F32)
                for s in range(4):
                    if s != m and {s, m} != {0, 3}:
                        value = value + slots[s][...].astype(F32)
                total[...] = value

    def scatter_drain(self, phase, parts, slots):
        for m in range(4):
            @pl.when(self.me == m)
            def _():
                for t in range(4):
                    if t != m:
                        self.copy(phase, parts[t], slots[m], t, t, m).wait_send()


TURN_AT = 1


class Turns:
    def __init__(self, gate):
        self.gate = gate
        self.me = lax.axis_index("dp")
        self.second = lax.rem(self.me, 2)
        self.sibling = self.me + 1 - 2 * self.second

    def greet(self):
        pl.semaphore_signal(
            pltpu.get_barrier_semaphore(), inc=1, device_id={"dp": self.sibling}, device_id_type=MESH
        )

    def wait(self):
        @pl.when(self.second == 1)
        def _():
            pl.semaphore_wait(self.gate, 1)

    def give(self):
        @pl.when(self.second == 0)
        def _():
            pl.semaphore_signal(self.gate, inc=1, device_id={"dp": self.sibling}, device_id_type=MESH)


class Sums:
    def __init__(self, source, near, far, near_send, near_recv, far_send, far_recv):
        self.source, self.near, self.far = source, near, far
        self.near_send, self.near_recv, self.far_send, self.far_recv = near_send, near_recv, far_send, far_recv
        self.pairs = source.shape[0]
        self.group = self.pairs // 4
        me = lax.axis_index("dp")
        self.parity, self.mine = lax.rem(me, 2), lax.div(me, 2)

    def greet(self):
        barrier = pltpu.get_barrier_semaphore()
        sibling = 2 * self.mine + 1 - self.parity
        pl.semaphore_signal(barrier, inc=1, device_id={"dp": sibling}, device_id_type=MESH)

        def signal(i, carry):
            other = 2 * lax.rem(self.mine + i, self.pairs) + self.parity
            pl.semaphore_signal(barrier, inc=1, device_id={"dp": other}, device_id_type=MESH)
            return carry

        lax.fori_loop(1, self.pairs, signal, 0)
        return self.pairs

    def greet_late(self, gate):
        self.gate = gate
        barrier = pltpu.get_barrier_semaphore()
        sibling = 2 * self.mine + 1 - self.parity

        @pl.when(self.parity == 0)
        def _():
            pl.semaphore_signal(barrier, inc=1, device_id={"dp": sibling}, device_id_type=MESH)

        def signal(i, carry):
            other = 2 * lax.rem(self.mine + i, self.pairs) + self.parity
            pl.semaphore_signal(barrier, inc=1, device_id={"dp": other}, device_id_type=MESH)
            return carry

        lax.fori_loop(1, self.pairs, signal, 0)

    def meet_late(self, line):
        @pl.when(self.parity == 0)
        def _():
            line.meet(self.pairs - 1)

        @pl.when(self.parity == 1)
        def _():
            line.meet(self.pairs)
            pl.semaphore_signal(self.gate, inc=1, device_id={"dp": 2 * self.mine}, device_id_type=MESH)
            for m in range(4):
                self.start(m)

    def start_late(self):
        @pl.when(self.parity == 0)
        def _():
            pl.semaphore_wait(self.gate, 1)
            for m in range(4):
                self.start(m)

    def near_copy(self, m):
        span = pl.ds(m * self.group, self.group)
        return pltpu.make_async_remote_copy(
            src_ref=self.source.at[span, 1 - self.parity], dst_ref=self.near.at[span],
            send_sem=self.near_send.at[m], recv_sem=self.near_recv.at[m],
            device_id={"dp": 2 * self.mine + 1 - self.parity}, device_id_type=MESH,
        )

    def far_copy(self, j, slot, to):
        return pltpu.make_async_remote_copy(
            src_ref=self.near.at[j], dst_ref=self.far.at[slot], send_sem=self.far_send.at[j],
            recv_sem=self.far_recv.at[slot], device_id={"dp": 2 * to + self.parity}, device_id_type=MESH,
        )

    def start(self, m):
        self.near_copy(m).start()

    def turn(self, m):
        self.near_copy(m).wait_recv()
        rows = self.near.shape[1]
        step = 16

        def add(i, carry):
            j = m * self.group + lax.div(i, rows // step)
            span = pl.ds(pl.multiple_of(lax.rem(i, rows // step) * step, step), step)
            both = self.source[j, self.parity, span, :].astype(F32) + self.near[j, span, :].astype(F32)
            self.near[j, span, :] = both.astype(BF16)
            return carry

        lax.fori_loop(0, self.group * (rows // step), add, 0)

        def send(i, carry):
            j = m * self.group + i

            @pl.when(j != self.mine)
            def _():
                self.far_copy(j, self.mine, j).start()

            return carry

        lax.fori_loop(0, self.group, send, 0)

    def finish(self, out):
        def arrive(i, carry):
            slot = lax.rem(self.mine + i, self.pairs)
            self.far_copy(slot, slot, slot).wait_recv()
            return carry

        lax.fori_loop(1, self.pairs, arrive, 0)
        rows = out.shape[0]
        step = 16

        def add(i, carry):
            span = pl.ds(pl.multiple_of(i * step, step), step)
            total = self.near[self.mine, span, :].astype(F32)

            def more(j, value):
                return value + self.far[lax.rem(self.mine + j, self.pairs), span, :].astype(F32)

            if self.pairs <= 4:
                for j in range(1, self.pairs):
                    total = more(j, total)
            else:
                total = lax.fori_loop(1, self.pairs, more, total)
            out[span, :] = total
            return carry

        lax.fori_loop(0, rows // step, add, 0)

        def sent(i, carry):
            slot = lax.rem(self.mine + i, self.pairs)
            self.far_copy(slot, slot, slot).wait_send()
            return carry

        lax.fori_loop(1, self.pairs, sent, 0)
        for m in range(4):
            self.near_copy(m).wait_send()


class Spread:
    def __init__(self, whole, far_send, far_recv, near_send, near_recv):
        self.whole = whole
        self.far_send, self.far_recv, self.near_send, self.near_recv = far_send, far_recv, near_send, near_recv
        self.pairs = whole.shape[0] // 2
        self.me = lax.axis_index("dp")
        self.parity, self.mine = lax.rem(self.me, 2), lax.div(self.me, 2)

    def greet(self):
        barrier = pltpu.get_barrier_semaphore()
        sibling = self.me + 1 - 2 * self.parity
        pl.semaphore_signal(barrier, inc=1, device_id={"dp": sibling}, device_id_type=MESH)

        def signal(i, carry):
            other = 2 * lax.rem(self.mine + i, self.pairs) + self.parity
            pl.semaphore_signal(barrier, inc=1, device_id={"dp": other}, device_id_type=MESH)
            return carry

        lax.fori_loop(1, self.pairs, signal, 0)
        return self.pairs

    def far_copy(self, block, to, slot):
        return pltpu.make_async_remote_copy(
            src_ref=self.whole.at[block], dst_ref=self.whole.at[block], send_sem=self.far_send.at[to],
            recv_sem=self.far_recv.at[slot], device_id={"dp": 2 * to + self.parity}, device_id_type=MESH,
        )

    def near_copy(self, j, parity):
        block = 2 * j + parity
        return pltpu.make_async_remote_copy(
            src_ref=self.whole.at[block], dst_ref=self.whole.at[block], send_sem=self.near_send.at[j],
            recv_sem=self.near_recv.at[j], device_id={"dp": self.me + 1 - 2 * self.parity}, device_id_type=MESH,
        )

    def over_others(self, step):
        def run(i, carry):
            step(lax.rem(self.mine + i, self.pairs))
            return carry

        lax.fori_loop(1, self.pairs, run, 0)

    def start(self):
        self.over_others(lambda j: self.far_copy(self.me, j, self.mine).start())
        self.near_copy(self.mine, self.parity).start()

    def forward(self):
        def step(j):
            self.far_copy(2 * j + self.parity, j, j).wait_recv()
            self.near_copy(j, self.parity).start()

        self.over_others(step)

    def finish(self):
        other = 1 - self.parity
        self.over_others(lambda j: self.near_copy(j, other).wait_recv())
        self.near_copy(self.mine, other).wait_recv()
        self.over_others(lambda j: self.far_copy(self.me, j, self.mine).wait_send())
        self.over_others(lambda j: self.near_copy(j, self.parity).wait_send())
        self.near_copy(self.mine, self.parity).wait_send()


class Smalls:
    def __init__(self, axis, land, send_sem, recv_sem):
        self.axis, self.land, self.send_sem, self.recv_sem = axis, land, send_sem, recv_sem
        self.me, self.count = lax.axis_index(axis), land.shape[0]

    def other(self, i):
        return lax.rem(self.me + i, self.count)

    def greet(self):
        barrier = pltpu.get_barrier_semaphore()

        def signal(i, carry):
            pl.semaphore_signal(barrier, inc=1, device_id={self.axis: self.other(i)}, device_id_type=MESH)
            return carry

        lax.fori_loop(1, self.count, signal, 0)
        return self.count - 1

    def copy(self, slot, to):
        return pltpu.make_async_remote_copy(
            src_ref=self.land.at[self.me], dst_ref=self.land.at[slot], send_sem=self.send_sem.at[to],
            recv_sem=self.recv_sem.at[slot], device_id={self.axis: to}, device_id_type=MESH,
        )

    def start(self):
        def send(i, carry):
            self.copy(self.me, self.other(i)).start()
            return carry

        lax.fori_loop(1, self.count, send, 0)

    def finish(self):
        def arrive(i, carry):
            self.copy(self.other(i), self.other(i)).wait_recv()
            return carry

        lax.fori_loop(1, self.count, arrive, 0)

        def add(i, value):
            return value + self.land[i]

        total = lax.fori_loop(1, self.count, add, self.land[0])

        def sent(i, carry):
            self.copy(self.me, self.other(i)).wait_send()
            return carry

        lax.fori_loop(1, self.count, sent, 0)
        return total


def half_of(ref, h):
    value = ref[:, h]
    return value.reshape(value.shape[0] * value.shape[1], value.shape[2])


def blocks_of(ref, h):
    return [ref.at[b, h] for b in range(4)]


def parts_of(part, slots, k, h):
    return [part.at[k, h, t] for t in range(4)], [slots.at[k, h, s] for s in range(5)]


def for_tiles(size, tile, step):
    def run(i, carry):
        step(pl.multiple_of(i * tile, tile))
        return carry

    lax.fori_loop(0, size // tile, run, 0)


def partial_sums(left, weight, part, k, h):
    def step(n):
        value = lax.dot_general(left, weight[pl.ds(n, 256), :], NT, preferred_element_type=F32)
        part[k, h, :, :, pl.ds(n, 256)] = value.astype(BF16).reshape(4, left.shape[0] // 4, 256)

    for_tiles(weight.shape[0], 256, step)


def row_grads(left, right, out, column):
    rows = left.shape[0] * left.shape[1] * left.shape[2]
    width = right.shape[3]
    pairs, _, own, _ = out.shape
    group = pairs // 4
    tall = group * 2 * own

    def piece(m):
        start = pl.multiple_of(m * tall, tall)
        turned = jnp.transpose(left[:, :, :, pl.ds(start, tall)].reshape(rows, tall))
        for n in range(0, width, 512):
            size = min(512, width - n)
            tile = right[:, :, :, n : n + size].reshape(rows, size)
            value = lax.dot_general(turned, tile, NN, preferred_element_type=F32)
            span = pl.ds(m * group, group)
            out[span, :, :, column + n : column + n + size] = value.astype(BF16).reshape(group, 2, own, size)

    return piece


def run_pieces(pieces, first, last):
    def run(m, carry):
        for piece in pieces:
            piece(m)
        return carry

    lax.fori_loop(first, last, run, 0)


def rms(value, gain):
    return value * lax.rsqrt(jnp.mean(value * value, axis=1, keepdims=True) + EPS) * gain


def rms_back(value, gain, grad):
    scale = lax.rsqrt(jnp.mean(value * value, axis=1, keepdims=True) + EPS)
    scaled = gain * grad
    back = scale * scaled - value * (scale * scale * scale) * jnp.mean(value * scaled, axis=1, keepdims=True)
    return back, jnp.sum(value * scale * grad, axis=0, keepdims=True)


def is_turned(shape):
    return shape[1] % 128 == 0 and shape[2] % 128 != 0


def turn(array):
    return jnp.swapaxes(array, 1, 2) if is_turned(array.shape) else array


def fetch_start(sources, held, sems, l):
    for i, source in enumerate(sources):
        pltpu.make_async_copy(source.at[l], held[i], sems.at[i]).start()


def cast_into(out, sources, held, sems, l, places):
    start = 0
    for i, (turned, width, padded) in enumerate(places):
        pltpu.make_async_copy(sources[i].at[l], held[i], sems.at[i]).wait()
        value = held[i][...]
        if turned:
            tall = -(-width // 128) * 128
            if tall > width:
                value = jnp.concatenate([value, jnp.zeros((tall - width, value.shape[1]), F32)], axis=0)
            value = jnp.transpose(value)
            width = tall
        out[:, start : start + width] = value.astype(BF16)
        if padded > width:
            out[:, start + width : start + padded] = jnp.zeros((value.shape[0], padded - width), BF16)
        start += padded


def cast_places(weights, units):
    return [(is_turned(w.shape), w.shape[2], -(-w.shape[2] // u) * u) for w, u in zip(weights, units)]


def cast_scratch(weights):
    return [pltpu.VMEM(held_shape(w), F32) for w in weights] + [DMA((len(weights),))]


def held_shape(w):
    _, own, width = w.shape
    return (width, own) if is_turned(w.shape) else (own, width)


def cast_kernel(l, places, *refs):
    count = len(places)
    sources, out, held, sems = refs[:count], refs[count], refs[count + 1 : -1], refs[-1]
    fetch_start(sources, held, sems, l)
    cast_into(out, sources, held, sems, l, places)


def cast_call(weights, units, l):
    places = cast_places(weights, units)
    return pl.pallas_call(
        functools.partial(cast_kernel, l, places),
        in_specs=[pl.BlockSpec(memory_space=pl.ANY)] * len(weights),
        out_specs=pl.BlockSpec(memory_space=pltpu.VMEM),
        out_shape=jax.ShapeDtypeStruct((weights[0].shape[1], sum(p[2] for p in places)), BF16),
        scratch_shapes=cast_scratch(weights),
        compiler_params=pltpu.CompilerParams(vmem_limit_bytes=VMEM_LIMIT),
        cost_estimate=cost(2),
        name="cast",
    )(*[turn(w) for w in weights])


def start_kernel(in_places, rest_places, rows, cot, gain, *refs):
    first, second = len(in_places), len(rest_places)
    sources, refs = refs[: first + second], refs[first + second :]
    (normed, cot_all, w_in), refs = refs[:3], refs[3:]
    low, refs = refs[: 2 * (LAYERS - 1)], refs[2 * (LAYERS - 1) :]
    held, (in_sems, rest_sems, send_sem, recv_sem, *spread_sems) = refs[: first + second], refs[first + second :]
    in_refs = sources[:first], held[:first], in_sems
    rest_refs = sources[first:], held[first:], rest_sems
    line = Line(send_sem, recv_sem)
    spread = Spread(w_in, *spread_sems)
    fetch_start(*in_refs, 0)
    line.greet()
    others = spread.greet()
    cast_into(w_in.at[spread.me], *in_refs, 0, in_places)
    for h in range(HALVES):
        normed[line.me, h] = rms(rows[h].astype(F32), gain[...]).astype(BF16)
        cot_all[line.me, h] = cot[h]
    line.meet(others)
    spread.start()
    both = [(k + h, blocks_of(ref, h)) for k, ref in ((0, normed), (2, cot_all)) for h in range(HALVES)]
    for item in both:
        line.gather_start(*item)
    for l in range(1, LAYERS):
        fetch_start(*in_refs, l)
        fetch_start(*rest_refs, l)
        cast_into(low[2 * l - 2], *in_refs, l, in_places)
        cast_into(low[2 * l - 1], *rest_refs, l, rest_places)
    for item in both[:2]:
        line.gather_forward(*item)
    spread.forward()
    for item in both[2:]:
        line.gather_forward(*item)
    for item in both:
        line.gather_wait(*item)
    for item in both:
        line.gather_drain(*item)
    spread.finish()


def slices_of(weights, v_width, wide):
    return (
        weights.at[:, :v_width],
        weights.at[:, v_width : v_width + 2 * wide],
        weights.at[:, v_width + 2 * wide :],
    )


def ffn_forward_kernel(last, mixer, weights, rows, gain, gain_next, middle, normed, pre, hidden, out_rows, *rest):
    if last:
        part, slots, total, send_sem, recv_sem = rest
    else:
        normed_next, part, slots, total, send_sem, recv_sem, gate = rest
    line = Line(send_sem, recv_sem)
    wide = hidden.shape[3]
    w_out, w_up, w_down = slices_of(weights, mixer.shape[3], wide)
    block = rows.shape[1]
    line.greet()
    if last:
        partial_sums(half_of(mixer, 0), w_out, part, 0, 0)
        line.meet()
    else:
        turns = Turns(gate)
        turns.greet()
        partial_sums(half_of(mixer, 0), w_out, part, 0, 0)
        line.meet(1)
        turns.wait()
    line.scatter_start(0, *parts_of(part, slots, 0, 0))
    partial_sums(half_of(mixer, 1), w_out, part, 0, 1)
    line.scatter_relay(0, *parts_of(part, slots, 0, 0))
    line.scatter_start(1, *parts_of(part, slots, 0, 1))
    line.scatter_relay(1, *parts_of(part, slots, 0, 1))
    for h in range(HALVES):
        both = parts_of(part, slots, 0, h)
        line.scatter_wait(h, *both)
        line.scatter_sum(total, *both)
        value = rows[h].astype(F32) + total[...]
        middle[h] = value
        normed[line.me, h] = rms(value, gain[...]).astype(BF16)
        line.gather_start(2 + h, blocks_of(normed, h))
    line.gather_forward(2, blocks_of(normed, 0))
    for h in range(HALVES):
        if h == 1:
            line.gather_forward(3, blocks_of(normed, 1))
        line.gather_wait(2 + h, blocks_of(normed, h))
        if h == TURN_AT and not last:
            turns.give()
        left = half_of(normed, h)

        def step(n):
            gate = jnp.dot(left, w_up[:, pl.ds(n, 256)], preferred_element_type=F32)
            up = jnp.dot(left, w_up[:, pl.ds(n + wide, 256)], preferred_element_type=F32)
            pre[:, h, :, pl.ds(n, 256)] = gate.reshape(4, block, 256)
            pre[:, h, :, pl.ds(n + wide, 256)] = up.reshape(4, block, 256)
            value = gate * lax.logistic(gate) * up
            hidden[:, h, :, pl.ds(n, 256)] = value.astype(BF16).reshape(4, block, 256)

        for_tiles(wide, 256, step)
        partial_sums(half_of(hidden, h), w_down, part, 1, h)
        if h == 1:
            line.scatter_relay(4, *parts_of(part, slots, 1, 0))
        line.scatter_start(4 + h, *parts_of(part, slots, 1, h))
    line.scatter_relay(5, *parts_of(part, slots, 1, 1))
    for h in range(HALVES):
        both = parts_of(part, slots, 1, h)
        line.scatter_wait(4 + h, *both)
        line.scatter_sum(total, *both)
        value = middle[h] + total[...]
        out_rows[h] = value
        if not last:
            normed_next[line.me, h] = rms(value, gain_next[...]).astype(BF16)
            line.gather_start(6 + h, blocks_of(normed_next, h))
    if not last:
        for h in range(HALVES):
            line.gather_forward(6 + h, blocks_of(normed_next, h))
        for h in range(HALVES):
            line.gather_wait(6 + h, blocks_of(normed_next, h))
    for h in range(HALVES):
        line.scatter_drain(h, *parts_of(part, slots, 0, h))
        line.gather_drain(2 + h, blocks_of(normed, h))
        line.scatter_drain(4 + h, *parts_of(part, slots, 1, h))
        if not last:
            line.gather_drain(6 + h, blocks_of(normed_next, h))


def ffn_backward_kernel(owes, cot, hidden, pre, normed, middle, grad, gain, weights, *rest):
    if owes:
        owed, d_mixer, grads, mixer_cot, grad_out, d_gain, summed, *rest = rest
    else:
        d_mixer, grads, mixer_cot, grad_out, d_gain, *rest = rest
    d_pre, part, slots, total, send_sem, recv_sem, *rest = rest
    sums = None
    if owes:
        near, far, near_send, near_recv, far_send, far_recv, gate = rest
        sums = Sums(owed, near, far, near_send, near_recv, far_send, far_recv)
    line = Line(send_sem, recv_sem)
    wide = hidden.shape[3]
    w_out, w_up, w_down = slices_of(weights, d_mixer.shape[3], wide)
    block = middle.shape[1]
    line.greet()
    if owes:
        sums.greet_late(gate)
        sums.meet_late(line)
    else:
        line.meet()
    for h in range(HALVES):
        left = half_of(cot, h)

        def step(n):
            d_hidden = jnp.dot(left, w_down[:, pl.ds(n, 256)], preferred_element_type=F32)
            gate = pre[:, h, :, pl.ds(n, 256)].reshape(4 * block, 256)
            up = pre[:, h, :, pl.ds(n + wide, 256)].reshape(4 * block, 256)
            sig = lax.logistic(gate)
            d_gate = d_hidden * up * sig * (1.0 + gate * (1.0 - sig))
            d_up = d_hidden * gate * sig
            d_pre[:, h, :, pl.ds(n, 256)] = d_gate.astype(BF16).reshape(4, block, 256)
            d_pre[:, h, :, pl.ds(n + wide, 256)] = d_up.astype(BF16).reshape(4, block, 256)

        for_tiles(wide, 256, step)
        partial_sums(half_of(d_pre, h), w_up, part, 0, h)
        if h == 1:
            line.scatter_relay(0, *parts_of(part, slots, 0, 0))
        line.scatter_start(h, *parts_of(part, slots, 0, h))
    if owes:
        @pl.when(sums.parity == 1)
        def _():
            for m in range(4):
                sums.turn(m)

    line.scatter_relay(1, *parts_of(part, slots, 0, 1))
    pieces = [row_grads(cot, hidden, grads, 0), row_grads(normed, d_pre, grads, wide)]
    run_pieces(pieces, 0, 2)
    if owes:
        sums.start_late()
    d_gain[...] = jnp.zeros_like(d_gain)
    for h in range(HALVES):
        both = parts_of(part, slots, 0, h)
        line.scatter_wait(h, *both)
        line.scatter_sum(total, *both)
        back, gain_part = rms_back(middle[h], gain[...], total[...])
        d_gain[...] += gain_part
        value = grad[h].astype(F32) + back
        grad_out[h] = value
        mixer_cot[line.me, h] = value.astype(BF16)
        line.gather_start(2 + h, blocks_of(mixer_cot, h))
        if owes:
            @pl.when(sums.parity == 0)
            def _():
                sums.turn(2 * h)
                sums.turn(2 * h + 1)

    run_pieces(pieces, 2, 3)
    line.gather_forward(2, blocks_of(mixer_cot, 0))
    line.gather_forward(3, blocks_of(mixer_cot, 1))
    run_pieces(pieces, 3, 4)
    for h in range(HALVES):
        line.gather_wait(2 + h, blocks_of(mixer_cot, h))
        left = half_of(mixer_cot, h)
        for n in range(0, w_out.shape[1], 256):
            value = jnp.dot(left, w_out[:, n : n + 256], preferred_element_type=F32)
            d_mixer[:, h, :, n : n + 256] = value.reshape(4, block, 256)
    for h in range(HALVES):
        line.scatter_drain(h, *parts_of(part, slots, 0, h))
        line.gather_drain(2 + h, blocks_of(mixer_cot, h))
    if owes:
        sums.finish(summed)


def mixer_backward_kernel(
    d_proj, w_in, normed, mixer, mixer_cot, rows, grad, gain,
    grad_out, d_gain, grads, cot, part, slots, total, send_sem, recv_sem,
):
    line = Line(send_sem, recv_sem)
    line.greet()
    line.meet()
    partial_sums(half_of(d_proj, 0), w_in, part, 0, 0)
    line.scatter_start(0, *parts_of(part, slots, 0, 0))
    partial_sums(half_of(d_proj, 1), w_in, part, 0, 1)
    line.scatter_relay(0, *parts_of(part, slots, 0, 0))
    line.scatter_start(1, *parts_of(part, slots, 0, 1))
    line.scatter_relay(1, *parts_of(part, slots, 0, 1))
    width = mixer.shape[3]
    pieces = [row_grads(mixer_cot, mixer, grads, 0), row_grads(normed, d_proj, grads, width)]
    run_pieces(pieces, 0, 2)
    d_gain[...] = jnp.zeros_like(d_gain)
    for h in range(HALVES):
        both = parts_of(part, slots, 0, h)
        line.scatter_wait(h, *both)
        line.scatter_sum(total, *both)
        back, gain_part = rms_back(rows[h].astype(F32), gain[...], total[...])
        d_gain[...] += gain_part
        value = grad[h] + back
        grad_out[h] = value
        cot[line.me, h] = value.astype(BF16)
        line.gather_start(2 + h, blocks_of(cot, h))
    run_pieces(pieces, 2, 3)
    line.gather_forward(2, blocks_of(cot, 0))
    line.gather_forward(3, blocks_of(cot, 1))
    run_pieces(pieces, 3, 4)
    for h in range(HALVES):
        line.gather_wait(2 + h, blocks_of(cot, h))
    for h in range(HALVES):
        line.scatter_drain(h, *parts_of(part, slots, 0, h))
        line.gather_drain(2 + h, blocks_of(cot, h))


def last_kernel(heads, d_proj, w_in, normed, mixer, mixer_cot, rows, grad, gain, *refs):
    smalls, refs = refs[: 5 * LAYERS + LAYERS - 1], refs[5 * LAYERS + LAYERS - 1 :]
    per_layer = [smalls[5 * l : 5 * l + 5] for l in range(LAYERS)]
    first_gains = smalls[5 * LAYERS :]
    (grad_out, summed, taps_out, norms_out,
     d_gain, grads, taps_land, line_land, norms_land,
     taps_send, taps_recv, line_send, line_recv, norms_send, norms_recv,
     part, slots, total, send_sem, recv_sem, *sum_refs) = refs
    line = Line(send_sem, recv_sem)
    sums = Sums(grads, *sum_refs)
    small_taps = Smalls("dp", taps_land, taps_send, taps_recv)
    small_line = Smalls("tensor", line_land, line_send, line_recv)
    small_norms = Smalls("dp", norms_land, norms_send, norms_recv)
    line.greet()
    others = sums.greet() + small_taps.greet() + small_line.greet()
    taps_land[small_taps.me] = jnp.zeros(taps_land.shape[1:], F32)
    line_land[line.me] = jnp.zeros(line_land.shape[1:], F32)
    for l, (d_qk, d_v, d_head, d_out_gain, second_gain) in enumerate(per_layer):
        top = TAP_ROWS * l
        seqs = d_qk.shape[0]
        for i in range(2):
            taps_land[small_taps.me, top + 4 * i : top + 4 * i + 4, : d_qk.shape[3]] = sum(d_qk[s, i] for s in range(seqs))
        taps_land[small_taps.me, top + 8 : top + 12, : d_v.shape[2]] = sum(d_v[s] for s in range(seqs))
        lane = iota((1, 128), 1)
        row = jnp.zeros((1, 128), F32)
        for kind in range(2):
            for h in range(heads):
                value = sum(d_head[s, h, kind : kind + 1, :] for s in range(seqs))
                row = row + jnp.where(lane == kind * heads + h, value, 0.0)
        taps_land[small_taps.me, top + 12 : top + 13, :128] = row
        line_land[line.me, 2 * l + 1 : 2 * l + 2, :] = second_gain[...]
        value = sum(d_out_gain[s, h] for s in range(seqs) for h in range(heads))
        line_land[line.me, 2 * LAYERS + l : 2 * LAYERS + l + 1, : value.shape[1]] = value
        if l > 0:
            line_land[line.me, 2 * l : 2 * l + 1, :] = first_gains[l - 1][...]
    partial_sums(half_of(d_proj, 0), w_in, part, 0, 0)
    line.meet(others)
    line.scatter_start(0, *parts_of(part, slots, 0, 0))
    small_taps.start()
    width = mixer.shape[3]
    pieces = [row_grads(mixer_cot, mixer, grads, 0), row_grads(normed, d_proj, grads, width)]
    run_pieces(pieces, 0, 1)
    sums.start(0)
    line.scatter_relay(0, *parts_of(part, slots, 0, 0))
    partial_sums(half_of(d_proj, 1), w_in, part, 0, 1)
    line.scatter_start(1, *parts_of(part, slots, 0, 1))
    for m in range(1, 4):
        run_pieces(pieces, m, m + 1)
        sums.start(m)
        sums.turn(m - 1)
    line.scatter_relay(1, *parts_of(part, slots, 0, 1))
    sums.turn(3)
    d_gain[...] = jnp.zeros_like(d_gain)
    for h in range(HALVES):
        both = parts_of(part, slots, 0, h)
        line.scatter_wait(h, *both)
        line.scatter_sum(total, *both)
        back, gain_part = rms_back(rows[h].astype(F32), gain[...], total[...])
        d_gain[...] += gain_part
        grad_out[h] = grad[h] + back
    line_land[line.me, 0:1, :] = d_gain[...]
    small_line.start()
    norms_land[small_norms.me] = small_line.finish()
    small_norms.start()
    taps_out[...] = small_taps.finish()
    for h in range(HALVES):
        line.scatter_drain(h, *parts_of(part, slots, 0, h))
    sums.finish(summed)
    norms_out[...] = small_norms.finish()


TAP_ROWS = 16
DMA = pltpu.SemaphoreType.DMA


def line_call(kernel, operands, outs, scratch, number, name, micros, spaces=None):
    return pl.pallas_call(
        kernel,
        in_specs=[pl.BlockSpec(memory_space=s) for s in spaces or [pltpu.VMEM] * len(operands)],
        out_specs=[pl.BlockSpec(memory_space=pltpu.VMEM)] * len(outs),
        out_shape=[jax.ShapeDtypeStruct(*out) for out in outs],
        scratch_shapes=scratch,
        compiler_params=pltpu.CompilerParams(
            collective_id=number, has_side_effects=True, vmem_limit_bytes=VMEM_LIMIT
        ),
        cost_estimate=cost(micros),
        name=name,
    )(*operands)


def line_scratch(sums, block, width, phases):
    return [
        pltpu.VMEM((sums, HALVES, 4, block, width), BF16),
        pltpu.VMEM((sums, HALVES, 5, block, width), BF16),
        pltpu.VMEM((block, width), F32),
        DMA((phases, 4)),
        DMA((phases, 5)),
    ]


def sums_scratch(shape):
    pairs, _, own, width = shape
    return [
        pltpu.VMEM((pairs, own, width), BF16), pltpu.VMEM((pairs, own, width), BF16),
        DMA((4,)), DMA((4,)), DMA((pairs,)), DMA((pairs,)),
    ]


def start_call(rows, cot, gain, in_weights, rest_weights, rest_units, dp):
    _, block, width = rows.shape
    in_places = cast_places(in_weights, (128,) * len(in_weights))
    rest_places = cast_places(rest_weights, rest_units)
    own = in_weights[0].shape[1]
    in_width, rest_width = (sum(p[2] for p in places) for places in (in_places, rest_places))
    whole = ((4, HALVES, block, width), BF16)
    outs = [whole, whole, ((dp, own, in_width), BF16)]
    outs += [((own, in_width), BF16), ((own, rest_width), BF16)] * (LAYERS - 1)
    half = dp // 2
    scratch = [pltpu.VMEM(held_shape(w), F32) for w in in_weights + rest_weights] + [
        DMA((len(in_weights),)), DMA((len(rest_weights),)),
        DMA((4, 4)), DMA((4, 5)), DMA((half,)), DMA((half,)), DMA((half,)), DMA((half,)),
    ]
    return line_call(
        functools.partial(start_kernel, in_places, rest_places),
        (rows, cot, gain, *[turn(w) for w in in_weights + rest_weights]), outs, scratch, 1, "start", 35,
        [pltpu.VMEM] * 3 + [pl.ANY] * len(in_weights + rest_weights),
    )


def ffn_forward_call(mixer, weights, rows, gain, gain_next, layer, last):
    _, block, width = rows.shape
    wide = (weights.shape[1] - mixer.shape[3]) // 3
    own, whole = ((HALVES, block, width), F32), ((4, HALVES, block, width), BF16)
    outs = [own, whole, ((4, HALVES, block, 2 * wide), F32), ((4, HALVES, block, wide), BF16), own]
    if not last:
        outs.append(whole)
    return line_call(
        functools.partial(ffn_forward_kernel, last), (mixer, weights, rows, gain, gain_next), outs,
        line_scratch(2, block, width, 8) + ([] if last else [pltpu.SemaphoreType.REGULAR]), 2 + layer, "ffn_forward", 65,
    )


def ffn_backward_call(cot, hidden, pre, normed, middle, grad, gain, weights, v_width, grads_shape, owed, layer):
    _, block, width = middle.shape
    wide = hidden.shape[3]
    whole = ((4, HALVES, block, width), BF16)
    outs = [
        ((4, HALVES, block, v_width), F32), (grads_shape + (3 * wide,), BF16), whole,
        ((HALVES, block, width), F32), ((1, width), F32),
    ]
    scratch = [pltpu.VMEM((4, HALVES, block, 2 * wide), BF16)] + line_scratch(1, block, width, 4)
    operands = [cot, hidden, pre, normed, middle, grad, gain, weights]
    if owed is not None:
        operands.append(owed)
        outs.append((owed.shape[2:], F32))
        scratch += sums_scratch(owed.shape) + [pltpu.SemaphoreType.REGULAR]
    return line_call(
        functools.partial(ffn_backward_kernel, owed is not None), operands, outs, scratch,
        4 + layer, "ffn_backward", 40,
    )


def mixer_backward_call(d_proj, w_in, normed, mixer, mixer_cot, rows, grad, gain, grads_shape, layer):
    _, block, width = rows.shape
    outs = [
        ((HALVES, block, width), F32), ((1, width), F32),
        (grads_shape + (mixer.shape[3] + w_in.shape[1],), BF16), ((4, HALVES, block, width), BF16),
    ]
    return line_call(
        mixer_backward_kernel, (d_proj, w_in, normed, mixer, mixer_cot, rows, grad, gain), outs,
        line_scratch(1, block, width, 4), 6 + layer, "mixer_backward", 40,
    )


def last_call(d_proj, w_in, normed, mixer, mixer_cot, rows, grad, gain, smalls, first_gains, grads_shape, heads):
    _, block, width = rows.shape
    dp = 2 * grads_shape[0]
    shape = grads_shape + (mixer.shape[3] + w_in.shape[1],)
    taps_width = max(smalls[0][0].shape[3], smalls[0][1].shape[2])
    taps_shape, norms_shape = (TAP_ROWS * LAYERS, taps_width), (8, width)
    outs = [((HALVES, block, width), F32), (shape[2:], F32), (taps_shape, F32), (norms_shape, F32)]
    scratch = [
        pltpu.VMEM((1, width), F32), pltpu.VMEM(shape, BF16), pltpu.VMEM((dp,) + taps_shape, F32),
        pltpu.VMEM((4,) + norms_shape, F32), pltpu.VMEM((dp,) + norms_shape, F32),
        DMA((dp,)), DMA((dp,)), DMA((4,)), DMA((4,)), DMA((dp,)), DMA((dp,)),
    ]
    flat = [array for layer in smalls for array in layer] + list(first_gains)
    return line_call(
        functools.partial(last_kernel, heads),
        (d_proj, w_in, normed, mixer, mixer_cot, rows, grad, gain, *flat), outs,
        scratch + line_scratch(1, block, width, 2) + sums_scratch(shape), 8, "last", 40,
    )


def finish_kernel(places, heads, *refs):
    sources, refs = refs[: 2 * LAYERS + 4], refs[2 * LAYERS + 4 :]
    rows, grad, taps, norms = sources[2 * LAYERS :]
    outs, refs = refs[: len(places) + 2], refs[len(places) + 2 :]
    (conv_qk, conv_v, head, norm_gains, out_gain), refs = refs[:5], refs[5:]
    held, sems = refs[:-1], refs[-1]
    copies = [
        pltpu.make_async_copy(rows, outs[len(places)], sems.at[len(places)]),
        pltpu.make_async_copy(grad, outs[len(places) + 1], sems.at[len(places) + 1]),
    ]
    for copy in copies:
        copy.start()
    for i, (kind, width, start, turned) in enumerate(places):
        for l in range(LAYERS):
            source = sources[kind * LAYERS + l]
            if turned:
                tall = -(-width // 128) * 128
                held[i][l] = jnp.transpose(source[:, start : start + tall].astype(F32))[:width]
            else:
                held[i][l] = source[:, start : start + width].astype(F32)
        copies.append(pltpu.make_async_copy(held[i], outs[i], sems.at[i]))
        copies[-1].start()
    for l in range(LAYERS):
        top = TAP_ROWS * l
        for i in range(2):
            conv_qk[l, i] = taps[top + 4 * i : top + 4 * i + 4, : conv_qk.shape[3]]
            head[l, i : i + 1, :] = taps[top + 12 : top + 13, i * heads : (i + 1) * heads]
            norm_gains[l, i : i + 1, :] = norms[2 * l + i : 2 * l + i + 1, :]
        conv_v[l] = taps[top + 8 : top + 12, : conv_v.shape[2]]
        out_gain[l : l + 1, :] = norms[2 * LAYERS + l : 2 * LAYERS + l + 1, : out_gain.shape[1]]
    for copy in copies:
        copy.wait()


def finish_call(mixer_grads, ffn_grads, rows, grad, taps, norms, places, like):
    operands = list(mixer_grads) + list(ffn_grads) + [rows, grad, taps, norms]
    own = mixer_grads[0].shape[0]
    heads = like[2].shape[2]
    full = [(LAYERS, own, width) for _, width, _ in places]
    turned = [is_turned(shape) for shape in full]
    shapes = [(s[0], s[2], s[1]) if t else s for s, t in zip(full, turned)]
    places = [p + (t,) for p, t in zip(places, turned)]
    count = len(places)
    outs = pl.pallas_call(
        functools.partial(finish_kernel, places, heads),
        in_specs=[pl.BlockSpec(memory_space=pltpu.VMEM)] * len(operands),
        out_specs=[pl.BlockSpec(memory_space=pl.ANY)] * (count + 2) + [pl.BlockSpec(memory_space=pltpu.VMEM)] * 5,
        out_shape=[jax.ShapeDtypeStruct(shape, F32) for shape in shapes + [rows.shape, grad.shape]]
        + [jax.ShapeDtypeStruct(array.shape, F32) for array in like],
        scratch_shapes=[pltpu.VMEM(shape, F32) for shape in shapes] + [DMA((count + 2,))],
        compiler_params=pltpu.CompilerParams(vmem_limit_bytes=VMEM_LIMIT),
        name="finish",
    )(*operands)
    weight_grads = [jnp.swapaxes(o, 1, 2) if t else o for o, t in zip(outs[:count], turned)]
    return outs[count], outs[count + 1], weight_grads, outs[count + 2 :]


CHUNK = 128
REFINE = 2


def body(
    tokens,
    segment_ids,
    query_weight,
    key_weight,
    value_weight,
    gate_weight,
    decay_weight,
    out_weight,
    swiglu_gate,
    swiglu_up,
    swiglu_down,
    conv_query_key,
    conv_value,
    head_params,
    norm_gains,
    out_gain,
    cotangent,
):
    seqs, length = segment_ids.shape
    heads = head_params.shape[2]
    qk_width, v_width, pair_width = query_weight.shape[2], value_weight.shape[2], decay_weight.shape[2]
    hidden_width = swiglu_gate.shape[2]
    hidden_pad = -(-hidden_width // 256) * 256
    local_rows, width = tokens.shape
    block = local_rows // HALVES
    total_rows = 4 * local_rows
    tables = segment_tables(segment_ids, CHUNK)

    def gathered(matrix):
        return lax.all_gather(matrix, "dp", axis=0, tiled=True)

    def reduced(matrix):
        return lax.psum_scatter(matrix, "dp", scatter_dimension=0, tiled=True)

    in_weights = (query_weight, key_weight, value_weight, gate_weight, decay_weight)
    rest_weights = (out_weight, swiglu_gate, swiglu_up, swiglu_down)
    rest_units = (128, 256, 256, 256)

    def split_rows(matrix):
        return matrix.reshape(HALVES, block, matrix.shape[1])

    def split_all(matrix):
        return matrix.reshape(4, HALVES, block, matrix.shape[1])

    def merged(array):
        return array.reshape(total_rows, array.shape[3])

    def gain_of(l, i):
        return norm_gains[l, i][None]

    dp = lax.axis_size("dp")
    rows = split_rows(tokens)
    cot_rows = split_rows(cotangent)
    w_rest = [gathered(cast_call(rest_weights, rest_units, 0))]
    normed, cot, w_in, *low = start_call(rows, cot_rows, gain_of(0, 0), in_weights, rest_weights, rest_units, dp)
    w_in = [w_in.reshape(width, w_in.shape[2])] + [gathered(part) for part in low[::2]]
    w_rest += [gathered(part) for part in low[1::2]]
    kept = []
    for l in range(LAYERS):
        last = l == LAYERS - 1
        proj = jnp.dot(merged(normed), w_in[l], preferred_element_type=F32)
        small = (conv_query_key[l], conv_value[l], head_params[l], out_gain[l][None])
        mixer, *saved = delta_forward(proj, *small, tables, seqs, heads, CHUNK, REFINE)
        mixer = split_all(mixer)
        gain_next = gain_of(min(l + 1, LAYERS - 1), 0)
        middle, normed_ffn, pre, hidden, out_rows, *following = ffn_forward_call(
            mixer, w_rest[l], rows, gain_of(l, 1), gain_next, l, last
        )
        kept.append((rows, normed, proj, small, mixer, saved, middle, normed_ffn, pre, hidden))
        rows = out_rows
        if not last:
            normed = following[0]
    output = rows
    grad = cot_rows
    grads_shape = (dp // 2, 2, width // dp)
    ffn_grads, mixer_grads, smalls, first_gains = ([None] * LAYERS for _ in range(4))
    owed = None
    for l in reversed(range(LAYERS)):
        rows, normed, proj, small, mixer, saved, middle, normed_ffn, pre, hidden = kept[l]
        d_mixer, ffn_grad, mixer_cot, grad, second_gain, *summed = ffn_backward_call(
            cot, hidden, pre, normed_ffn, middle, grad, gain_of(l, 1), w_rest[l], v_width, grads_shape, owed, l
        )
        if summed:
            mixer_grads[l + 1] = summed[0]
        ffn_grads[l] = reduced(ffn_grad.reshape(width, 3 * hidden_pad))
        if l < LAYERS - 1:
            d_mixer, ffn_grads[l + 1] = lax.optimization_barrier((d_mixer, ffn_grads[l + 1]))
        d_proj, d_qk, d_v, d_head, d_gain = delta_backward(
            proj, *small, tables, saved, merged(d_mixer), seqs, heads, CHUNK
        )
        smalls[l] = (d_qk, d_v, d_head, d_gain, second_gain)
        d_proj = split_all(d_proj)
        if l > 0:
            grad, first_gains[l], owed, cot = mixer_backward_call(
                d_proj, w_in[l], normed, mixer, mixer_cot, rows, grad, gain_of(l, 0), grads_shape, l
            )
    grad, mixer_grads[0], taps, norms = last_call(
        d_proj, w_in[0], normed, mixer, mixer_cot, rows, grad, gain_of(0, 0), smalls, first_gains[1:], grads_shape, heads
    )
    output, grad, weight_grads, others = finish_call(
        mixer_grads, ffn_grads, output, grad, taps, norms,
        [(0, qk_width, v_width), (0, qk_width, v_width + qk_width), (0, v_width, v_width + 2 * qk_width),
         (0, v_width, 2 * v_width + 2 * qk_width), (0, pair_width, 3 * v_width + 2 * qk_width), (0, v_width, 0),
         (1, hidden_width, hidden_pad), (1, hidden_width, 2 * hidden_pad), (1, hidden_width, 0)],
        (conv_query_key, conv_value, head_params, norm_gains, out_gain),
    )
    return (output.reshape(local_rows, width), grad.reshape(local_rows, width), *weight_grads, *others)


def solution(mesh):
    rows = P(("dp", "tensor"), None)
    weight = P(None, "dp", "tensor")
    small = (P(None, None, None, "tensor"), P(None, None, "tensor"), P(None, None, "tensor"), P(), P())
    return jax.shard_map(
        body,
        mesh=mesh,
        in_specs=(rows, P("dp", None)) + (weight,) * 9 + small + (rows,),
        out_specs=(rows, rows) + (weight,) * 9 + small,
        check_vma=False,
    )
```

```python
import functools
import jax
import jax.numpy as jnp
from jax import lax
from jax.experimental import pallas as pl
from jax.experimental.pallas import tpu as pltpu
from jax.sharding import PartitionSpec as P

F32 = jnp.float32
BF16 = jnp.bfloat16
NN = (((1,), (0,)), ((), ()))
NT = (((1,), (1,)), ((), ()))
TN = (((0,), (0,)), ((), ()))
EPS = 1e-6
FLOOR = 0.01


def cost(micros):
    return pl.CostEstimate(flops=0, bytes_accessed=int(micros * 3.5e6), transcendentals=0)


def split(x):
    high = x.astype(BF16)
    return high, (x - high.astype(F32)).astype(BF16)


def mm(a, b, dims, passes=3):
    def one(p, q):
        return lax.dot_general(p, q, dims, preferred_element_type=F32)

    if passes == 1:
        return one(a.astype(BF16), b.astype(BF16))
    ah, al = split(a)
    bh, bl = split(b)
    return one(ah, bh) + (one(ah, bl) + one(al, bh))


def iota(shape, axis):
    return lax.broadcasted_iota(jnp.int32, shape, axis)


def shifted_rows(x, by):
    return pltpu.roll(x, by % x.shape[0], 0) if by else x


def conv(signal, taps, masks):
    total = signal * taps[0:1]
    for j in range(1, 4):
        total = total + shifted_rows(signal, j) * masks[j - 1] * taps[j : j + 1]
    return total


def chunk_scan(row, chunk, backward=False):
    length = row.shape[1]
    place = iota(row.shape, 1) % chunk
    step = 1
    while step < chunk:
        if backward:
            moved = pltpu.roll(row, length - step, 1)
            row = row + jnp.where(place < chunk - step, moved, 0.0)
        else:
            moved = pltpu.roll(row, step, 1)
            row = row + jnp.where(place >= step, moved, 0.0)
        step *= 2
    return row


def unit_lower_inverse(lower, refine):
    size = lower[0].shape[0]
    rows, cols = iota((size, size), 0), iota((size, size), 1)
    eye = (rows == cols).astype(F32)

    def off(block):
        return ((rows // (2 * block) == cols // (2 * block)) & (rows // block != cols // block)).astype(F32)

    found = [eye - part * off(1) for part in lower]
    block = 2
    while block < size:
        mask = off(block)
        half = [mm(x, part * mask, NN, 1) for x, part in zip(found, lower)]
        found = [x - mm(t, x, NN, 1) for x, t in zip(found, half)]
        block *= 2
    for _ in range(refine):
        rest = [(x - eye) + mm(part, x, NN) for x, part in zip(found, lower)]
        found = [x - mm(x, r, NN, 1) for x, r in zip(found, rest)]
    return found


def prepared(head, chunk, qref, kref, vref, pair_ref, tap_qk, tap_v, head_table, col_info, row_info):
    length, dk = qref.shape
    masks = [col_info[:, j : j + 1] for j in range(3)]
    masks = [jnp.broadcast_to(m, (length, dk)) for m in masks]
    dv = vref.shape[1]
    wide = [jnp.concatenate([m] * (dv // dk), axis=1) for m in masks]
    pre_q = conv(qref[...], tap_qk[0], masks)
    pre_k = conv(kref[...], tap_qk[1], masks)
    pre_v = conv(vref[...], tap_v[...], wide)
    out = dict(masks=masks, wide=wide, pre_q=pre_q, pre_k=pre_k, pre_v=pre_v)
    for name, pre in (("q", pre_q), ("k", pre_k), ("v", pre_v)):
        sig = lax.logistic(pre)
        out["sig_" + name] = sig
        out["act_" + name] = pre * sig
    out["inv_q"] = lax.rsqrt(jnp.sum(out["act_q"] ** 2, axis=1, keepdims=True) + EPS)
    out["inv_k"] = lax.rsqrt(jnp.sum(out["act_k"] ** 2, axis=1, keepdims=True) + EPS)
    out["q"] = out["act_q"] * out["inv_q"] * dk ** (-0.5)
    out["k"] = out["act_k"] * out["inv_k"]
    out["v"] = out["act_v"]
    picked = (iota((8, 128), 1) == 2 * head + iota((8, 128), 0)).astype(BF16)
    pair = jnp.zeros((8, length), F32)
    rest = pair_ref[...]
    for _ in range(3):
        high = rest.astype(BF16)
        rest = rest - high.astype(F32)
        pair = pair + lax.dot_general(picked, high, NT, preferred_element_type=F32)
    a_row, b_row = pair[0:1], pair[1:2]
    rate = jnp.exp(jnp.full((1, length), head_table[0, head], F32))
    a_row = a_row + head_table[1, head]
    softplus = jnp.maximum(a_row, 0.0) + jnp.log1p(jnp.exp(-jnp.abs(a_row)))
    decay = -rate * softplus
    beta = lax.logistic(b_row)
    total = chunk_scan(decay, chunk)
    entry = jnp.exp(total) * row_info[0:1]
    chunks = length // chunk
    place = iota((1, length), 1)
    ends = [total[:, (i + 1) * chunk - 1 : (i + 1) * chunk] for i in range(chunks)]
    last = ends[0]
    for i in range(1, chunks):
        last = jnp.where(place >= i * chunk, ends[i], jnp.broadcast_to(last, (1, length)))
    tail = jnp.exp(last - total) * row_info[1:2]
    rows = jnp.concatenate([beta, total, entry, tail, a_row, decay, jnp.zeros((2, length), F32)], axis=0)
    cols = jnp.transpose(rows)
    out.update(rows=rows, cols=cols)
    out.update(named_parts(rows, cols))
    return out


def named_parts(rows, cols):
    return dict(
        total_row=rows[1:2], entry_row=rows[2:3],
        beta=cols[:, 0:1], total=cols[:, 1:2], entry=cols[:, 2:3], tail=cols[:, 3:4],
    )


def chunk_parts(pre, i, chunk, col_info, row_info):
    s = slice(i * chunk, (i + 1) * chunk)
    q, k, v = pre["q"][s], pre["k"][s], pre["v"][s]
    beta, total, entry, tail = pre["beta"][s], pre["total"][s], pre["entry"][s], pre["tail"][s]
    rows, cols = iota((chunk, chunk), 0), iota((chunk, chunk), 1)
    allowed = (col_info[s, 3:4] == row_info[2:3, s]) & (rows >= cols)
    fading = jnp.where(allowed, jnp.exp(jnp.where(allowed, total - pre["total_row"][:, s], 0.0)), 0.0)
    both = mm(jnp.concatenate([q, k], axis=0), k, NT)
    strict_fading = jnp.where(rows > cols, fading, 0.0)
    qk, kk = both[:chunk], both[chunk:]
    return dict(
        q=q, k=k, v=v, beta=beta, entry=entry, tail=tail, fading=fading, strict=strict_fading,
        mixed=qk * fading, kk_faded=kk * strict_fading, lower=beta * (kk * strict_fading),
        exit=pre["entry_row"][:, (i + 1) * chunk - 1 : (i + 1) * chunk], rows=s,
    )


def silu_grad(pre, sig):
    return sig * (1.0 + pre * (1.0 - sig))


def forward_kernel(
    chunk, refine, qref, kref, vref, gref, pair_ref, tap_qk, tap_v, head_table, gain, col_ref, row_ref,
    mix_ref, rec_ref, fix_ref, inv_ref, state_ref, act_ref, slope_ref, cols_ref, rows_ref,
):
    head = pl.program_id(1)
    col_info, row_info = col_ref[0], row_ref[0]
    pre = prepared(head, chunk, qref, kref, vref, pair_ref, tap_qk, tap_v, head_table, col_info, row_info)
    length, dk = qref.shape
    dv = vref.shape[1]
    for name, start, width in (("q", 0, dk), ("k", dk, dk), ("v", 2 * dk, dv)):
        act_ref[:, start : start + width] = pre[name]
        slope_ref[:, start : start + width] = silu_grad(pre["pre_" + name], pre["sig_" + name]).astype(BF16)
    cols_ref[0, 0] = pre["cols"]
    cols_ref[0, 0, :, 4:5] = pre["inv_q"]
    cols_ref[0, 0, :, 5:6] = pre["inv_k"]
    rows_ref[0, 0] = pre["rows"]
    chunks = length // chunk
    parts = [chunk_parts(pre, i, chunk, col_info, row_info) for i in range(chunks)]
    inverses = unit_lower_inverse([p["lower"] for p in parts], refine)
    state = jnp.zeros((dk, dv), F32)
    steps = []
    for p, inverse in zip(parts, inverses):
        target = jnp.concatenate([p["beta"] * p["entry"] * p["k"], p["beta"] * p["v"]], axis=1)
        solved = mm(inverse, target, NN)
        pushed = mm(p["k"] * p["tail"], solved, TN)
        steps.append((solved, pushed))
    states = []
    for p, (solved, pushed) in zip(parts, steps):
        states.append(state)
        state = p["exit"] * state - mm(pushed[:, :dk], state, NN) + pushed[:, dk:]
    gain_row = gain[...]
    for i, (p, inverse, (solved, pushed)) in enumerate(zip(parts, inverses, steps)):
        seen = mm(jnp.concatenate([solved[:, :dk], p["q"] * p["entry"]], axis=0), states[i], NN)
        fixed = solved[:, dk:] - seen[:chunk]
        rec = seen[chunk:] + mm(p["mixed"], fixed, NN)
        s = p["rows"]
        rec_ref[s, :] = rec
        fix_ref[s, :] = fixed
        inv_ref[0, 0, i] = inverse
        state_ref[0, 0, i] = states[i]
        normal = rec * lax.rsqrt(jnp.mean(rec * rec, axis=1, keepdims=True) + FLOOR)
        gate = gref[s, :]
        mix_ref[s, :] = (normal * gain_row * (gate * lax.logistic(gate))).astype(BF16)


def backward_kernel(
    chunk, heads, qref, kref, vref, gref, pair_ref, tap_qk, tap_v, head_table, gain, col_ref, row_ref,
    rec_ref, fix_ref, inv_ref, state_ref, act_ref, slope_ref, cols_ref, rows_ref, dmix_ref,
    dproj_ref, dtap_qk, dtap_v, dhead_ref, dgain_ref,
):
    seq, head = pl.program_id(0), pl.program_id(1)
    col_info, row_info = col_ref[0], row_ref[0]
    length, dk = qref.shape
    dv = vref.shape[1]
    rows, cols = rows_ref[0, 0], cols_ref[0, 0]
    pre = dict(q=act_ref[:, :dk], k=act_ref[:, dk : 2 * dk], v=act_ref[:, 2 * dk :], **named_parts(rows, cols))
    rate = jnp.exp(jnp.full((1, length), head_table[0, head], F32))
    masks = [jnp.broadcast_to(col_info[:, j : j + 1], (length, dk)) for j in range(3)]
    wide = [jnp.concatenate([m] * (dv // dk), axis=1) for m in masks]
    chunks = length // chunk
    parts = [chunk_parts(pre, i, chunk, col_info, row_info) for i in range(chunks)]
    gain_row = gain[...]
    dgain = jnp.zeros((1, dv), F32)
    v_at = 2 * heads * dk
    g_at = v_at + heads * dv
    p_at = g_at + heads * dv
    for p in parts:
        s = p["rows"]
        rec, gate, dmix = rec_ref[s, :], gref[s, :], dmix_ref[s, :]
        scale = lax.rsqrt(jnp.mean(rec * rec, axis=1, keepdims=True) + FLOOR)
        sig = lax.logistic(gate)
        gated = dmix * (gate * sig)
        normal = rec * scale
        dgain = dgain + jnp.sum(gated * normal, axis=0, keepdims=True)
        dgate = dmix * normal * gain_row * silu_grad(gate, sig)
        dproj_ref[s, pl.ds(pl.multiple_of(g_at + head * dv, dv), dv)] = dgate.astype(BF16)
        dn = gated * gain_row
        p["drec"] = scale * dn - rec * (scale * scale * scale) * jnp.mean(dn * rec, axis=1, keepdims=True)
    for i, p in enumerate(parts):
        inverse = inv_ref[0, 0, i]
        p["inverse"] = inverse
        solved = mm(inverse, p["beta"] * p["entry"] * p["k"], NN)
        back = mm(p["mixed"], p["drec"], TN)
        p["back"] = back
        ahead = mm(solved, p["k"] * p["tail"], TN)
        given = mm(
            jnp.concatenate([p["q"] * p["entry"], -solved], axis=0),
            jnp.concatenate([p["drec"], back], axis=0), TN,
        )
        p["ahead"], p["given"] = ahead, given
    dstate = jnp.zeros((dk, dv), F32)
    for p in reversed(parts):
        p["dstate"] = dstate
        dstate = p["exit"] * dstate - mm(p["ahead"], dstate, NN) + p["given"]
    lane = iota((chunk, 8), 1)
    col_parts, row_parts, dqs, dks, dvs = [], [], [], [], []
    for i, p in enumerate(parts):
        s = p["rows"]
        state, dstate, fixed, drec = state_ref[0, 0, i], p["dstate"], fix_ref[s, :], p["drec"]
        q, k, v, beta, entry, tail = p["q"], p["k"], p["v"], p["beta"], p["entry"], p["tail"]
        dfixed = p["back"] + mm(k * tail, dstate, NN)
        dtarget = mm(p["inverse"], dfixed, TN)
        outer = mm(
            jnp.concatenate([drec, dtarget], axis=0), jnp.concatenate([state, fixed], axis=0), NT
        )
        drec_state, dtarget_state = outer[:chunk, :dk], outer[chunk:, :dk]
        dmixed, dlower = outer[:chunk, dk:], -outer[chunk:, dk:]
        fixed_dstate = mm(fixed, dstate, NT)
        g1 = dmixed * p["fading"]
        g2 = (beta * dlower) * p["strict"]
        stacked = jnp.concatenate([g1, g2], axis=0)
        first = mm(stacked, k, NN)
        second = mm(stacked, jnp.concatenate([q, k], axis=0), TN)
        key_state = jnp.sum(dtarget_state * k, axis=1, keepdims=True)
        dqs.append(entry * drec_state + first[:chunk])
        dks.append(first[chunk:] + second + tail * fixed_dstate - (beta * entry) * dtarget_state)
        dvs.append(beta * dtarget)
        dentry = jnp.sum(drec_state * q, axis=1, keepdims=True) - beta * key_state
        dtail = jnp.sum(fixed_dstate * k, axis=1, keepdims=True) * tail
        high = dmixed * p["mixed"] + dlower * p["lower"]
        dbeta = (
            jnp.sum(dtarget * v, axis=1, keepdims=True)
            - entry * key_state
            + jnp.sum(dlower * p["kk_faded"], axis=1, keepdims=True)
        )
        dtotal = jnp.sum(high, axis=1, keepdims=True) + dentry * entry - dtail
        end = p["exit"] * jnp.sum(jnp.sum(dstate * state, axis=1, keepdims=True), axis=0, keepdims=True)
        end = end + jnp.sum(dtail, axis=0, keepdims=True)
        dtotal = dtotal + jnp.where(iota((chunk, 1), 0) == chunk - 1, end, 0.0)
        row_parts.append(jnp.sum(high, axis=0, keepdims=True))
        col_parts.append(jnp.where(lane == 0, dtotal, jnp.where(lane == 1, dbeta, 0.0)))
    turned = jnp.transpose(jnp.concatenate(col_parts, axis=0))
    dtotal_row = turned[0:1] - jnp.concatenate(row_parts, axis=1)
    dbeta_row = turned[1:2]
    ddecay = chunk_scan(dtotal_row, chunk, backward=True)
    da = -ddecay * rate * lax.logistic(rows[4:5])
    db = dbeta_row * rows[0:1] * (1.0 - rows[0:1])
    which = iota((8, length), 0)
    both = jnp.transpose(jnp.where(which == 0, da, jnp.where(which == 1, db, 0.0)))
    spread = iota((length, 128), 1)
    dpair = jnp.where(spread == 2 * head, both[:, 0:1], jnp.where(spread == 2 * head + 1, both[:, 1:2], 0.0)).astype(BF16)

    @pl.when(head == 0)
    def _():
        dproj_ref[:, p_at:] = dpair

    @pl.when(head != 0)
    def _():
        dproj_ref[:, p_at:] = dproj_ref[:, p_at:] + dpair

    dscale = jnp.sum(ddecay * rows[5:6], axis=1, keepdims=True)
    dbias = jnp.sum(da, axis=1, keepdims=True)
    which = iota((8, 128), 0)
    dhead = jnp.where(which == 0, dscale, jnp.where(which == 1, dbias, 0.0))
    dq, dk_all, dv_all = (jnp.concatenate(x, axis=0) for x in (dqs, dks, dvs))

    def through_norm(grad, unit, inv, factor):
        along = jnp.sum(grad * unit, axis=1, keepdims=True) * factor ** (-2)
        return (factor * inv) * (grad - unit * along)

    dq = through_norm(dq, pre["q"], cols[:, 4:5], dk ** (-0.5))
    dk_all = through_norm(dk_all, pre["k"], cols[:, 5:6], 1.0)
    taps_out = []
    for grad, where, src, taps, kept, at in (
        (dq, 0, qref, tap_qk[0], masks, head * dk),
        (dk_all, dk, kref, tap_qk[1], masks, heads * dk + head * dk),
        (dv_all, 2 * dk, vref, tap_v[...], wide, v_at + head * dv),
    ):
        dpre = grad * slope_ref[:, where : where + grad.shape[1]].astype(F32)
        signal = src[...]
        dsignal = dpre * taps[0:1]
        dtaps = [jnp.sum(dpre * signal, axis=0, keepdims=True)]
        for j in range(1, 4):
            masked = dpre * kept[j - 1]
            dsignal = dsignal + shifted_rows(masked, -j) * taps[j : j + 1]
            dtaps.append(jnp.sum(masked * shifted_rows(signal, j), axis=0, keepdims=True))
        width = grad.shape[1]
        dproj_ref[:, pl.ds(pl.multiple_of(at, width), width)] = dsignal.astype(BF16)
        taps_out.append(jnp.concatenate(dtaps, axis=0))
    dtap_qk[0, 0] = taps_out[0]
    dtap_qk[0, 1] = taps_out[1]
    dtap_v[0] = taps_out[2]
    dhead_ref[0, 0] = dhead
    dgain_ref[0, 0] = dgain


def specs(length, heads, dk, dv):
    v_block = 2 * heads * dk // dv
    return [
        pl.BlockSpec((length, dk), lambda s, h: (s, h)),
        pl.BlockSpec((length, dk), lambda s, h: (s, heads + h)),
        pl.BlockSpec((length, dv), lambda s, h: (s, v_block + h)),
        pl.BlockSpec((length, dv), lambda s, h: (s, v_block + heads + h)),
        pl.BlockSpec((length, 128), lambda s, h: (s, (2 * heads * dk + 2 * heads * dv) // 128)),
        pl.BlockSpec((2, 4, dk), lambda s, h: (0, 0, h)),
        pl.BlockSpec((4, dv), lambda s, h: (0, h)),
        pl.BlockSpec(memory_space=pltpu.SMEM),
        pl.BlockSpec((1, dv), lambda s, h: (0, 0)),
        pl.BlockSpec((1, length, 8), lambda s, h: (s, 0, 0)),
        pl.BlockSpec((1, 8, length), lambda s, h: (s, 0, 0)),
    ]


def delta_forward(proj, taps_qk, taps_v, head_table, gain, tables, seqs, heads, chunk, refine):
    cols, rows = tables
    length = cols.shape[1]
    dk, dv = taps_qk.shape[2] // heads, taps_v.shape[1] // heads
    chunks = length // chunk
    tokens = seqs * length
    column = pl.BlockSpec((length, dv), lambda s, h: (s, h))
    return pl.pallas_call(
        functools.partial(forward_kernel, chunk, refine),
        grid=(seqs, heads),
        in_specs=specs(length, heads, dk, dv),
        out_specs=[
            column, column, column,
            pl.BlockSpec((1, 1, chunks, chunk, chunk), lambda s, h: (s, h, 0, 0, 0)),
            pl.BlockSpec((1, 1, chunks, dk, dv), lambda s, h: (s, h, 0, 0, 0)),
            pl.BlockSpec((length, 2 * dk + dv), lambda s, h: (s, h)),
            pl.BlockSpec((length, 2 * dk + dv), lambda s, h: (s, h)),
            pl.BlockSpec((1, 1, length, 8), lambda s, h: (s, h, 0, 0)),
            pl.BlockSpec((1, 1, 8, length), lambda s, h: (s, h, 0, 0)),
        ],
        out_shape=[
            jax.ShapeDtypeStruct((tokens, heads * dv), BF16),
            pltpu.HBM((tokens, heads * dv), F32),
            pltpu.HBM((tokens, heads * dv), F32),
            pltpu.HBM((seqs, heads, chunks, chunk, chunk), F32),
            pltpu.HBM((seqs, heads, chunks, dk, dv), F32),
            pltpu.HBM((tokens, heads * (2 * dk + dv)), F32),
            pltpu.HBM((tokens, heads * (2 * dk + dv)), BF16),
            pltpu.HBM((seqs, heads, length, 8), F32),
            pltpu.HBM((seqs, heads, 8, length), F32),
        ],
        compiler_params=pltpu.CompilerParams(vmem_limit_bytes=48 * 2**20),
        cost_estimate=cost(15),
        name="delta_forward",
    )(proj, proj, proj, proj, proj, taps_qk, taps_v, head_table, gain, cols, rows)


def delta_backward(proj, taps_qk, taps_v, head_table, gain, tables, saved, dmix, seqs, heads, chunk):
    cols, rows = tables
    length = cols.shape[1]
    dk, dv = taps_qk.shape[2] // heads, taps_v.shape[1] // heads
    chunks = length // chunk
    tokens = seqs * length
    width = proj.shape[1]
    column = pl.BlockSpec((length, dv), lambda s, h: (s, h))
    return pl.pallas_call(
        functools.partial(backward_kernel, chunk, heads),
        grid=(seqs, heads),
        in_specs=specs(length, heads, dk, dv)
        + [
            column, column,
            pl.BlockSpec((1, 1, chunks, chunk, chunk), lambda s, h: (s, h, 0, 0, 0)),
            pl.BlockSpec((1, 1, chunks, dk, dv), lambda s, h: (s, h, 0, 0, 0)),
            pl.BlockSpec((length, 2 * dk + dv), lambda s, h: (s, h)),
            pl.BlockSpec((length, 2 * dk + dv), lambda s, h: (s, h)),
            pl.BlockSpec((1, 1, length, 8), lambda s, h: (s, h, 0, 0)),
            pl.BlockSpec((1, 1, 8, length), lambda s, h: (s, h, 0, 0)),
            column,
        ],
        out_specs=[
            pl.BlockSpec((length, width), lambda s, h: (s, 0)),
            pl.BlockSpec((1, 2, 4, dk), lambda s, h: (s, 0, 0, h)),
            pl.BlockSpec((1, 4, dv), lambda s, h: (s, 0, h)),
            pl.BlockSpec((1, 1, 8, 128), lambda s, h: (s, h, 0, 0)),
            pl.BlockSpec((1, 1, 1, dv), lambda s, h: (s, h, 0, 0)),
        ],
        out_shape=[
            jax.ShapeDtypeStruct((tokens, width), BF16),
            jax.ShapeDtypeStruct((seqs, 2, 4, heads * dk), F32),
            jax.ShapeDtypeStruct((seqs, 4, heads * dv), F32),
            jax.ShapeDtypeStruct((seqs, heads, 8, 128), F32),
            jax.ShapeDtypeStruct((seqs, heads, 1, dv), F32),
        ],
        compiler_params=pltpu.CompilerParams(vmem_limit_bytes=56 * 2**20),
        cost_estimate=cost(25),
        name="delta_backward",
    )(proj, proj, proj, proj, proj, taps_qk, taps_v, head_table, gain, cols, rows, *saved, dmix)


MESH = pl.DeviceIdType.MESH
VMEM_LIMIT = 58 * 2**20
HALVES = 2
LAYERS = 2


class Line:
    def __init__(self, send_sem, recv_sem):
        self.send_sem, self.recv_sem = send_sem, recv_sem
        self.me = lax.axis_index("tensor")

    def greet(self):
        barrier = pltpu.get_barrier_semaphore()
        for m in range(4):
            @pl.when(self.me == m)
            def _():
                for t in range(4):
                    if t != m and {t, m} != {0, 3}:
                        pl.semaphore_signal(barrier, inc=1, device_id={"tensor": t}, device_id_type=MESH)

    def meet(self, others=0):
        barrier = pltpu.get_barrier_semaphore()
        for m in range(4):
            @pl.when(self.me == m)
            def _():
                pl.semaphore_wait(barrier, others + (2 if m in (0, 3) else 3))

    def copy(self, phase, source, target, to, send_at, recv_at):
        return pltpu.make_async_remote_copy(
            src_ref=source, dst_ref=target, send_sem=self.send_sem.at[phase, send_at],
            recv_sem=self.recv_sem.at[phase, recv_at], device_id={"tensor": to}, device_id_type=MESH,
        )

    def gather_start(self, phase, blocks):
        for m in range(4):
            @pl.when(self.me == m)
            def _():
                for t in range(4):
                    if t != m and {t, m} != {0, 3}:
                        self.copy(phase, blocks[m], blocks[m], t, t, m).start()

    def gather_forward(self, phase, blocks):
        for m in (1, 2):
            @pl.when(self.me == m)
            def _():
                far, to = (3, 0) if m == 1 else (0, 3)
                self.copy(phase, blocks[far], blocks[far], to, m, far).wait_recv()
                self.copy(phase, blocks[far], blocks[far], to, m, far).start()

    def gather_wait(self, phase, blocks):
        for m in range(4):
            @pl.when(self.me == m)
            def _():
                for b in range(4):
                    if b != m and not (m in (1, 2) and b == (3 if m == 1 else 0)):
                        self.copy(phase, blocks[b], blocks[b], b, b, b).wait_recv()

    def gather_drain(self, phase, blocks):
        for m in range(4):
            @pl.when(self.me == m)
            def _():
                for t in range(4):
                    if t != m and {t, m} != {0, 3}:
                        self.copy(phase, blocks[m], blocks[m], t, t, m).wait_send()
                if m in (1, 2):
                    far, to = (3, 0) if m == 1 else (0, 3)
                    self.copy(phase, blocks[far], blocks[far], to, m, far).wait_send()

    def scatter_start(self, phase, parts, slots):
        for m in range(4):
            @pl.when(self.me == m)
            def _():
                if m in (0, 3):
                    through = 1 if m == 0 else 2
                    self.copy(phase, parts[3 - m], slots[4], through, 3 - m, 4).start()
                for t in range(4):
                    if t != m and {t, m} != {0, 3}:
                        if not (m in (1, 2) and t == (3 if m == 1 else 0)):
                            self.copy(phase, parts[t], slots[m], t, t, m).start()

    def scatter_relay(self, phase, parts, slots):
        for m in (1, 2):
            @pl.when(self.me == m)
            def _():
                t = 3 if m == 1 else 0
                self.copy(phase, parts[t], slots[4], t, t, 4).wait_recv()
                parts[t][...] = (parts[t][...].astype(F32) + slots[4][...].astype(F32)).astype(BF16)
                self.copy(phase, parts[t], slots[m], t, t, m).start()

    def scatter_wait(self, phase, parts, slots):
        for m in range(4):
            @pl.when(self.me == m)
            def _():
                for s in range(4):
                    if s != m and {s, m} != {0, 3}:
                        self.copy(phase, parts[s], slots[s], s, s, s).wait_recv()

    def scatter_sum(self, total, parts, slots):
        for m in range(4):
            @pl.when(self.me == m)
            def _():
                value = parts[m][...].astype(F32)
                for s in range(4):
                    if s != m and {s, m} != {0, 3}:
                        value = value + slots[s][...].astype(F32)
                total[...] = value

    def scatter_drain(self, phase, parts, slots):
        for m in range(4):
            @pl.when(self.me == m)
            def _():
                for t in range(4):
                    if t != m:
                        self.copy(phase, parts[t], slots[m], t, t, m).wait_send()


TURN_AT = 1


class Turns:
    def __init__(self, gate):
        self.gate = gate
        self.me = lax.axis_index("dp")
        self.second = lax.rem(self.me, 2)
        self.sibling = self.me + 1 - 2 * self.second

    def greet(self):
        pl.semaphore_signal(
            pltpu.get_barrier_semaphore(), inc=1, device_id={"dp": self.sibling}, device_id_type=MESH
        )

    def wait(self):
        @pl.when(self.second == 1)
        def _():
            pl.semaphore_wait(self.gate, 1)

    def give(self):
        @pl.when(self.second == 0)
        def _():
            pl.semaphore_signal(self.gate, inc=1, device_id={"dp": self.sibling}, device_id_type=MESH)


class Sums:
    def __init__(self, source, near, far, near_send, near_recv, far_send, far_recv):
        self.source, self.near, self.far = source, near, far
        self.near_send, self.near_recv, self.far_send, self.far_recv = near_send, near_recv, far_send, far_recv
        self.pairs = source.shape[0]
        self.group = self.pairs // 4
        me = lax.axis_index("dp")
        self.parity, self.mine = lax.rem(me, 2), lax.div(me, 2)

    def greet(self):
        barrier = pltpu.get_barrier_semaphore()
        sibling = 2 * self.mine + 1 - self.parity
        pl.semaphore_signal(barrier, inc=1, device_id={"dp": sibling}, device_id_type=MESH)

        def signal(i, carry):
            other = 2 * lax.rem(self.mine + i, self.pairs) + self.parity
            pl.semaphore_signal(barrier, inc=1, device_id={"dp": other}, device_id_type=MESH)
            return carry

        lax.fori_loop(1, self.pairs, signal, 0)
        return self.pairs

    def greet_late(self, gate):
        self.gate = gate
        barrier = pltpu.get_barrier_semaphore()
        sibling = 2 * self.mine + 1 - self.parity

        @pl.when(self.parity == 0)
        def _():
            pl.semaphore_signal(barrier, inc=1, device_id={"dp": sibling}, device_id_type=MESH)

        def signal(i, carry):
            other = 2 * lax.rem(self.mine + i, self.pairs) + self.parity
            pl.semaphore_signal(barrier, inc=1, device_id={"dp": other}, device_id_type=MESH)
            return carry

        lax.fori_loop(1, self.pairs, signal, 0)

    def meet_late(self, line):
        @pl.when(self.parity == 0)
        def _():
            line.meet(self.pairs - 1)

        @pl.when(self.parity == 1)
        def _():
            line.meet(self.pairs)
            pl.semaphore_signal(self.gate, inc=1, device_id={"dp": 2 * self.mine}, device_id_type=MESH)
            for m in range(4):
                self.start(m)

    def start_late(self):
        @pl.when(self.parity == 0)
        def _():
            pl.semaphore_wait(self.gate, 1)
            for m in range(4):
                self.start(m)

    def near_copy(self, m):
        span = pl.ds(m * self.group, self.group)
        return pltpu.make_async_remote_copy(
            src_ref=self.source.at[span, 1 - self.parity], dst_ref=self.near.at[span],
            send_sem=self.near_send.at[m], recv_sem=self.near_recv.at[m],
            device_id={"dp": 2 * self.mine + 1 - self.parity}, device_id_type=MESH,
        )

    def far_copy(self, j, slot, to):
        return pltpu.make_async_remote_copy(
            src_ref=self.near.at[j], dst_ref=self.far.at[slot], send_sem=self.far_send.at[j],
            recv_sem=self.far_recv.at[slot], device_id={"dp": 2 * to + self.parity}, device_id_type=MESH,
        )

    def order(self, i):
        return lax.rem(lax.div(self.mine, self.group) + 1 + i, 4)

    def start(self, i):
        self.near_copy(self.order(i)).start()

    def turn(self, i):
        m = self.order(i)
        self.near_copy(m).wait_recv()
        rows = self.near.shape[1]
        step = 16

        def add(i, carry):
            j = m * self.group + lax.div(i, rows // step)
            span = pl.ds(pl.multiple_of(lax.rem(i, rows // step) * step, step), step)
            both = self.source[j, self.parity, span, :].astype(F32) + self.near[j, span, :].astype(F32)
            self.near[j, span, :] = both.astype(BF16)
            return carry

        lax.fori_loop(0, self.group * (rows // step), add, 0)

        def send(i, carry):
            j = m * self.group + i

            @pl.when(j != self.mine)
            def _():
                self.far_copy(j, self.mine, j).start()

            return carry

        lax.fori_loop(0, self.group, send, 0)

    def finish(self, out):
        def arrive(i, carry):
            slot = lax.rem(self.mine + i, self.pairs)
            self.far_copy(slot, slot, slot).wait_recv()
            return carry

        lax.fori_loop(1, self.pairs, arrive, 0)
        rows = out.shape[0]
        step = 16

        def add(i, carry):
            span = pl.ds(pl.multiple_of(i * step, step), step)
            total = self.near[self.mine, span, :].astype(F32)

            def more(j, value):
                return value + self.far[lax.rem(self.mine + j, self.pairs), span, :].astype(F32)

            if self.pairs <= 4:
                for j in range(1, self.pairs):
                    total = more(j, total)
            else:
                total = lax.fori_loop(1, self.pairs, more, total)
            out[span, :] = total
            return carry

        lax.fori_loop(0, rows // step, add, 0)

        def sent(i, carry):
            slot = lax.rem(self.mine + i, self.pairs)
            self.far_copy(slot, slot, slot).wait_send()
            return carry

        lax.fori_loop(1, self.pairs, sent, 0)
        for m in range(4):
            self.near_copy(m).wait_send()


class Spread:
    def __init__(self, whole, far_send, far_recv, near_send, near_recv):
        self.whole = whole
        self.far_send, self.far_recv, self.near_send, self.near_recv = far_send, far_recv, near_send, near_recv
        self.pairs = whole.shape[0] // 2
        self.me = lax.axis_index("dp")
        self.parity, self.mine = lax.rem(self.me, 2), lax.div(self.me, 2)

    def greet(self):
        barrier = pltpu.get_barrier_semaphore()
        sibling = self.me + 1 - 2 * self.parity
        pl.semaphore_signal(barrier, inc=1, device_id={"dp": sibling}, device_id_type=MESH)

        def signal(i, carry):
            other = 2 * lax.rem(self.mine + i, self.pairs) + self.parity
            pl.semaphore_signal(barrier, inc=1, device_id={"dp": other}, device_id_type=MESH)
            return carry

        lax.fori_loop(1, self.pairs, signal, 0)
        return self.pairs

    def far_copy(self, block, to, slot):
        return pltpu.make_async_remote_copy(
            src_ref=self.whole.at[block], dst_ref=self.whole.at[block], send_sem=self.far_send.at[to],
            recv_sem=self.far_recv.at[slot], device_id={"dp": 2 * to + self.parity}, device_id_type=MESH,
        )

    def near_copy(self, j, parity):
        block = 2 * j + parity
        return pltpu.make_async_remote_copy(
            src_ref=self.whole.at[block], dst_ref=self.whole.at[block], send_sem=self.near_send.at[j],
            recv_sem=self.near_recv.at[j], device_id={"dp": self.me + 1 - 2 * self.parity}, device_id_type=MESH,
        )

    def over_others(self, step):
        def run(i, carry):
            step(lax.rem(self.mine + i, self.pairs))
            return carry

        lax.fori_loop(1, self.pairs, run, 0)

    def start(self):
        self.over_others(lambda j: self.far_copy(self.me, j, self.mine).start())
        self.near_copy(self.mine, self.parity).start()

    def forward(self):
        def step(j):
            self.far_copy(2 * j + self.parity, j, j).wait_recv()
            self.near_copy(j, self.parity).start()

        self.over_others(step)

    def finish(self):
        self.receive()
        self.drain()

    def receive(self):
        other = 1 - self.parity
        self.over_others(lambda j: self.near_copy(j, other).wait_recv())
        self.near_copy(self.mine, other).wait_recv()

    def drain(self):
        self.over_others(lambda j: self.far_copy(self.me, j, self.mine).wait_send())
        self.over_others(lambda j: self.near_copy(j, self.parity).wait_send())
        self.near_copy(self.mine, self.parity).wait_send()


class Smalls:
    def __init__(self, axis, land, send_sem, recv_sem):
        self.axis, self.land, self.send_sem, self.recv_sem = axis, land, send_sem, recv_sem
        self.me, self.count = lax.axis_index(axis), land.shape[0]

    def other(self, i):
        return lax.rem(self.me + i, self.count)

    def greet(self):
        barrier = pltpu.get_barrier_semaphore()

        def signal(i, carry):
            pl.semaphore_signal(barrier, inc=1, device_id={self.axis: self.other(i)}, device_id_type=MESH)
            return carry

        lax.fori_loop(1, self.count, signal, 0)
        return self.count - 1

    def copy(self, slot, to):
        return pltpu.make_async_remote_copy(
            src_ref=self.land.at[self.me], dst_ref=self.land.at[slot], send_sem=self.send_sem.at[to],
            recv_sem=self.recv_sem.at[slot], device_id={self.axis: to}, device_id_type=MESH,
        )

    def start(self):
        def send(i, carry):
            self.copy(self.me, self.other(i)).start()
            return carry

        lax.fori_loop(1, self.count, send, 0)

    def finish(self):
        def arrive(i, carry):
            self.copy(self.other(i), self.other(i)).wait_recv()
            return carry

        lax.fori_loop(1, self.count, arrive, 0)

        def add(i, value):
            return value + self.land[i]

        total = lax.fori_loop(1, self.count, add, self.land[0])

        def sent(i, carry):
            self.copy(self.me, self.other(i)).wait_send()
            return carry

        lax.fori_loop(1, self.count, sent, 0)
        return total


def half_of(ref, h):
    value = ref[:, h]
    return value.reshape(value.shape[0] * value.shape[1], value.shape[2])


def blocks_of(ref, h):
    return [ref.at[b, h] for b in range(4)]


def parts_of(part, slots, k, h):
    return [part.at[k, h, t] for t in range(4)], [slots.at[k, h, s] for s in range(5)]


def for_tiles(size, tile, step):
    def run(i, carry):
        step(pl.multiple_of(i * tile, tile))
        return carry

    lax.fori_loop(0, size // tile, run, 0)


def partial_sums(left, weight, part, k, h):
    def step(n):
        value = lax.dot_general(left, weight[pl.ds(n, 256), :], NT, preferred_element_type=F32)
        part[k, h, :, :, pl.ds(n, 256)] = value.astype(BF16).reshape(4, left.shape[0] // 4, 256)

    for_tiles(weight.shape[0], 256, step)


def partial_sums_of(left, weight, start, part, k, h):
    devices, own, _ = weight.shape
    stop = start + left.shape[1]

    def step(n):
        tile = weight[pl.ds(lax.div(n, own), 256 // own), :, start:stop].reshape(256, stop - start)
        value = lax.dot_general(left, tile, NT, preferred_element_type=F32)
        part[k, h, :, :, pl.ds(n, 256)] = value.astype(BF16).reshape(4, left.shape[0] // 4, 256)

    for_tiles(devices * own, 256, step)


def row_grads(left, right, out, column):
    rows = left.shape[0] * left.shape[1] * left.shape[2]
    width = right.shape[3]
    pairs, _, own, _ = out.shape
    group = pairs // 4
    tall = group * 2 * own

    def piece(m):
        start = pl.multiple_of(m * tall, tall)
        turned = jnp.transpose(left[:, :, :, pl.ds(start, tall)].reshape(rows, tall))
        for n in range(0, width, 512):
            size = min(512, width - n)
            tile = right[:, :, :, n : n + size].reshape(rows, size)
            value = lax.dot_general(turned, tile, NN, preferred_element_type=F32)
            span = pl.ds(m * group, group)
            out[span, :, :, column + n : column + n + size] = value.astype(BF16).reshape(group, 2, own, size)

    return piece


def run_pieces(pieces, first, last):
    def run(m, carry):
        for piece in pieces:
            piece(m)
        return carry

    lax.fori_loop(first, last, run, 0)


def rms(value, gain):
    return value * lax.rsqrt(jnp.mean(value * value, axis=1, keepdims=True) + EPS) * gain


def rms_back(value, gain, grad):
    scale = lax.rsqrt(jnp.mean(value * value, axis=1, keepdims=True) + EPS)
    scaled = gain * grad
    back = scale * scaled - value * (scale * scale * scale) * jnp.mean(value * scaled, axis=1, keepdims=True)
    return back, jnp.sum(value * scale * grad, axis=0, keepdims=True)


def is_turned(shape):
    return shape[1] % 128 == 0 and shape[2] % 128 != 0


def turn(array):
    return jnp.swapaxes(array, 1, 2) if is_turned(array.shape) else array


def fetch_start(sources, held, sems, l):
    for i, source in enumerate(sources):
        pltpu.make_async_copy(source.at[l], held[i], sems.at[i]).start()


def cast_into(out, sources, held, sems, l, places):
    start = 0
    for i, (turned, width, padded) in enumerate(places):
        pltpu.make_async_copy(sources[i].at[l], held[i], sems.at[i]).wait()
        value = held[i][...]
        if turned:
            tall = -(-width // 128) * 128
            if tall > width:
                value = jnp.concatenate([value, jnp.zeros((tall - width, value.shape[1]), F32)], axis=0)
            value = jnp.transpose(value)
            width = tall
        out[:, start : start + width] = value.astype(BF16)
        if padded > width:
            out[:, start + width : start + padded] = jnp.zeros((value.shape[0], padded - width), BF16)
        start += padded


def cast_places(weights, units):
    return [(is_turned(w.shape), w.shape[2], -(-w.shape[2] // u) * u) for w, u in zip(weights, units)]


def cast_scratch(weights):
    return [pltpu.VMEM(held_shape(w), F32) for w in weights] + [DMA((len(weights),))]


def held_shape(w):
    _, own, width = w.shape
    return (width, own) if is_turned(w.shape) else (own, width)


def cast_kernel(l, places, *refs):
    count = len(places)
    sources, out, held, sems = refs[:count], refs[count], refs[count + 1 : -1], refs[-1]
    fetch_start(sources, held, sems, l)
    cast_into(out, sources, held, sems, l, places)


def cast_call(weights, units, l):
    places = cast_places(weights, units)
    return pl.pallas_call(
        functools.partial(cast_kernel, l, places),
        in_specs=[pl.BlockSpec(memory_space=pl.ANY)] * len(weights),
        out_specs=pl.BlockSpec(memory_space=pltpu.VMEM),
        out_shape=jax.ShapeDtypeStruct((weights[0].shape[1], sum(p[2] for p in places)), BF16),
        scratch_shapes=cast_scratch(weights),
        compiler_params=pltpu.CompilerParams(vmem_limit_bytes=VMEM_LIMIT),
        cost_estimate=cost(2),
        name="cast",
    )(*[turn(w) for w in weights])


def tables_into(segments, chunk, cols, rows):
    length = segments.shape[1]
    place = iota((1, length), 1)
    for s in range(segments.shape[0]):
        ids = segments[s : s + 1, :].astype(F32)
        masks = [
            jnp.where((pltpu.roll(ids, j, 1) == ids) & (place >= j), 1.0, 0.0) for j in range(1, 4)
        ]
        before, final = ids[:, :1], ids[:, chunk - 1 : chunk]
        before, final = (jnp.broadcast_to(x, (1, length)) for x in (before, final))
        for i in range(1, length // chunk):
            before = jnp.where(place >= i * chunk, ids[:, i * chunk - 1 : i * chunk], before)
            final = jnp.where(place >= i * chunk, ids[:, (i + 1) * chunk - 1 : (i + 1) * chunk], final)
        carried, tailed = (jnp.where(ids == x, 1.0, 0.0) for x in (before, final))
        rows[s] = jnp.concatenate([carried, tailed, ids, jnp.zeros((5, length), F32)], axis=0)
        cols[s] = jnp.transpose(jnp.concatenate(masks + [ids, jnp.zeros((4, length), F32)], axis=0))


def start_kernel(chunk, in_places, rest_places, rows, cot, gain, segments, *refs):
    first, second = len(in_places), len(rest_places)
    sources, refs = refs[: first + second], refs[first + second :]
    (normed, cot_all, w_in), refs = refs[:3], refs[3:]
    (low_down, table_cols, table_rows), refs = refs[:3], refs[3:]
    low, refs = refs[: 2 * LAYERS - 2], refs[2 * LAYERS - 2 :]
    held, (in_sems, rest_sems, down_sem, send_sem, recv_sem, *spread_sems) = refs[: first + second], refs[first + second :]
    in_refs = sources[:first], held[:first], in_sems
    rest_refs = sources[first:], held[first:], rest_sems
    line = Line(send_sem, recv_sem)
    spread = Spread(w_in, *spread_sems)
    down_refs = sources[-1:], held[-1:], down_sem
    fetch_start(*in_refs, 0)
    fetch_start(*down_refs, 0)
    line.greet()
    others = spread.greet()
    cast_into(w_in.at[spread.me], *in_refs, 0, in_places)
    for h in range(HALVES):
        normed[line.me, h] = rms(rows[h].astype(F32), gain[...]).astype(BF16)
        cot_all[line.me, h] = cot[h]
    line.meet(others)
    spread.start()
    both = [(k + h, blocks_of(ref, h)) for k, ref in ((0, normed), (2, cot_all)) for h in range(HALVES)]
    for item in both:
        line.gather_start(*item)
    tables_into(segments, chunk, table_cols, table_rows)
    cast_into(low_down, *down_refs, 0, rest_places[-1:])
    for l in range(1, LAYERS):
        fetch_start(*in_refs, l)
        fetch_start(*rest_refs, l)
        cast_into(low[2 * l - 2], *in_refs, l, in_places)
        cast_into(low[2 * l - 1], *rest_refs, l, rest_places)
    for item in both[:2]:
        line.gather_forward(*item)
    spread.forward()
    for item in both[2:]:
        line.gather_forward(*item)
    for item in both:
        line.gather_wait(*item)
    for item in both:
        line.gather_drain(*item)
    spread.finish()


def slices_of(weights, v_width, wide):
    return weights.at[:, :v_width], weights.at[:, v_width : v_width + 2 * wide]


def ffn_forward_kernel(last, reads, writes, mixer, weights, rows, gain, gain_next, down, middle, normed, pre, hidden, out_rows, *rest):
    if last:
        part, slots, total, send_sem, recv_sem = rest
    else:
        normed_next, whole_down, part, slots, total, send_sem, recv_sem, *spread_sems, gate = rest
    line = Line(send_sem, recv_sem)
    wide = hidden.shape[3]
    w_out, w_up = slices_of(weights, mixer.shape[3], wide)
    block = rows.shape[1]
    line.greet()
    for copy in reads[:2]:
        copy.wait()
    if last:
        partial_sums(half_of(mixer, 0), w_out, part, 0, 0)
        line.meet()
    else:
        turns = Turns(gate)
        spread = Spread(whole_down, *spread_sems)
        others = spread.greet()
        whole_down[spread.me] = down[...]
        partial_sums(half_of(mixer, 0), w_out, part, 0, 0)
        line.meet(others)
        spread.start()

        @pl.when(turns.second == 1)
        def _():
            spread.forward()

        turns.wait()
    line.scatter_start(0, *parts_of(part, slots, 0, 0))
    partial_sums(half_of(mixer, 1), w_out, part, 0, 1)
    line.scatter_relay(0, *parts_of(part, slots, 0, 0))
    line.scatter_start(1, *parts_of(part, slots, 0, 1))
    line.scatter_relay(1, *parts_of(part, slots, 0, 1))
    for copy in reads[2:]:
        copy.wait()
    for h in range(HALVES):
        both = parts_of(part, slots, 0, h)
        line.scatter_wait(h, *both)
        line.scatter_sum(total, *both)
        value = rows[h].astype(F32) + total[...]
        middle[h] = value
        normed[line.me, h] = rms(value, gain[...]).astype(BF16)
        line.gather_start(2 + h, blocks_of(normed, h))
    writes[0].start()
    line.gather_forward(2, blocks_of(normed, 0))
    for h in range(HALVES):
        if h == 1:
            line.gather_forward(3, blocks_of(normed, 1))
        line.gather_wait(2 + h, blocks_of(normed, h))
        if h == TURN_AT and not last:
            turns.give()
        left = half_of(normed, h)

        def step(n):
            gate = jnp.dot(left, w_up[:, pl.ds(n, 256)], preferred_element_type=F32)
            up = jnp.dot(left, w_up[:, pl.ds(n + wide, 256)], preferred_element_type=F32)
            pre[:, h, :, pl.ds(n, 256)] = gate.reshape(4, block, 256)
            pre[:, h, :, pl.ds(n + wide, 256)] = up.reshape(4, block, 256)
            value = gate * lax.logistic(gate) * up
            hidden[:, h, :, pl.ds(n, 256)] = value.astype(BF16).reshape(4, block, 256)

        for_tiles(wide, 256, step)
        if last:
            partial_sums_of(half_of(hidden, h), down, down.shape[2] - wide, part, 1, h)
        else:
            if h == 0:
                @pl.when(turns.second == 0)
                def _():
                    spread.forward()

                spread.receive()
                writes[6].start()
            partial_sums_of(half_of(hidden, h), whole_down, 0, part, 1, h)
        if h == 1:
            line.scatter_relay(4, *parts_of(part, slots, 1, 0))
        line.scatter_start(4 + h, *parts_of(part, slots, 1, h))
    for copy in writes[1:4]:
        copy.start()
    line.scatter_relay(5, *parts_of(part, slots, 1, 1))
    for h in range(HALVES):
        both = parts_of(part, slots, 1, h)
        line.scatter_wait(4 + h, *both)
        line.scatter_sum(total, *both)
        value = middle[h] + total[...]
        out_rows[h] = value
        if not last:
            normed_next[line.me, h] = rms(value, gain_next[...]).astype(BF16)
            line.gather_start(6 + h, blocks_of(normed_next, h))
    if not last:
        for h in range(HALVES):
            line.gather_forward(6 + h, blocks_of(normed_next, h))
        writes[4].start()
        for h in range(HALVES):
            line.gather_wait(6 + h, blocks_of(normed_next, h))
        writes[5].start()
    else:
        writes[4].start()
    for h in range(HALVES):
        line.scatter_drain(h, *parts_of(part, slots, 0, h))
        line.gather_drain(2 + h, blocks_of(normed, h))
        line.scatter_drain(4 + h, *parts_of(part, slots, 1, h))
        if not last:
            line.gather_drain(6 + h, blocks_of(normed_next, h))
    if not last:
        spread.drain()


def ffn_backward_kernel(owes, reads, writes, cot, hidden, pre, normed, middle, grad, gain, weights, down, *rest):
    if owes:
        owed, d_mixer, grads, mixer_cot, grad_out, d_gain, summed, *rest = rest
    else:
        d_mixer, grads, mixer_cot, grad_out, d_gain, *rest = rest
    d_pre, part, slots, total, send_sem, recv_sem, *rest = rest
    sums = None
    if owes:
        near, far, near_send, near_recv, far_send, far_recv, gate = rest
        sums = Sums(owed, near, far, near_send, near_recv, far_send, far_recv)
    line = Line(send_sem, recv_sem)
    wide = hidden.shape[3]
    w_out, w_up = slices_of(weights, d_mixer.shape[3], wide)
    down_at = down.shape[2] - wide
    block = middle.shape[1]
    line.greet()
    if owes:
        sums.greet_late(gate)
        reads[8].wait()
        sums.meet_late(line)
    else:
        line.meet()
    for copy in reads[:2]:
        copy.wait()
    for h in range(HALVES):
        reads[2 + h].wait()
        left = half_of(cot, h)

        def step(n):
            tile = down[:, :, pl.ds(down_at + n, 256)].reshape(left.shape[1], 256)
            d_hidden = jnp.dot(left, tile, preferred_element_type=F32)
            gate = pre[:, h, :, pl.ds(n, 256)].reshape(4 * block, 256)
            up = pre[:, h, :, pl.ds(n + wide, 256)].reshape(4 * block, 256)
            sig = lax.logistic(gate)
            d_gate = d_hidden * up * sig * (1.0 + gate * (1.0 - sig))
            d_up = d_hidden * gate * sig
            d_pre[:, h, :, pl.ds(n, 256)] = d_gate.astype(BF16).reshape(4, block, 256)
            d_pre[:, h, :, pl.ds(n + wide, 256)] = d_up.astype(BF16).reshape(4, block, 256)

        for_tiles(wide, 256, step)
        if h == 0:
            reads[4].wait()
        partial_sums(half_of(d_pre, h), w_up, part, 0, h)
        if h == 1:
            line.scatter_relay(0, *parts_of(part, slots, 0, 0))
        line.scatter_start(h, *parts_of(part, slots, 0, h))
    for copy in reads[5:8]:
        copy.wait()
    if owes:
        @pl.when(sums.parity == 1)
        def _():
            for m in range(4):
                sums.turn(m)

    line.scatter_relay(1, *parts_of(part, slots, 0, 1))
    pieces = [row_grads(cot, hidden, grads, 0), row_grads(normed, d_pre, grads, wide)]
    run_pieces(pieces, 0, 2)
    if owes:
        sums.start_late()
    d_gain[...] = jnp.zeros_like(d_gain)
    for h in range(HALVES):
        both = parts_of(part, slots, 0, h)
        line.scatter_wait(h, *both)
        line.scatter_sum(total, *both)
        back, gain_part = rms_back(middle[h], gain[...], total[...])
        d_gain[...] += gain_part
        value = grad[h].astype(F32) + back
        grad_out[h] = value
        mixer_cot[line.me, h] = value.astype(BF16)
        line.gather_start(2 + h, blocks_of(mixer_cot, h))
        if owes:
            @pl.when(sums.parity == 0)
            def _():
                sums.turn(2 * h)
                sums.turn(2 * h + 1)

    run_pieces(pieces, 2, 3)
    line.gather_forward(2, blocks_of(mixer_cot, 0))
    line.gather_forward(3, blocks_of(mixer_cot, 1))
    run_pieces(pieces, 3, 4)
    writes[0].start()
    writes[1].start()
    for h in range(HALVES):
        line.gather_wait(2 + h, blocks_of(mixer_cot, h))
        left = half_of(mixer_cot, h)
        for n in range(0, w_out.shape[1], 256):
            value = jnp.dot(left, w_out[:, n : n + 256], preferred_element_type=F32)
            d_mixer[:, h, :, n : n + 256] = value.reshape(4, block, 256)
        writes[2 + h].start()
    writes[4].start()
    for h in range(HALVES):
        line.scatter_drain(h, *parts_of(part, slots, 0, h))
        line.gather_drain(2 + h, blocks_of(mixer_cot, h))
    if owes:
        sums.finish(summed)


def mixer_backward_kernel(
    reads, writes, d_proj, w_in, normed, mixer, mixer_cot, rows, grad, gain,
    grad_out, d_gain, grads, cot, part, slots, total, send_sem, recv_sem,
):
    line = Line(send_sem, recv_sem)
    line.greet()
    line.meet()
    reads[0].wait()
    reads[1].wait()
    partial_sums(half_of(d_proj, 0), w_in, part, 0, 0)
    line.scatter_start(0, *parts_of(part, slots, 0, 0))
    reads[2].wait()
    partial_sums(half_of(d_proj, 1), w_in, part, 0, 1)
    line.scatter_relay(0, *parts_of(part, slots, 0, 0))
    line.scatter_start(1, *parts_of(part, slots, 0, 1))
    line.scatter_relay(1, *parts_of(part, slots, 0, 1))
    width = mixer.shape[3]
    pieces = [row_grads(mixer_cot, mixer, grads, 0), row_grads(normed, d_proj, grads, width)]
    for copy in reads[3:]:
        copy.wait()
    run_pieces(pieces, 0, 2)
    d_gain[...] = jnp.zeros_like(d_gain)
    for h in range(HALVES):
        both = parts_of(part, slots, 0, h)
        line.scatter_wait(h, *both)
        line.scatter_sum(total, *both)
        back, gain_part = rms_back(rows[h].astype(F32), gain[...], total[...])
        d_gain[...] += gain_part
        value = grad[h] + back
        grad_out[h] = value
        cot[line.me, h] = value.astype(BF16)
        line.gather_start(2 + h, blocks_of(cot, h))
    run_pieces(pieces, 2, 3)
    line.gather_forward(2, blocks_of(cot, 0))
    line.gather_forward(3, blocks_of(cot, 1))
    run_pieces(pieces, 3, 4)
    writes[0].start()
    writes[1].start()
    for h in range(HALVES):
        line.gather_wait(2 + h, blocks_of(cot, h))
    writes[2].start()
    for h in range(HALVES):
        line.scatter_drain(h, *parts_of(part, slots, 0, h))
        line.gather_drain(2 + h, blocks_of(cot, h))


def last_kernel(heads, reads, writes, d_proj, w_in, normed, mixer, mixer_cot, rows, grad, gain, *refs):
    smalls, refs = refs[: 5 * LAYERS + LAYERS - 1], refs[5 * LAYERS + LAYERS - 1 :]
    per_layer = [smalls[5 * l : 5 * l + 5] for l in range(LAYERS)]
    first_gains = smalls[5 * LAYERS :]
    (grad_out, summed, taps_out, norms_out,
     d_gain, grads, taps_land, line_land, norms_land,
     taps_send, taps_recv, line_send, line_recv, norms_send, norms_recv,
     part, slots, total, send_sem, recv_sem, *sum_refs) = refs
    line = Line(send_sem, recv_sem)
    sums = Sums(grads, *sum_refs)
    small_taps = Smalls("dp", taps_land, taps_send, taps_recv)
    small_line = Smalls("tensor", line_land, line_send, line_recv)
    small_norms = Smalls("dp", norms_land, norms_send, norms_recv)
    line.greet()
    others = sums.greet() + small_taps.greet() + small_line.greet()
    taps_land[small_taps.me] = jnp.zeros(taps_land.shape[1:], F32)
    line_land[line.me] = jnp.zeros(line_land.shape[1:], F32)
    for l, (d_qk, d_v, d_head, d_out_gain, second_gain) in enumerate(per_layer):
        top = TAP_ROWS * l
        seqs = d_qk.shape[0]
        for i in range(2):
            taps_land[small_taps.me, top + 4 * i : top + 4 * i + 4, : d_qk.shape[3]] = sum(d_qk[s, i] for s in range(seqs))
        taps_land[small_taps.me, top + 8 : top + 12, : d_v.shape[2]] = sum(d_v[s] for s in range(seqs))
        lane = iota((1, 128), 1)
        row = jnp.zeros((1, 128), F32)
        for kind in range(2):
            for h in range(heads):
                value = sum(d_head[s, h, kind : kind + 1, :] for s in range(seqs))
                row = row + jnp.where(lane == kind * heads + h, value, 0.0)
        taps_land[small_taps.me, top + 12 : top + 13, :128] = row
        line_land[line.me, 2 * l + 1 : 2 * l + 2, :] = second_gain[...]
        value = sum(d_out_gain[s, h] for s in range(seqs) for h in range(heads))
        line_land[line.me, 2 * LAYERS + l : 2 * LAYERS + l + 1, : value.shape[1]] = value
        if l > 0:
            line_land[line.me, 2 * l : 2 * l + 1, :] = first_gains[l - 1][...]
    reads[0].wait()
    reads[1].wait()
    partial_sums(half_of(d_proj, 0), w_in, part, 0, 0)
    line.meet(others)
    line.scatter_start(0, *parts_of(part, slots, 0, 0))
    small_taps.start()
    width = mixer.shape[3]
    pieces = [row_grads(mixer_cot, mixer, grads, 0), row_grads(normed, d_proj, grads, width)]
    for copy in reads[2:]:
        copy.wait()
    for piece in pieces:
        piece(sums.order(0))
    sums.start(0)
    line.scatter_relay(0, *parts_of(part, slots, 0, 0))
    partial_sums(half_of(d_proj, 1), w_in, part, 0, 1)
    line.scatter_start(1, *parts_of(part, slots, 0, 1))
    for m in range(1, 4):
        for piece in pieces:
            piece(sums.order(m))
        sums.start(m)
        sums.turn(m - 1)
    line.scatter_relay(1, *parts_of(part, slots, 0, 1))
    sums.turn(3)
    d_gain[...] = jnp.zeros_like(d_gain)
    for h in range(HALVES):
        both = parts_of(part, slots, 0, h)
        line.scatter_wait(h, *both)
        line.scatter_sum(total, *both)
        back, gain_part = rms_back(rows[h].astype(F32), gain[...], total[...])
        d_gain[...] += gain_part
        grad_out[h] = grad[h] + back
    line_land[line.me, 0:1, :] = d_gain[...]
    small_line.start()
    norms_land[small_norms.me] = small_line.finish()
    small_norms.start()
    taps_out[...] = small_taps.finish()
    for h in range(HALVES):
        line.scatter_drain(h, *parts_of(part, slots, 0, h))
    sums.finish(summed)
    norms_out[...] = small_norms.finish()


TAP_ROWS = 16
DMA = pltpu.SemaphoreType.DMA


def line_call(kernel, operands, outs, scratch, number, name, micros, spaces=None, fetches=(), puts=()):
    staged_in = sorted({i for i, _ in fetches})
    staged_out = sorted({i for i, _ in puts})
    count_in, count_out, count = len(operands), len(outs), len(scratch)
    held = [pltpu.VMEM(operands[i].shape, operands[i].dtype) for i in staged_in]
    held += [pltpu.VMEM(*outs[i]) for i in staged_out]
    if fetches or puts:
        held += [DMA((len(fetches),)), DMA((len(puts),))]

    def staged(*refs):
        ins, results = list(refs[:count_in]), list(refs[count_in : count_in + count_out])
        own = refs[count_in + count_out : count_in + count_out + count]
        *arrays, in_sems, out_sems = refs[count_in + count_out + count :]
        sources, targets = list(ins), list(results)
        for i, ref in zip(staged_in, arrays):
            ins[i] = ref
        for i, ref in zip(staged_out, arrays[len(staged_in) :]):
            results[i] = ref
        reads = [
            pltpu.make_async_copy(cut(sources[i]), cut(ins[i]), in_sems.at[j]) for j, (i, cut) in enumerate(fetches)
        ]
        writes = [
            pltpu.make_async_copy(cut(results[i]), cut(targets[i]), out_sems.at[j]) for j, (i, cut) in enumerate(puts)
        ]
        for copy in reads:
            copy.start()
        kernel(reads, writes, *ins, *results, *own)
        for copy in writes:
            copy.wait()

    spaces = list(spaces or [pltpu.VMEM] * count_in)
    out_spaces = [pltpu.VMEM] * count_out
    for i in staged_in:
        spaces[i] = pl.ANY
    for i in staged_out:
        out_spaces[i] = pl.ANY
    return pl.pallas_call(
        staged if fetches or puts else kernel,
        in_specs=[pl.BlockSpec(memory_space=s) for s in spaces],
        out_specs=[pl.BlockSpec(memory_space=s) for s in out_spaces],
        out_shape=[jax.ShapeDtypeStruct(*out) for out in outs],
        scratch_shapes=list(scratch) + held,
        compiler_params=pltpu.CompilerParams(
            collective_id=number, has_side_effects=True, vmem_limit_bytes=VMEM_LIMIT
        ),
        cost_estimate=cost(micros),
        name=name,
    )(*operands)


def every(ref):
    return ref


def columns_cut(start, stop):
    return lambda ref: ref.at[:, start:stop]


def last_cut(start):
    return lambda ref: ref.at[:, :, start:]


def half_cut(h):
    return lambda ref: ref.at[:, h]


def line_scratch(sums, block, width, phases):
    return [
        pltpu.VMEM((sums, HALVES, 4, block, width), BF16),
        pltpu.VMEM((sums, HALVES, 5, block, width), BF16),
        pltpu.VMEM((block, width), F32),
        DMA((phases, 4)),
        DMA((phases, 5)),
    ]


def sums_scratch(shape):
    pairs, _, own, width = shape
    return [
        pltpu.VMEM((pairs, own, width), BF16), pltpu.VMEM((pairs, own, width), BF16),
        DMA((4,)), DMA((4,)), DMA((pairs,)), DMA((pairs,)),
    ]


def start_call(rows, cot, gain, segments, chunk, in_weights, rest_weights, rest_units, dp):
    _, block, width = rows.shape
    in_places = cast_places(in_weights, (128,) * len(in_weights))
    rest_places = cast_places(rest_weights, rest_units)
    own = in_weights[0].shape[1]
    in_width, rest_width = (sum(p[2] for p in places) for places in (in_places, rest_places))
    whole = ((4, HALVES, block, width), BF16)
    outs = [whole, whole, ((dp, own, in_width), BF16), ((own, rest_places[-1][2]), BF16)]
    seqs, length = segments.shape
    outs += [((seqs, length, 8), F32), ((seqs, 8, length), F32)]
    outs += [((own, in_width), BF16), ((own, rest_width), BF16)] * (LAYERS - 1)
    half = dp // 2
    scratch = [pltpu.VMEM(held_shape(w), F32) for w in in_weights + rest_weights] + [
        DMA((len(in_weights),)), DMA((len(rest_weights),)), DMA((1,)),
        DMA((4, 4)), DMA((4, 5)), DMA((half,)), DMA((half,)), DMA((half,)), DMA((half,)),
    ]
    return line_call(
        functools.partial(start_kernel, chunk, in_places, rest_places),
        (rows, cot, gain, segments, *[turn(w) for w in in_weights + rest_weights]), outs, scratch, 1, "start", 35,
        [pltpu.VMEM] * 4 + [pl.ANY] * len(in_weights + rest_weights),
    )


def ffn_forward_call(mixer, weights, down, rows, gain, gain_next, layer, last, dp, wide):
    _, block, width = rows.shape
    up_at = mixer.shape[3]
    own, whole = ((HALVES, block, width), F32), ((4, HALVES, block, width), BF16)
    outs = [own, whole, ((4, HALVES, block, 2 * wide), F32), ((4, HALVES, block, wide), BF16), own]
    scratch = line_scratch(2, block, width, 8)
    fetches = [(0, every), (1, columns_cut(0, up_at)), (2, every), (1, columns_cut(up_at, up_at + 2 * wide))]
    if last:
        fetches.append((5, last_cut(down.shape[2] - wide)))
    else:
        outs += [whole, ((dp,) + down.shape, BF16)]
        half = dp // 2
        scratch += [DMA((half,)), DMA((half,)), DMA((half,)), DMA((half,)), pltpu.SemaphoreType.REGULAR]
    return line_call(
        functools.partial(ffn_forward_kernel, last), (mixer, weights, rows, gain, gain_next, down), outs,
        scratch, 2 + layer, "ffn_forward", 65, None, fetches, [(i, every) for i in range(len(outs))],
    )


def ffn_backward_call(cot, hidden, pre, normed, middle, grad, gain, weights, down, v_width, grads_shape, owed, layer):
    _, block, width = middle.shape
    wide = hidden.shape[3]
    whole = ((4, HALVES, block, width), BF16)
    outs = [
        ((4, HALVES, block, v_width), F32), (grads_shape + (3 * wide,), BF16), whole,
        ((HALVES, block, width), F32), ((1, width), F32),
    ]
    scratch = [pltpu.VMEM((4, HALVES, block, 2 * wide), BF16)] + line_scratch(1, block, width, 4)
    operands = [cot, hidden, pre, normed, middle, grad, gain, weights, down]
    if owed is not None:
        operands.append(owed)
        outs.append((owed.shape[2:], F32))
        scratch += sums_scratch(owed.shape) + [pltpu.SemaphoreType.REGULAR]
    up_at = v_width
    down_at = up_at + 2 * wide
    fetches = [
        (8, last_cut(down.shape[2] - wide)), (0, every), (2, half_cut(0)), (2, half_cut(1)),
        (7, columns_cut(up_at, down_at)), (1, every), (3, every), (7, columns_cut(0, up_at)),
    ]
    if owed is not None:
        fetches.append((9, every))
    return line_call(
        functools.partial(ffn_backward_kernel, owed is not None), operands, outs, scratch,
        4 + layer, "ffn_backward", 40, None, fetches,
        [(1, every), (3, every), (0, half_cut(0)), (0, half_cut(1)), (2, every)],
    )


def mixer_backward_call(d_proj, w_in, normed, mixer, mixer_cot, rows, grad, gain, grads_shape, layer):
    _, block, width = rows.shape
    outs = [
        ((HALVES, block, width), F32), ((1, width), F32),
        (grads_shape + (mixer.shape[3] + w_in.shape[1],), BF16), ((4, HALVES, block, width), BF16),
    ]
    return line_call(
        mixer_backward_kernel, (d_proj, w_in, normed, mixer, mixer_cot, rows, grad, gain), outs,
        line_scratch(1, block, width, 4), 6 + layer, "mixer_backward", 40, None,
        [(1, every), (0, half_cut(0)), (0, half_cut(1)), (4, every), (3, every), (2, every)],
        [(2, every), (0, every), (3, every)],
    )


def last_call(d_proj, w_in, normed, mixer, mixer_cot, rows, grad, gain, smalls, first_gains, grads_shape, heads):
    _, block, width = rows.shape
    dp = 2 * grads_shape[0]
    shape = grads_shape + (mixer.shape[3] + w_in.shape[1],)
    taps_width = max(smalls[0][0].shape[3], smalls[0][1].shape[2])
    taps_shape, norms_shape = (TAP_ROWS * LAYERS, taps_width), (8, width)
    outs = [((HALVES, block, width), F32), (shape[2:], F32), (taps_shape, F32), (norms_shape, F32)]
    scratch = [
        pltpu.VMEM((1, width), F32), pltpu.VMEM(shape, BF16), pltpu.VMEM((dp,) + taps_shape, F32),
        pltpu.VMEM((4,) + norms_shape, F32), pltpu.VMEM((dp,) + norms_shape, F32),
        DMA((dp,)), DMA((dp,)), DMA((4,)), DMA((4,)), DMA((dp,)), DMA((dp,)),
    ]
    flat = [array for layer in smalls for array in layer] + list(first_gains)
    return line_call(
        functools.partial(last_kernel, heads),
        (d_proj, w_in, normed, mixer, mixer_cot, rows, grad, gain, *flat), outs,
        scratch + line_scratch(1, block, width, 2) + sums_scratch(shape), 8, "last", 40, None,
        [(1, every), (0, half_cut(0)), (0, half_cut(1)), (4, every), (3, every), (2, every)],
    )


def cut_grads(places, sources, outs, held, sems):
    copies = []
    for i, (width, start, turned) in enumerate(places):
        for l, source in enumerate(sources):
            if turned:
                tall = -(-width // 128) * 128
                held[i][l] = jnp.transpose(source[:, start : start + tall].astype(F32))[:width]
            else:
                held[i][l] = source[:, start : start + width].astype(F32)
        copies.append(pltpu.make_async_copy(held[i], outs[i], sems.at[i]))
        copies[-1].start()
    return copies


def finish_kernel(places, heads, *refs):
    sources, refs = refs[:LAYERS], refs[LAYERS:]
    count = len(places)
    if heads:
        (rows, grad, taps, norms), refs = refs[:4], refs[4:]
        outs, refs = refs[: count + 2], refs[count + 2 :]
        (conv_qk, conv_v, head, norm_gains, out_gain), refs = refs[:5], refs[5:]
        copies = [
            pltpu.make_async_copy(rows, outs[count], refs[-1].at[count]),
            pltpu.make_async_copy(grad, outs[count + 1], refs[-1].at[count + 1]),
        ]
        for copy in copies:
            copy.start()
    else:
        outs, refs, copies = refs[:count], refs[count:], []
    copies += cut_grads(places, sources, outs, refs[:-1], refs[-1])
    if heads:
        for l in range(LAYERS):
            top = TAP_ROWS * l
            for i in range(2):
                conv_qk[l, i] = taps[top + 4 * i : top + 4 * i + 4, : conv_qk.shape[3]]
                head[l, i : i + 1, :] = taps[top + 12 : top + 13, i * heads : (i + 1) * heads]
                norm_gains[l, i : i + 1, :] = norms[2 * l + i : 2 * l + i + 1, :]
            conv_v[l] = taps[top + 8 : top + 12, : conv_v.shape[2]]
            out_gain[l : l + 1, :] = norms[2 * LAYERS + l : 2 * LAYERS + l + 1, : out_gain.shape[1]]
    for copy in copies:
        copy.wait()


def finish_call(sums, places, others=(), like=()):
    own = sums[0].shape[0]
    heads = like[2].shape[2] if like else 0
    full = [(LAYERS, own, width) for width, _ in places]
    turned = [is_turned(shape) for shape in full]
    shapes = [(s[0], s[2], s[1]) if t else s for s, t in zip(full, turned)]
    places = [p + (t,) for p, t in zip(places, turned)]
    count = len(places)
    direct = [array.shape for array in others[:2]]
    outs = pl.pallas_call(
        functools.partial(finish_kernel, places, heads),
        in_specs=[pl.BlockSpec(memory_space=pltpu.VMEM)] * (len(sums) + len(others)),
        out_specs=[pl.BlockSpec(memory_space=pl.ANY)] * (count + len(direct))
        + [pl.BlockSpec(memory_space=pltpu.VMEM)] * len(like),
        out_shape=[jax.ShapeDtypeStruct(shape, F32) for shape in shapes + direct]
        + [jax.ShapeDtypeStruct(array.shape, F32) for array in like],
        scratch_shapes=[pltpu.VMEM(shape, F32) for shape in shapes] + [DMA((count + len(direct),))],
        compiler_params=pltpu.CompilerParams(vmem_limit_bytes=VMEM_LIMIT),
        cost_estimate=cost(3),
        name="finish",
    )(*sums, *others)
    return [jnp.swapaxes(o, 1, 2) if t else o for o, t in zip(outs[:count], turned)], outs[count:]


CHUNK = 128
REFINE = 2


def body(
    tokens,
    segment_ids,
    query_weight,
    key_weight,
    value_weight,
    gate_weight,
    decay_weight,
    out_weight,
    swiglu_gate,
    swiglu_up,
    swiglu_down,
    conv_query_key,
    conv_value,
    head_params,
    norm_gains,
    out_gain,
    cotangent,
):
    seqs, length = segment_ids.shape
    heads = head_params.shape[2]
    qk_width, v_width, pair_width = query_weight.shape[2], value_weight.shape[2], decay_weight.shape[2]
    hidden_width = swiglu_gate.shape[2]
    hidden_pad = -(-hidden_width // 256) * 256
    local_rows, width = tokens.shape
    block = local_rows // HALVES
    total_rows = 4 * local_rows

    def gathered(matrix):
        return lax.all_gather(matrix, "dp", axis=0, tiled=True)

    def reduced(matrix):
        return lax.psum_scatter(matrix, "dp", scatter_dimension=0, tiled=True)

    in_weights = (query_weight, key_weight, value_weight, gate_weight, decay_weight)
    rest_weights = (out_weight, swiglu_gate, swiglu_up, swiglu_down)
    rest_units = (128, 256, 256, 256)

    def split_rows(matrix):
        return matrix.reshape(HALVES, block, matrix.shape[1])

    def split_all(matrix):
        return matrix.reshape(4, HALVES, block, matrix.shape[1])

    def merged(array):
        return array.reshape(total_rows, array.shape[3])

    def gain_of(l, i):
        return norm_gains[l, i][None]

    dp = lax.axis_size("dp")
    rows = split_rows(tokens)
    cot_rows = split_rows(cotangent)
    w_rest = [gathered(cast_call(rest_weights[:3], rest_units[:3], 0))]
    normed, cot, w_in, first_down, *low = start_call(
        rows, cot_rows, gain_of(0, 0), segment_ids, CHUNK, in_weights, rest_weights, rest_units, dp
    )
    tables, low = low[:2], low[2:]
    w_in = [w_in.reshape(width, w_in.shape[2])] + [gathered(part) for part in low[::2]]
    w_rest += [gathered(part) for part in low[1::2]]
    w_down = [first_down] + [w.reshape(dp, width // dp, w.shape[1]) for w in w_rest[1:]]
    kept = []
    for l in range(LAYERS):
        last = l == LAYERS - 1
        proj = jnp.dot(merged(normed), w_in[l], preferred_element_type=F32)
        small = (conv_query_key[l], conv_value[l], head_params[l], out_gain[l][None])
        mixer, *saved = delta_forward(proj, *small, tables, seqs, heads, CHUNK, REFINE)
        mixer = split_all(mixer)
        gain_next = gain_of(min(l + 1, LAYERS - 1), 0)
        middle, normed_ffn, pre, hidden, out_rows, *following = ffn_forward_call(
            mixer, w_rest[l], w_down[l], rows, gain_of(l, 1), gain_next, l, last, dp, hidden_pad
        )
        kept.append((rows, normed, proj, small, mixer, saved, middle, normed_ffn, pre, hidden))
        rows = out_rows
        if not last:
            normed, w_down[l] = following
    output = rows
    grad = cot_rows
    grads_shape = (dp // 2, 2, width // dp)
    ffn_grads, mixer_grads, smalls, first_gains = ([None] * LAYERS for _ in range(4))
    owed = None
    for l in reversed(range(LAYERS)):
        rows, normed, proj, small, mixer, saved, middle, normed_ffn, pre, hidden = kept[l]
        d_mixer, ffn_grad, mixer_cot, grad, second_gain, *summed = ffn_backward_call(
            cot, hidden, pre, normed_ffn, middle, grad, gain_of(l, 1), w_rest[l], w_down[l], v_width, grads_shape, owed, l
        )
        if summed:
            mixer_grads[l + 1] = summed[0]
        ffn_grads[l] = reduced(ffn_grad.reshape(width, 3 * hidden_pad))
        if l < LAYERS - 1:
            d_mixer, ffn_grads[l + 1] = lax.optimization_barrier((d_mixer, ffn_grads[l + 1]))
        d_proj, d_qk, d_v, d_head, d_gain = delta_backward(
            proj, *small, tables, saved, merged(d_mixer), seqs, heads, CHUNK
        )
        smalls[l] = (d_qk, d_v, d_head, d_gain, second_gain)
        d_proj = split_all(d_proj)
        if l > 0:
            grad, first_gains[l], owed, cot = mixer_backward_call(
                d_proj, w_in[l], normed, mixer, mixer_cot, rows, grad, gain_of(l, 0), grads_shape, l
            )
    grad, mixer_grads[0], taps, norms = last_call(
        d_proj, w_in[0], normed, mixer, mixer_cot, rows, grad, gain_of(0, 0), smalls, first_gains[1:], grads_shape, heads
    )
    places, start = [], v_width
    for size in (qk_width, qk_width, v_width, v_width, pair_width):
        places.append((size, start))
        start += size
    mixer_outs, others = finish_call(
        mixer_grads, places + [(v_width, 0)], (output, grad, taps, norms),
        (conv_query_key, conv_value, head_params, norm_gains, out_gain),
    )
    ffn_outs, _ = finish_call(
        ffn_grads, [(hidden_width, hidden_pad), (hidden_width, 2 * hidden_pad), (hidden_width, 0)]
    )
    output, grad, *smalls = others
    return (
        output.reshape(local_rows, width), grad.reshape(local_rows, width), *mixer_outs, *ffn_outs, *smalls
    )


def solution(mesh):
    rows = P(("dp", "tensor"), None)
    weight = P(None, "dp", "tensor")
    small = (P(None, None, None, "tensor"), P(None, None, "tensor"), P(None, None, "tensor"), P(), P())
    return jax.shard_map(
        body,
        mesh=mesh,
        in_specs=(rows, P("dp", None)) + (weight,) * 9 + small + (rows,),
        out_specs=(rows, rows) + (weight,) * 9 + small,
        check_vma=False,
    )
```
